32 devices in a mesh: expert: 2 (over x), context: 4 (over y, core), dp: 4 (over z).
Axes of the slice: x: 2, y: 2, z: 4, core: 2. Of those that a mesh axis runs over, the one named last changes fastest.
Arguments:
- hidden: bfloat16 [8, 1024, 1536], P(('expert', 'dp'), 'context'), may hold values from -6 to 6
- cotangent: bfloat16 [8, 1024, 1536], P(('expert', 'dp'), 'context'), may hold values from -6 to 6
- token_order: int32 [8, 1024], P(('expert', 'dp')), may hold values from 0 to 1023, each once within a row
- lengths: int32 [8, 3], P(('expert', 'dp')), may hold values from 1 to 512, 1024 in all within a row
- routes: int32 [8, 1024, 4], P(('expert', 'dp'), 'context'), may hold values from 0 to 7, all different within a row; in each aligned block of 256 rows (0 to 255, 256 to 511, ..., all dimensions but the last counted through in order) at most 144 rows name the same one
- attn_gain: bfloat16 [1536], P(('context', 'dp')), may hold values from 0.5 to 1.5
- w_query: bfloat16 [1536, 1536], P(('context', 'dp')), may hold values from -0.15625 to 0.15625
- key_weight: bfloat16 [1536, 512], P(('context', 'dp')), may hold values from -0.15625 to 0.15625
- value_weight: bfloat16 [1536, 512], P(('context', 'dp')), may hold values from -0.15625 to 0.15625
- w_out: bfloat16 [1536, 1536], P(('context', 'dp')), may hold values from -1.25 to 1.25
- ffn_gain: bfloat16 [1536], P(('context', 'dp')), may hold values from 0.5 to 1.5
- w_router: bfloat16 [1536, 8], P(('context', 'dp')), may hold values from -0.078125 to 0.078125
- w_gate: bfloat16 [8, 1536, 512], P(('expert', 'context')), may hold values from -0.15625 to 0.15625
- w_up: bfloat16 [8, 1536, 512], P(('expert', 'context')), may hold values from -0.15625 to 0.15625
- w_down: bfloat16 [8, 512, 1536], P(('expert', 'context')), may hold values from -1 to 1
Outputs:
- output: bfloat16 [8, 1024, 1536], P(('expert', 'dp'), 'context')
- grad_hidden: bfloat16 [8, 1024, 1536], P(('expert', 'dp'), 'context')
- grad_attn_gain: float32 [1536], P(('context', 'dp'))
- grad_query: float32 [1536, 1536], P(('context', 'dp'))
- grad_key: float32 [1536, 512], P(('context', 'dp'))
- grad_value: float32 [1536, 512], P(('context', 'dp'))
- grad_out: float32 [1536, 1536], P(('context', 'dp'))
- grad_ffn_gain: float32 [1536], P(('context', 'dp'))
- grad_router: float32 [1536, 8], P(('context', 'dp'))
- grad_gate: float32 [8, 1536, 512], P(('expert', 'context'), 'dp')
- grad_up: float32 [8, 1536, 512], P(('expert', 'context'), 'dp')
- grad_down: float32 [8, 512, 1536], P(('expert', 'context'), None, 'dp')
The draws below stay inside these ranges and needn't reach their ends.
Inputs may be any that keep to these rules, and one draw needn't show every extreme that they name: `token_order`: each row names every place of its group once. `lengths`: each row sums to 1024; its largest length is exactly 512. `routes`: a token names 4 different experts; in the rows of one device no expert is named more than 144 times, a bound that some block reaches.
All inputs are finite; a program needn't handle non-finite values.
Results may differ from the reference program's by a relative error of at most 0.025.
Values may be sent and summed in bfloat16 or wider, within the bound.
No kernel may reach another device: no remote copies, remote signals or barrier semaphores. Data moves between devices by JAX's collectives and lax.ppermute only.
A program may use at most 192 MiB of HBM per device.

```python
import math
from functools import partial
import jax
import jax.numpy as jnp
import numpy as np
from jax import lax

MODEL_WIDTH = 1536
QUERY_HEADS = 24
KEY_VALUE_HEADS = 8
HEAD_SIZE = 64
FF = 512
TOK_DEV = 256
NSEQ = 3
GROUP_TOK = 1024
MOST_LEN = 512
GROUPS = 8
EXPERTS = 8
TOP = 4
CAP = 144
N_EXPERT = 2
N_DP = 4


def shard_levels(rng, shape, pieces, least, largest):
    factor_of = 1.0
    for dim, shards_of in pieces:
        heights = jax.random.uniform(jax.random.fold_in(jax.random.fold_in(rng, 6), dim), (shards_of,), jnp.float32, least / len(pieces), largest / len(pieces))
        factor_of = factor_of * jnp.repeat(jnp.exp(heights), shape[dim] // shards_of).reshape((-1,) + (1,) * (len(shape) - 1 - dim))
    return factor_of


def profile(count, total, limit, skew):
    loads = [(1 << 20) // math.isqrt(standing ** skew) + 1 for standing in range(2, count + 1)]
    surplus, holding = total - limit - (count - 1), [1] * (count - 1)
    while surplus > 0:
        movable = [i for i in range(count - 1) if holding[i] < limit]
        whole, remaining = sum([loads[i] for i in movable]), surplus
        for i in movable:
            extra = min(limit - holding[i], max(1, remaining * loads[i] // whole), surplus)
            holding[i] = holding[i] + extra
            surplus = surplus - extra
    return np.array([limit] + holding)


def uneven_parts(rng, amount, total, most, lean):
    if amount == 2:
        one = jax.random.randint(rng, (), max(1, total - most), min(most, total - 1) + 1)
        return jnp.stack([one, total - one])
    sizes = jnp.asarray(profile(amount, total, most, lean), jnp.int32)
    couples = (amount - 1) // 2
    source_of, sink = sizes[1:1 + 2 * couples:2], sizes[2:2 + 2 * couples:2]
    room = jnp.minimum(source_of - 1, most - sink)
    shifted = jax.random.randint(jax.random.fold_in(rng, 1), (couples,), 0, 1 << 20) % (room + 1)
    sizes = sizes.at[1:1 + 2 * couples:2].set(source_of - shifted).at[2:2 + 2 * couples:2].set(sink + shifted)
    return sizes[jax.random.permutation(jax.random.fold_in(rng, 2), amount)]


def routed_block(rng, own, number, rows, number_of, top, reach, slope):
    ranking = jax.random.permutation(rng, number_of)
    crowded, common = portions_of(number_of, rows * top, reach, slope, True), portions_of(number_of, rows * top, reach, slope, False)
    places = jnp.arange(number_of)

    def named(sizes, rotation):
        used = int((sizes > 0).sum())
        fixed = max(1, used // 4)
        shifted = fixed + (places - fixed + rotation * (used - fixed)) % max(1, number_of - fixed)
        return jnp.zeros((number_of,), jnp.int32).at[ranking[jnp.where(places < fixed, places, shifted)]].set(jnp.asarray(sizes, jnp.int32))

    sizes = jnp.where(number % 4 == 0, named(crowded, number // 4), named(common, number - number // 4 - 1))
    mixed = jax.random.permutation(jax.random.fold_in(own, 3), number_of)
    donor, sink = mixed[0:number_of // 2 * 2:2], mixed[1:number_of // 2 * 2:2]
    room = jnp.minimum(sizes[donor] - 1, reach - sizes[sink]) // 2
    room = jnp.where((donor == ranking[0]) | (sink == ranking[0]) | (sizes[sink] == 0), 0, jnp.maximum(room, 0))
    shifted = jax.random.randint(jax.random.fold_in(own, 4), (number_of // 2,), 0, 1 << 20) % (room + 1)
    sizes = sizes.at[donor].add(-shifted).at[sink].add(shifted)
    labels = jnp.searchsorted(jnp.cumsum(sizes), jnp.arange(rows * top), side="right").astype(jnp.int32)
    listing = labels.reshape(top, rows).T
    listing = listing[jax.random.permutation(jax.random.fold_in(own, 1), rows)]
    rotation = jax.random.randint(jax.random.fold_in(own, 2), (rows, 1), 0, top)
    return jnp.take_along_axis(listing, (jnp.arange(top)[None, :] + rotation) % top, axis=1)


def portions_of(count, total, most, skew, full):
    loads = [(1 << 20) // math.isqrt(rank ** skew) + 1 for rank in range(1, count + 1)]
    largest = most if full else min(most, max(-(-total // count), total * loads[0] // sum(loads)))
    least = 1 if total - largest >= count - 1 else 0
    holding, surplus = [largest] + [least] * (count - 1), total - largest - least * (count - 1)
    while surplus > 0:
        movable = [i for i in range(1, count) if holding[i] < largest] or [i for i in range(1, count) if holding[i] < most]
        pool, left = sum([loads[i] for i in movable]), surplus
        for i in movable:
            extra = min(most - holding[i], max(1, left * loads[i] // pool), surplus)
            holding[i] = holding[i] + extra
            surplus = surplus - extra
    return np.array(holding)


def bell_draw(key, extent, spread, most, shards=(), kind=jnp.bfloat16):
    entries = spread * jax.random.normal(key, extent, jnp.float32)
    if shards:
        entries = entries * shard_levels(key, extent, shards, -0.22, 0.18)
    return jnp.clip(entries, -most, most).astype(kind)


def setup_inputs(seed: int = 0) -> dict:
    keys = jax.random.split(jax.random.key(seed), 16)
    hidden = bell_draw(keys[0], (GROUPS, GROUP_TOK, MODEL_WIDTH), 1.0, 6.0, ((0, 8), (1, 4)))
    cotangent = bell_draw(keys[1], (GROUPS, GROUP_TOK, MODEL_WIDTH), 1.0, 6.0, ((0, 8), (1, 4)))
    token_order = jax.vmap(lambda own: jax.random.permutation(own, GROUP_TOK))(jax.random.split(keys[2], GROUPS)).reshape((GROUPS, GROUP_TOK)).astype(jnp.int32)
    lengths = jax.vmap(lambda own: uneven_parts(own, NSEQ, GROUP_TOK, MOST_LEN, 1))(jax.random.split(keys[3], GROUPS)).reshape((GROUPS, NSEQ)).astype(jnp.int32)
    routes_keys = jax.random.split(jax.random.fold_in(keys[4], 1), GROUPS * GROUP_TOK // TOK_DEV)
    routes_turns = jax.random.permutation(jax.random.fold_in(keys[4], 3), GROUPS * GROUP_TOK // TOK_DEV)
    routes = jax.vmap(lambda own, number: routed_block(jax.random.fold_in(keys[4], 2), own, number, TOK_DEV, EXPERTS, TOP, CAP, 1))(routes_keys, routes_turns).reshape((GROUPS, GROUP_TOK, TOP))
    attn_gain = jnp.clip(1.0 + 0.1 * jax.random.normal(keys[5], (MODEL_WIDTH,), jnp.float32), 0.5, 1.5).astype(jnp.bfloat16)
    w_query = bell_draw(keys[6], (MODEL_WIDTH, QUERY_HEADS * HEAD_SIZE), MODEL_WIDTH ** -0.5, 0.15625, ((0, 16),))
    key_weight = bell_draw(keys[7], (MODEL_WIDTH, KEY_VALUE_HEADS * HEAD_SIZE), MODEL_WIDTH ** -0.5, 0.15625, ((0, 16),))
    value_weight = bell_draw(keys[8], (MODEL_WIDTH, KEY_VALUE_HEADS * HEAD_SIZE), MODEL_WIDTH ** -0.5, 0.15625, ((0, 16),))
    w_out = bell_draw(keys[9], (QUERY_HEADS * HEAD_SIZE, MODEL_WIDTH), (QUERY_HEADS * HEAD_SIZE // 64) ** -0.5, 1.25, ((0, 16),))
    ffn_gain = jnp.clip(1.0 + 0.1 * jax.random.normal(keys[10], (MODEL_WIDTH,), jnp.float32), 0.5, 1.5).astype(jnp.bfloat16)
    w_router = bell_draw(keys[11], (MODEL_WIDTH, EXPERTS), (4 * MODEL_WIDTH) ** -0.5, 0.078125, ((0, 16),))
    w_gate = bell_draw(keys[12], (EXPERTS, MODEL_WIDTH, FF), MODEL_WIDTH ** -0.5, 0.15625, ((0, 8),))
    w_up = bell_draw(keys[13], (EXPERTS, MODEL_WIDTH, FF), MODEL_WIDTH ** -0.5, 0.15625, ((0, 8),))
    w_down = bell_draw(keys[14], (EXPERTS, FF, MODEL_WIDTH), (FF // 16) ** -0.5, 1.0, ((0, 8),))
    return {"hidden": hidden, "cotangent": cotangent, "token_order": token_order, "lengths": lengths, "routes": routes, "attn_gain": attn_gain, "w_query": w_query, "key_weight": key_weight, "value_weight": value_weight, "w_out": w_out, "ffn_gain": ffn_gain, "w_router": w_router, "w_gate": w_gate, "w_up": w_up, "w_down": w_down}


norm_eps = 1e-06
rope_base = 10000.0
masked_score = -1e+30

@jax.custom_vjp
def lower_precision(v):
    return lax.optimization_barrier(v.astype(jnp.bfloat16)).astype(jnp.float32)

@jax.custom_vjp
def lower_precision_backward(v):
    return v

def low_keep(v):
    return (lower_precision(v), None)

def low_pass(kept, grad):
    return (grad,)

def back_keep(v):
    return (v, None)

def back_low(kept, grad):
    return (lower_precision(grad),)
lower_precision.defvjp(low_keep, low_pass)
lower_precision_backward.defvjp(back_keep, back_low)

def matrix_product(left_arg, right_arg):
    return jnp.dot(left_arg, right_arg, precision=lax.Precision.HIGHEST, preferred_element_type=jnp.float32)

def rms_norm(values, gain_vec):
    inv_rms = lax.rsqrt(lax.optimization_barrier(jnp.mean(values * values, axis=-1, keepdims=True)) + norm_eps)
    return values * inv_rms * gain_vec

def angles(token_positions):
    half_dim = HEAD_SIZE // 2
    frequency = rope_base ** (-(jnp.arange(half_dim, dtype=jnp.float32) * 2.0 / HEAD_SIZE))
    turned = token_positions.astype(jnp.float32)[:, None] * frequency[None, :]
    return (jnp.cos(turned), jnp.sin(turned))

def rotate(values, cosine_table, sine_table):
    half_dim = HEAD_SIZE // 2
    front_half = values[..., :half_dim]
    back_half = values[..., half_dim:]
    cos_rows = cosine_table[:, None, :]
    sin_rows = sine_table[:, None, :]
    return jnp.concatenate([front_half * cos_rows - back_half * sin_rows, back_half * cos_rows + front_half * sin_rows], axis=-1)

def group_info(token_positions, seq_lengths):
    seq_ends = jnp.cumsum(seq_lengths).astype(jnp.int32)
    seq_starts = (seq_ends - seq_lengths).astype(jnp.int32)
    document_rows = lax.optimization_barrier(jnp.sum((token_positions[:, None] >= seq_ends[None, :]).astype(jnp.int32), axis=1)).astype(jnp.int32)
    picked = document_rows[:, None] == jnp.arange(NSEQ, dtype=jnp.int32)[None, :]
    offset = lax.optimization_barrier(jnp.sum(jnp.where(picked, seq_starts[None, :], 0), axis=1)).astype(jnp.int32)
    return (document_rows, (token_positions - offset).astype(jnp.int32))

def dispatch_index(route_rows, expert_count, capacity):
    flat_ids = route_rows.reshape(-1)
    pair_count = flat_ids.shape[0]
    one_hot = (flat_ids[:, None] == jnp.arange(expert_count, dtype=jnp.int32)[None, :]).astype(jnp.int32)
    before = (jnp.cumsum(one_hot, axis=0) - one_hot).astype(jnp.int32)
    slot_ids = lax.optimization_barrier(jnp.sum(before * one_hot, axis=1)).astype(jnp.int32)
    placed = (flat_ids * capacity + slot_ids).astype(jnp.int32)
    source = jnp.full((expert_count * capacity,), pair_count, jnp.int32).at[placed].set(jnp.arange(pair_count, dtype=jnp.int32))
    return (source, placed)

def attend(query_rows, key_matrix_rows, value_matrix_rows, document_rows, token_positions):
    local_tokens = query_rows.shape[0]
    grouped_rows = query_rows.reshape(local_tokens, KEY_VALUE_HEADS, QUERY_HEADS // KEY_VALUE_HEADS, HEAD_SIZE)
    scores = lower_precision_backward(jnp.einsum('tkgd,nkd->kgtn', grouped_rows, key_matrix_rows, precision=lax.Precision.HIGHEST))
    allowed = (document_rows[:, None] == document_rows[None, :]) & (token_positions[None, :] <= token_positions[:, None])
    probs_f = jax.nn.softmax(jnp.where(allowed[None, None], scores, masked_score), axis=-1)
    mixed_rows = jnp.einsum('kgtn,nkd->tkgd', lower_precision(probs_f), value_matrix_rows, precision=lax.Precision.HIGHEST)
    return mixed_rows.reshape(local_tokens, QUERY_HEADS * HEAD_SIZE)

def attend_packed_documents(packed):
    return attend(*packed)

def block_slice(params, block_x, document_rows, token_positions, rel_places, route_rows, row_index, pair_index):
    attn_gain, w_query, key_weight, value_weight, w_out, ffn_gain, w_router, w_gate, w_up, w_down = params
    head_groups = block_x.shape[0]
    flat_rows = block_x.reshape(-1, MODEL_WIDTH)
    count_of_rows = flat_rows.shape[0]
    normalized_input = lower_precision(rms_norm(flat_rows, attn_gain))
    cosine_table, sine_table = angles(rel_places.reshape(-1))
    q_proj = lower_precision_backward(matrix_product(normalized_input, w_query)).reshape(count_of_rows, QUERY_HEADS, HEAD_SIZE)
    query_rows = lower_precision(rotate(q_proj, cosine_table, sine_table) * HEAD_SIZE ** (-0.5))
    key_projected = lower_precision_backward(matrix_product(normalized_input, key_weight)).reshape(count_of_rows, KEY_VALUE_HEADS, HEAD_SIZE)
    key_matrix_rows = lower_precision(rotate(key_projected, cosine_table, sine_table))
    value_matrix_rows = lower_precision(lower_precision_backward(matrix_product(normalized_input, value_weight))).reshape(count_of_rows, KEY_VALUE_HEADS, HEAD_SIZE)
    attention_output = lax.map(jax.checkpoint(attend_packed_documents), (query_rows.reshape(head_groups, -1, QUERY_HEADS, HEAD_SIZE), key_matrix_rows.reshape(head_groups, -1, KEY_VALUE_HEADS, HEAD_SIZE), value_matrix_rows.reshape(head_groups, -1, KEY_VALUE_HEADS, HEAD_SIZE), document_rows, token_positions))
    attn_low = lower_precision(lower_precision_backward(attention_output.reshape(count_of_rows, QUERY_HEADS * HEAD_SIZE)))
    branch = lower_precision_backward(matrix_product(attn_low, w_out))
    middle = flat_rows + branch
    normed_ffn = lower_precision(rms_norm(middle, ffn_gain))
    logits = matrix_product(normed_ffn, w_router)
    gate_probs = jax.nn.softmax(jnp.take_along_axis(logits, route_rows, axis=1), axis=-1)
    padded = jnp.concatenate([normed_ffn, jnp.zeros((1, MODEL_WIDTH), jnp.float32)], axis=0)
    expert_in = lower_precision_backward(padded[row_index])
    gate_val = lower_precision_backward(jnp.einsum('erd,edf->erf', expert_in, w_gate, precision=lax.Precision.HIGHEST))
    up_val = lower_precision_backward(jnp.einsum('erd,edf->erf', expert_in, w_up, precision=lax.Precision.HIGHEST))
    active = lower_precision(jax.nn.silu(gate_val) * up_val)
    expert_out = lower_precision(lower_precision_backward(jnp.einsum('erf,efd->erd', active, w_down, precision=lax.Precision.HIGHEST)))
    pair_out = expert_out.reshape(-1, MODEL_WIDTH)[pair_index].reshape(count_of_rows, -1, MODEL_WIDTH)
    mixture = lax.optimization_barrier(jnp.sum(gate_probs[:, :, None] * pair_out, axis=1))
    return middle + mixture

def arrange(values):
    return jnp.swapaxes(values.reshape((N_EXPERT, N_DP) + values.shape[1:]), 0, 1)

def reference(hidden, cotangent, token_order, lengths, routes, attn_gain, w_query, key_weight, value_weight, w_out, ffn_gain, w_router, w_gate, w_up, w_down):
    params = tuple((weight.astype(jnp.float32) for weight in (attn_gain, w_query, key_weight, value_weight, w_out, ffn_gain, w_router, w_gate, w_up, w_down)))
    document_rows, rel_places = jax.vmap(group_info)(token_order, lengths)
    route_src = arrange(routes).reshape(N_DP, EXPERTS, TOK_DEV, TOP)
    source, placed = jax.vmap(jax.vmap(partial(dispatch_index, expert_count=EXPERTS, capacity=CAP)))(route_src)
    src_ids = jnp.arange(EXPERTS, dtype=jnp.int32)
    local_tok = (source // TOP).astype(jnp.int32)
    global_row = jnp.where(local_tok < TOK_DEV, src_ids[None, :, None] * TOK_DEV + local_tok, EXPERTS * TOK_DEV).astype(jnp.int32)
    row_index = jnp.swapaxes(global_row.reshape(N_DP, EXPERTS, EXPERTS, CAP), 1, 2).reshape(N_DP, EXPERTS, EXPERTS * CAP)
    pair_index = (placed // CAP * (EXPERTS * CAP) + src_ids[None, :, None] * CAP + placed % CAP).astype(jnp.int32).reshape(N_DP, -1)
    route_flat = route_src.reshape(N_DP, EXPERTS * TOK_DEV, TOP)
    doc_arranged = arrange(document_rows)
    order_arranged = arrange(token_order)
    rel_arranged = arrange(rel_places)

    def forward(weights, inputs):
        blocks = arrange(inputs)

        def scan_step(unused_state, packed):
            return (unused_state, jax.checkpoint(block_slice)(weights, *packed))
        _, outputs = lax.scan(scan_step, None, (blocks, doc_arranged, order_arranged, rel_arranged, route_flat, row_index, pair_index))
        return jnp.swapaxes(outputs.reshape(N_DP, N_EXPERT, GROUP_TOK, MODEL_WIDTH), 0, 1).reshape(GROUPS, GROUP_TOK, MODEL_WIDTH)
    result, pullback = jax.vjp(forward, params, hidden.astype(jnp.float32))
    grad_params, grad_input = pullback(cotangent.astype(jnp.float32))
    return (result.astype(jnp.bfloat16), grad_input.astype(jnp.bfloat16), grad_params[0], grad_params[1], grad_params[2], grad_params[3], grad_params[4], grad_params[5], grad_params[6], grad_params[7], grad_params[8], grad_params[9])
```

```python
import functools

import jax
import jax.numpy as jnp
from jax import lax
from jax.experimental import pallas as pl
from jax.experimental.pallas import tpu as pltpu
from jax.sharding import PartitionSpec as P

MODEL_WIDTH = 1536
QUERY_HEADS = 24
KEY_VALUE_HEADS = 8
HEAD_SIZE = 64
MOST_LEN = 512
NORM_EPS = 1e-06
ROPE_BASE = 10000.0
MASKED = -1e30
QROWS = 128
LANES = 128
bf16 = jnp.bfloat16
f32 = jnp.float32
ANY = pl.BlockSpec(memory_space=pl.ANY)
VMEM = pl.BlockSpec(memory_space=pltpu.VMEM)
SMEM = pl.BlockSpec(memory_space=pltpu.SMEM)
NT = (((1,), (1,)), ((), ()))
TN = (((0,), (0,)), ((), ()))


def params(limit=56):
    return pltpu.CompilerParams(vmem_limit_bytes=limit * 1024 * 1024)


def cost(flops, nbytes):
    return pl.CostEstimate(flops=int(flops), bytes_accessed=int(nbytes), transcendentals=0)


def dot(a, b, dims=(((1,), (0,)), ((), ()))):
    return lax.dot_general(a, b, dims, preferred_element_type=f32)


def lane_iota(rows):
    return lax.broadcasted_iota(jnp.int32, (rows, LANES), 1)


def half_swap(v):
    lane = lane_iota(v.shape[0])
    low = lax.rem(lane, HEAD_SIZE) < HEAD_SIZE // 2
    up = pltpu.roll(v, LANES - HEAD_SIZE // 2, 1)
    down = pltpu.roll(v, HEAD_SIZE // 2, 1)
    return jnp.where(low, up, down)


def three_parts(v):
    hi = v.astype(bf16).astype(f32)
    mid = (v - hi).astype(bf16).astype(f32)
    return hi, mid, v - hi - mid


def with_parts(base, v):
    lane = lane_iota(base.shape[0])
    hi, mid, lo = three_parts(v)
    out = jnp.where(lane == HEAD_SIZE, hi, base)
    out = jnp.where(lane == HEAD_SIZE + 1, mid, out)
    return jnp.where(lane == HEAD_SIZE + 2, lo, out)


def attn_fwd_kernel(
    n_ctx, n_dp, qh, kvh, place_ref, *refs
):
    x_refs, refs = refs[:n_ctx], refs[n_ctx:]
    w_refs, refs = refs[:n_dp], refs[n_dp:]
    (gain_ref, row_ref, col_ref, start_ref, cos_ref, sin_ref), refs = refs[:6], refs[6:]
    (h1_ref, attn_ref, q_ref, k_ref, v_ref, w_ref), refs = refs[:6], refs[6:]
    x_buf, qkv_buf, sorted_buf, sem_x, sem_w = refs
    tok = x_buf.shape[1]
    total = n_ctx * tok
    group = qh // kvh
    copies = [pltpu.make_async_copy(x_refs[m], x_buf.at[m], sem_x.at[m]) for m in range(n_ctx)]
    w_copies = [
        pltpu.make_async_copy(
            w_refs[k].at[m], w_ref.at[place_ref[k * n_ctx + m]], sem_w.at[k * n_ctx + m]
        )
        for k in range(n_dp)
        for m in range(n_ctx)
    ]
    for c in copies + w_copies:
        c.start()
    for c in copies + w_copies:
        c.wait()
    q_chunks = qh * HEAD_SIZE // LANES
    k_chunks = kvh * HEAD_SIZE // LANES

    def project(m, carry):
        x = x_buf[m].astype(f32)
        r = lax.rsqrt(jnp.mean(x * x, axis=-1, keepdims=True) + NORM_EPS)
        h = (x * r * gain_ref[...]).astype(bf16)
        h1_ref[m] = h
        w = w_ref[...].reshape(MODEL_WIDTH, w_ref.shape[2])
        qkv = dot(h, w)
        rows = pl.ds(m * tok, tok)
        cos, sin = cos_ref[rows, :], sin_ref[rows, :]
        out = []
        for j in range(q_chunks + 2 * k_chunks):
            piece = qkv[:, j * LANES : (j + 1) * LANES]
            if j < q_chunks + k_chunks:
                piece = piece * cos + half_swap(piece) * sin
                if j < q_chunks:
                    piece = piece * HEAD_SIZE**-0.5
            out.append(piece)
        qkv_buf[rows, :] = jnp.concatenate(out, axis=1).astype(bf16)
        return carry

    lax.fori_loop(0, n_ctx, project, 0)

    def arrange(b, carry):
        rows = pl.ds(b * tok, tok)
        place = lax.broadcasted_iota(jnp.int32, (tok, total), 0) + b * tok
        pick = (place == row_ref[...]).astype(f32).astype(bf16)
        s = dot(pick, qkv_buf[...])
        lane = lane_iota(tok)
        ones = jnp.where(lane < HEAD_SIZE + 3, 1.0, 0.0)
        for h in range(qh + 2 * kvh):
            piece = s[:, (h // 2) * LANES : (h // 2 + 1) * LANES]
            if h % 2:
                piece = pltpu.roll(piece, HEAD_SIZE, 1)
            fill = jnp.zeros_like(ones) if h < qh else ones
            piece = jnp.where(lane < HEAD_SIZE, piece, fill).astype(bf16)
            if h < qh:
                q_ref[h, rows, :] = piece
            elif h < qh + kvh:
                k_ref[h - qh, rows, :] = piece
            else:
                v_ref[h - qh - kvh, rows, :] = piece
        return carry

    lax.fori_loop(0, n_ctx, arrange, 0)
    window = min(MOST_LEN + QROWS, total)

    def attend(b, carry):
        q0 = pl.multiple_of(b * QROWS, QROWS)
        k0 = pl.multiple_of(jnp.maximum(q0 + QROWS - window, 0), QROWS)
        rows, keys = pl.ds(q0, QROWS), pl.ds(k0, window)
        kidx = lax.broadcasted_iota(jnp.int32, (QROWS, window), 1) + k0
        qidx = lax.broadcasted_iota(jnp.int32, (QROWS, window), 0) + q0
        allowed = (kidx <= qidx) & (kidx >= start_ref[rows, :])
        outs = []
        for g in range(kvh):
            q = q_ref[g * group : (g + 1) * group, rows, :].reshape(group * QROWS, LANES)
            s = dot(q, k_ref[g, keys, :], NT).reshape(group, QROWS, window)
            s = jnp.where(allowed[None], s, MASKED)
            top = jnp.max(s, axis=-1, keepdims=True)
            e = jnp.exp(s - top)
            o = dot(e.astype(bf16).reshape(group * QROWS, window), v_ref[g, keys, :])
            o = o.reshape(group, QROWS, LANES)
            total_e = o[:, :, HEAD_SIZE : HEAD_SIZE + 1]
            lse = top + jnp.log(total_e)
            o = o / total_e
            for i in range(group):
                h = g * group + i
                base = q_ref[h, rows, :].astype(f32)
                q_ref[h, rows, :] = with_parts(base, -lse[i]).astype(bf16)
                outs.append(o[i])
        lane = lane_iota(QROWS)
        for j in range(q_chunks):
            pair = jnp.where(lane < HEAD_SIZE, outs[2 * j], pltpu.roll(outs[2 * j + 1], HEAD_SIZE, 1))
            sorted_buf[rows, j * LANES : (j + 1) * LANES] = pair.astype(bf16)
        return carry

    lax.fori_loop(0, total // QROWS, attend, 0)

    def scatter(m, carry):
        place = lax.broadcasted_iota(jnp.int32, (tok, total), 1)
        pick = (place == col_ref[pl.ds(m * tok, tok), :]).astype(f32).astype(bf16)
        attn_ref[m] = dot(pick, sorted_buf[...]).astype(bf16)
        return carry

    lax.fori_loop(0, n_ctx, scatter, 0)


def attn_fwd(places, x_pieces, w_pieces, gain, row, col, start_col, cos, sin, qh, kvh):
    n_ctx, n_dp = len(x_pieces), len(w_pieces)
    tok = x_pieces[0].shape[0]
    total = n_ctx * tok
    rows, width = w_pieces[0].shape[1:]
    shape = jax.ShapeDtypeStruct
    return pl.pallas_call(
        functools.partial(attn_fwd_kernel, n_ctx, n_dp, qh, kvh),
        out_shape=(
            shape((n_ctx, tok, MODEL_WIDTH), bf16),
            shape((n_ctx, tok, qh * HEAD_SIZE), bf16),
            shape((qh, total, LANES), bf16),
            shape((kvh, total, LANES), bf16),
            shape((kvh, total, LANES), bf16),
            shape((n_ctx * n_dp, rows, width), bf16),
        ),
        in_specs=[SMEM] + [ANY] * (n_ctx + n_dp) + [VMEM] * 6,
        out_specs=(VMEM,) * 6,
        scratch_shapes=[
            pltpu.VMEM((n_ctx, tok, MODEL_WIDTH), bf16),
            pltpu.VMEM((total, width), bf16),
            pltpu.VMEM((total, qh * HEAD_SIZE), bf16),
            pltpu.SemaphoreType.DMA((n_ctx,)),
            pltpu.SemaphoreType.DMA((n_ctx * n_dp,)),
        ],
        compiler_params=params(),
        cost_estimate=cost(20e9, 20e6),
        name="attn_fwd",
    )(places, *x_pieces, *w_pieces, gain, row, col, start_col, cos, sin)


def attn_bwd_kernel(n_ctx, qh, kvh, *refs):
    db_refs, refs = refs[:n_ctx], refs[n_ctx:]
    (wo_ref, attn_ref, q_ref, k_ref, v_ref), refs = refs[:5], refs[5:]
    (row_ref, col_ref, start_ref, cos_ref, sin_ref), refs = refs[:5], refs[5:]
    out_ref, db_buf, dat_buf, do_buf, dq_buf, dk_buf, dv_buf, dqkv_buf, sem = refs
    tok = db_buf.shape[1]
    total = n_ctx * tok
    group = qh // kvh
    q_chunks = qh * HEAD_SIZE // LANES
    k_chunks = kvh * HEAD_SIZE // LANES
    copies = [pltpu.make_async_copy(db_refs[m], db_buf.at[m], sem.at[m]) for m in range(n_ctx)]
    for c in copies:
        c.start()
    dk_buf[...] = jnp.zeros_like(dk_buf)
    dv_buf[...] = jnp.zeros_like(dv_buf)
    for c in copies:
        c.wait()
    q_width = qh * HEAD_SIZE

    def lift(m, carry):
        rows = pl.ds(m * tok, tok)
        low = dot(db_buf[m], wo_ref[...], NT).astype(bf16)
        dat_buf[rows, :q_width] = low
        prod = low.astype(f32) * attn_ref[m].astype(f32)
        lane = lane_iota(tok)
        parts = jnp.zeros((tok, LANES), f32)
        for h in range(qh):
            delta = -jnp.sum(prod[:, h * HEAD_SIZE : (h + 1) * HEAD_SIZE], axis=1, keepdims=True)
            for i, v in enumerate(three_parts(delta)):
                parts = jnp.where(lane == 3 * h + i, v, parts)
        dat_buf[rows, q_width:] = parts.astype(bf16)
        return carry

    lax.fori_loop(0, n_ctx, lift, 0)

    def arrange(b, carry):
        rows = pl.ds(b * tok, tok)
        place = lax.broadcasted_iota(jnp.int32, (tok, total), 0) + b * tok
        pick = (place == row_ref[...]).astype(f32).astype(bf16)
        s = dot(pick, dat_buf[...])
        lane = lane_iota(tok)
        extra = s[:, q_width:]
        for h in range(qh):
            piece = s[:, (h // 2) * LANES : (h // 2 + 1) * LANES]
            if h % 2:
                piece = pltpu.roll(piece, HEAD_SIZE, 1)
            tail = pltpu.roll(extra, HEAD_SIZE - 3 * h, 1)
            tail = jnp.where(lane < HEAD_SIZE + 3, tail, 0.0)
            do_buf[h, rows, :] = jnp.where(lane < HEAD_SIZE, piece, tail).astype(bf16)
        return carry

    lax.fori_loop(0, n_ctx, arrange, 0)
    window = min(MOST_LEN + QROWS, total)

    def attend(b, carry):
        q0 = pl.multiple_of(b * QROWS, QROWS)
        k0 = pl.multiple_of(jnp.maximum(q0 + QROWS - window, 0), QROWS)
        rows, keys = pl.ds(q0, QROWS), pl.ds(k0, window)
        kidx = lax.broadcasted_iota(jnp.int32, (window, QROWS), 0) + k0
        qidx = lax.broadcasted_iota(jnp.int32, (window, QROWS), 1) + q0
        allowed = (kidx <= qidx) & (kidx >= start_ref[:, rows])
        allowed = jnp.concatenate([allowed.astype(f32)] * group, axis=1) > 0.5
        for g in range(kvh):
            heads = slice(g * group, (g + 1) * group)
            q = q_ref[heads, rows, :].reshape(group * QROWS, LANES)
            do = do_buf[heads, rows, :].reshape(group * QROWS, LANES)
            k, v = k_ref[g, keys, :], v_ref[g, keys, :]
            p = jnp.where(allowed, jnp.exp(dot(k, q, NT)), 0.0)
            ds = (p * dot(v, do, NT)).astype(bf16)
            dv_buf[g, keys, :] += dot(p.astype(bf16), do)
            dk_buf[g, keys, :] += dot(ds, q)
            dq = dot(ds, k, TN)
            dq_buf[heads, rows, :] = dq.reshape(group, QROWS, LANES)
        return carry

    lax.fori_loop(0, total // QROWS, attend, 0)

    def turn_back(b, carry):
        rows = pl.ds(b * tok, tok)
        cos, sin = cos_ref[rows, :], sin_ref[rows, :]
        lane = lane_iota(tok)
        heads = [dq_buf[h, rows, :] for h in range(qh)]
        heads += [dk_buf[h, rows, :] for h in range(kvh)]
        heads += [dv_buf[h, rows, :] for h in range(kvh)]
        for j in range(q_chunks + 2 * k_chunks):
            pair = jnp.where(lane < HEAD_SIZE, heads[2 * j], pltpu.roll(heads[2 * j + 1], HEAD_SIZE, 1))
            if j < q_chunks:
                pair = pair * HEAD_SIZE**-0.5
            if j < q_chunks + k_chunks:
                pair = pair * cos - half_swap(pair) * sin
            dqkv_buf[rows, j * LANES : (j + 1) * LANES] = pair.astype(bf16)
        return carry

    lax.fori_loop(0, n_ctx, turn_back, 0)

    def scatter(m, carry):
        place = lax.broadcasted_iota(jnp.int32, (tok, total), 1)
        pick = (place == col_ref[pl.ds(m * tok, tok), :]).astype(f32).astype(bf16)
        out_ref[m] = dot(pick, dqkv_buf[...]).astype(bf16)
        return carry

    lax.fori_loop(0, n_ctx, scatter, 0)


def attn_bwd(db_pieces, wo, attn, q, k, v, row, col, start_row, cos, sin, qh, kvh):
    n_ctx = len(db_pieces)
    tok = db_pieces[0].shape[0]
    total = n_ctx * tok
    width = (qh + 2 * kvh) * HEAD_SIZE
    return pl.pallas_call(
        functools.partial(attn_bwd_kernel, n_ctx, qh, kvh),
        out_shape=jax.ShapeDtypeStruct((n_ctx, tok, width), bf16),
        in_specs=[ANY] * n_ctx + [VMEM] * 10,
        out_specs=VMEM,
        scratch_shapes=[
            pltpu.VMEM((n_ctx, tok, MODEL_WIDTH), bf16),
            pltpu.VMEM((total, qh * HEAD_SIZE + LANES), bf16),
            pltpu.VMEM((qh, total, LANES), bf16),
            pltpu.VMEM((qh, total, LANES), f32),
            pltpu.VMEM((kvh, total, LANES), f32),
            pltpu.VMEM((kvh, total, LANES), f32),
            pltpu.VMEM((total, width), bf16),
            pltpu.SemaphoreType.DMA((n_ctx,)),
        ],
        compiler_params=params(),
        cost_estimate=cost(25e9, 20e6),
        name="attn_bwd",
    )(*db_pieces, wo, attn, q, k, v, row, col, start_row, cos, sin)


def expert_math(e, cap, experts, h_blocks, dy_blocks, route_blocks, wg, wu, wd, wr):
    tok = h_blocks[0].shape[0]
    before = lax.broadcasted_iota(jnp.int32, (tok, tok), 0) < lax.broadcasted_iota(
        jnp.int32, (tok, tok), 1
    )
    before = before.astype(f32).astype(bf16)
    names = lax.broadcasted_iota(jnp.int32, (LANES, tok), 0)
    slots = lax.broadcasted_iota(jnp.int32, (cap, tok), 0).astype(f32)
    picks, xs, dys, masks = [], [], [], []
    for h, dy, routes in zip(h_blocks, dy_blocks, route_blocks):
        hit = jnp.zeros((1, tok), f32)
        named = jnp.zeros((LANES, tok), f32)
        for j in range(routes.shape[0]):
            hit = hit + jnp.where(routes[j : j + 1] == e, 1.0, 0.0)
            named = named + jnp.where(names == routes[j : j + 1], 1.0, 0.0)
        hits = jnp.broadcast_to(hit, (8, tok)).astype(bf16)
        slot = dot(hits, before)[0:1]
        pick = jnp.where((slots == slot) & (hit > 0.5), 1.0, 0.0).astype(bf16)
        picks.append(pick)
        xs.append(dot(pick, h))
        dys.append(dot(pick, dy))
        masks.append(dot(pick, named.astype(bf16), NT))
    xs = jnp.concatenate(xs, axis=0).astype(bf16)
    dys = jnp.concatenate(dys, axis=0)
    mask = jnp.concatenate(masks, axis=0) > 0.5
    gate = dot(xs, wg)
    up = dot(xs, wu)
    sig = jax.nn.sigmoid(gate)
    silu = gate * sig
    act = (silu * up).astype(bf16)
    eout = dot(act, wd).astype(bf16).astype(f32)
    logits = jnp.where(mask, dot(xs, wr), MASKED)
    ex = jnp.where(mask, jnp.exp(logits - jnp.max(logits, axis=1, keepdims=True)), 0.0)
    lane = lax.broadcasted_iota(jnp.int32, ex.shape, 1)
    own = lane == e
    denom = jnp.sum(ex, axis=1, keepdims=True)
    probs = ex / jnp.where(denom > 0.0, denom, 1.0)
    gp = jnp.sum(jnp.where(own, probs, 0.0), axis=1, keepdims=True)
    dgp = jnp.sum(dys * eout, axis=1, keepdims=True)
    coef = gp * dgp * (jnp.where(own, 1.0, 0.0) - probs)
    hi = coef.astype(bf16).astype(f32)
    low = pltpu.roll(coef - hi, LANES // 2, 1)
    coef = jnp.where(lane < LANES // 2, hi, low).astype(bf16)
    deout = (gp * dys).astype(bf16)
    yrow = (gp * eout).astype(bf16)
    dact = dot(deout, wd, NT)
    dgate = (dact * up * sig * (1.0 + gate * (1.0 - sig))).astype(bf16)
    dup = (dact * silu).astype(bf16)
    lane_w = lax.broadcasted_iota(jnp.int32, wr.shape, 1)
    both = jnp.where(lane_w < LANES // 2, wr.astype(f32), pltpu.roll(wr.astype(f32), LANES // 2, 1))
    drow = dot(dgate, wg, NT) + dot(dup, wu, NT) + dot(coef, both.astype(bf16), NT)
    drow = drow.astype(bf16)
    d_out, y_out = [], []
    for i, pick in enumerate(picks):
        rows = slice(i * cap, (i + 1) * cap)
        d_out.append(dot(pick, drow[rows], TN).astype(bf16))
        y_out.append(dot(pick, yrow[rows], TN).astype(bf16))
    return d_out, y_out, xs, deout, act, dgate, dup, coef


def expert_kernel(pieces, cap, experts, e_ref, *refs):
    n_in = len(pieces)
    h_refs, refs = refs[:n_in], refs[n_in:]
    dy_refs, refs = refs[:n_in], refs[n_in:]
    (routes_ref, wg_ref, wu_ref, wd_ref, wr_ref), refs = refs[:5], refs[5:]
    outs, refs = refs[:10], refs[10:]
    step = pl.program_id(0)
    if len(refs):
        h_buf, dy_buf, sem = refs

        def copies(which):
            got = []
            for i, (block, col, width) in enumerate(pieces):
                if block // 2 == which:
                    spot = (block, slice(None), slice(col, col + width))
                    got.append(pltpu.make_async_copy(h_refs[i], h_buf.at[spot], sem.at[0, i]))
                    got.append(pltpu.make_async_copy(dy_refs[i], dy_buf.at[spot], sem.at[1, i]))
            return got

        n_steps = h_buf.shape[0] // 2

        @pl.when(step == 0)
        def _():
            for s in range(n_steps):
                for c in copies(s):
                    c.start()

        for s in range(n_steps):

            @pl.when(step == s)
            def _():
                for c in copies(s):
                    c.wait()

        h_blocks = [h_buf[2 * step + i] for i in range(2)]
        dy_blocks = [dy_buf[2 * step + i] for i in range(2)]
    else:
        h_blocks = [h_refs[0][i] for i in range(2)]
        dy_blocks = [dy_refs[0][i] for i in range(2)]
    routes = [routes_ref[2 * step + i] for i in range(2)]
    d_out, y_out, xs, deout, act, dgate, dup, coef = expert_math(
        e_ref[0], cap, experts, h_blocks, dy_blocks, routes,
        wg_ref[...], wu_ref[...], wd_ref[...], wr_ref[...],
    )
    outs[0][0] = d_out[0]
    outs[1][0] = d_out[1]
    outs[2][0] = y_out[0]
    outs[3][0] = y_out[1]
    for ref, v in zip(outs[4:], (xs, deout, act, dgate, dup, coef)):
        ref[...] = v


def run_experts(e, pieces, h_list, dy_list, routes_t, wg, wu, wd, wr, cap, experts, tok):
    n_blocks = routes_t.shape[0]
    steps = n_blocks // 2
    ff = wg.shape[1]
    rows = 2 * cap
    shape = jax.ShapeDtypeStruct
    block = pl.BlockSpec((1, tok, MODEL_WIDTH), lambda i, *_: (i, 0, 0))
    wide = pl.BlockSpec((rows, MODEL_WIDTH), lambda i, *_: (i, 0))
    thin = pl.BlockSpec((rows, ff), lambda i, *_: (i, 0))
    edge = pl.BlockSpec((rows, LANES), lambda i, *_: (i, 0))
    whole = pl.BlockSpec((2, tok, MODEL_WIDTH), lambda i, *_: (i, 0, 0))
    by_hand = pieces is not None
    n_in = len(h_list)
    scratch = []
    if by_hand:
        scratch = [
            pltpu.VMEM((n_blocks, tok, MODEL_WIDTH), bf16),
            pltpu.VMEM((n_blocks, tok, MODEL_WIDTH), bf16),
            pltpu.SemaphoreType.DMA((2, n_in)),
        ]
    grid_spec = pltpu.PrefetchScalarGridSpec(
        num_scalar_prefetch=1,
        grid=(steps,),
        in_specs=[ANY if by_hand else whole] * (2 * n_in) + [VMEM] * 5,
        out_specs=[block] * 4 + [wide] * 2 + [thin] * 3 + [edge],
        scratch_shapes=scratch,
    )
    half = shape((steps, tok, MODEL_WIDTH), bf16)
    return pl.pallas_call(
        functools.partial(
            expert_kernel, pieces if by_hand else [None] * n_in, cap, experts
        ),
        out_shape=[half] * 4
        + [shape((steps * rows, MODEL_WIDTH), bf16)] * 2
        + [shape((steps * rows, ff), bf16)] * 3
        + [shape((steps * rows, LANES), bf16)],
        grid_spec=grid_spec,
        compiler_params=params(60),
        cost_estimate=cost(30e9, 30e6),
        name="experts",
    )(e, *h_list, *dy_list, routes_t, wg, wu, wd, wr)


def flip(v, axis, bit):
    n = lax.axis_size(axis)
    return lax.ppermute(v, axis, [(i, i ^ bit) for i in range(n)])


def step_up(v, axis):
    n = lax.axis_size(axis)
    return lax.ppermute(v, axis, [(i, (i + 1) % n) for i in range(n)])


def ctx_gather(v):
    n = lax.axis_size("context")
    pieces = {0: v}
    bit = n // 2
    while bit:
        for m in list(pieces):
            pieces[m | bit] = flip(pieces[m], "context", bit)
        bit //= 2
    return [pieces[m] for m in range(n)]


def add_low(a, b):
    return (a.astype(f32) + b.astype(f32)).astype(bf16)


def ring(v, axis):
    pieces = [v]
    for _ in range(lax.axis_size(axis) - 1):
        pieces.append(step_up(pieces[-1], axis))
    return pieces


def ring_sum(chunk, axis):
    n = lax.axis_size(axis)
    d = lax.axis_index(axis)
    part = chunk(lax.rem(d + n - 1, n)).astype(bf16)
    for s in range(n - 1):
        got = step_up(part, axis)
        part = got.astype(f32) + chunk(lax.rem(d + 2 * n - 2 - s, n)).astype(f32)
        if s < n - 2:
            part = part.astype(bf16)
    return part


def after(v, *deps):
    return lax.optimization_barrier((v, *deps))[0]


HALF = MODEL_WIDTH // 2


def plane_gather(v, wide=True):
    if lax.axis_size("expert") != 2 or lax.axis_size("context") != 4:
        return None, [lax.all_gather(v, ("expert", "context"), axis=0, tiled=False)]
    a, b = v[:, :HALF], v[:, HALF:]
    ay, bx = flip(a, "context", 2), flip(b, "expert", 1)
    ax, by = flip(a, "expert", 1), flip(b, "context", 2)
    axy, bxy = flip(ay, "expert", 1), flip(bx, "context", 2)
    spec, out = [(0, 0, MODEL_WIDTH), (1, 0, MODEL_WIDTH)], [v, flip(v, "context", 1)]
    for block, col, p in (
        (2, 0, ay), (4, HALF, bx), (4, 0, ax), (2, HALF, by), (6, 0, axy), (6, HALF, bxy),
    ):
        spec += [(block, col, HALF), (block + 1, col, HALF)]
        out += [p, flip(p, "context", 1)]
    return spec, out


def plane_sum(even, odd):
    if lax.axis_size("expert") != 2 or lax.axis_size("context") != 4:
        both = jnp.stack([even, odd], axis=1)
        tok, width = even.shape[1:]
        return lax.psum_scatter(
            both.reshape(-1, width), ("expert", "context"), scatter_dimension=0, tiled=True
        ).astype(f32)
    got = flip(odd, "context", 1)
    d3 = add_low(even[3], got[3])
    ga, gb = flip(d3[:, :HALF], "expert", 1), flip(d3[:, HALF:], "context", 2)
    y = add_low(even[1], got[1])
    x = add_low(even[2], got[2])
    yb, xa = flip(y[:, HALF:], "context", 2), flip(x[:, :HALF], "expert", 1)
    ya = flip(add_low(y[:, :HALF], ga), "context", 2)
    xb = flip(add_low(x[:, HALF:], gb), "expert", 1)
    own = even[0].astype(f32) + got[0].astype(f32)
    left = own[:, :HALF] + ya.astype(f32) + xa.astype(f32)
    right = own[:, HALF:] + yb.astype(f32) + xb.astype(f32)
    return jnp.concatenate([left, right], axis=1)


def ctx_sum(p):
    own = p[0].astype(f32) + flip(p[1], "context", 1).astype(f32)
    far = add_low(p[2], flip(p[3], "context", 1))
    return own + flip(far, "context", 2).astype(f32)


def put_in_order(places, pieces, name):
    n = len(pieces)
    rows, width = pieces[0].shape

    def kernel(place_ref, *refs):
        out_ref, sem = refs[n:]
        copies = [
            pltpu.make_async_copy(refs[k], out_ref.at[place_ref[k]], sem.at[k]) for k in range(n)
        ]
        for c in copies:
            c.start()
        for c in copies:
            c.wait()

    return pl.pallas_call(
        kernel,
        out_shape=jax.ShapeDtypeStruct((n, rows, width), pieces[0].dtype),
        in_specs=[SMEM] + [ANY] * n,
        out_specs=ANY,
        scratch_shapes=[pltpu.SemaphoreType.DMA((n,))],
        cost_estimate=cost(0, 2 * n * rows * width * 2),
        name=name,
    )(places, *pieces)


def rms_back(dh, v, r, gain):
    inner = jnp.sum(gain * dh * v, axis=-1, keepdims=True)
    dv = r * gain * dh - v * (r * r * r) * (inner / MODEL_WIDTH)
    return dv, jnp.sum(dh * v * r, axis=0)


def body(
    hidden, cotangent, token_order, lengths, routes, attn_gain, w_query, key_weight,
    value_weight, w_out, ffn_gain, w_router, w_gate, w_up, w_down,
):
    tok, top = hidden.shape[1], routes.shape[2]
    n_exp, n_ctx, n_dp = (lax.axis_size(a) for a in ("expert", "context", "dp"))
    experts = n_exp * n_ctx
    cap = -(-(9 * tok * top // (8 * experts)) // 16) * 16
    qh, kvh = QUERY_HEADS // n_ctx, KEY_VALUE_HEADS // n_ctx
    qw, kw = qh * HEAD_SIZE, kvh * HEAD_SIZE
    rows = w_query.shape[0]
    ex, cx, dx = (lax.axis_index(a) for a in ("expert", "context", "dp"))
    my_expert = ex * n_ctx + cx
    total = n_ctx * tok

    def for_context(c):
        return jnp.concatenate(
            [
                lax.dynamic_slice_in_dim(w_query, c * qw, qw, 1),
                lax.dynamic_slice_in_dim(key_weight, c * kw, kw, 1),
                lax.dynamic_slice_in_dim(value_weight, c * kw, kw, 1),
            ],
            axis=1,
        )

    got = [for_context(cx)]
    for m in range(1, n_ctx):
        got.append(flip(for_context(cx ^ m), "context", m))
    w_pieces = ring(jnp.stack(got), "dp")
    small = jnp.concatenate([attn_gain[None], ffn_gain[None], w_router.T], axis=0)
    small_rows = small.shape[0]
    small = jnp.pad(small, ((0, -small_rows % 8), (0, LANES - rows)))
    small_got = [small] + [flip(small, "context", m) for m in range(1, n_ctx)]
    small_pieces = ring(jnp.stack(small_got), "dp")
    k_of = jnp.arange(n_dp, dtype=jnp.int32)
    d_of = lax.rem(dx - k_of + n_dp, n_dp)
    c_of = cx ^ jnp.arange(n_ctx, dtype=jnp.int32)
    places = (c_of[None, :] * n_dp + d_of[:, None]).reshape(-1).astype(jnp.int32)
    small_all = jnp.stack(small_pieces)[:, :, :small_rows, :rows]
    where_is = (lax.rem(dx - jnp.arange(n_dp) + n_dp, n_dp)[None, :] * n_ctx) + (
        cx ^ jnp.arange(n_ctx)
    )[:, None]
    small_all = small_all.reshape(n_dp * n_ctx, small_rows, rows)[where_is.reshape(-1)]
    small_all = small_all.transpose(1, 0, 2).reshape(small_rows, MODEL_WIDTH)
    gain_a = small_all[0:1].astype(f32)
    gain_b = small_all[1:2].astype(f32)
    wr = jnp.pad(small_all[2:].T, ((0, 0), (0, LANES - experts)))

    x_pieces = ctx_gather(hidden[0])
    order_rel = token_order[0].reshape(n_ctx, tok)[c_of].reshape(-1)
    place_ids = jnp.arange(total, dtype=jnp.int32)
    both = jnp.concatenate([order_rel, place_ids])
    end = jnp.zeros((), jnp.int32)
    start = jnp.zeros_like(both)
    for j in range(lengths.shape[1]):
        end = end + lengths[0, j]
        start = start + jnp.where(both >= end, lengths[0, j], 0)
    half = HEAD_SIZE // 2
    freq = ROPE_BASE ** (-(jnp.arange(half, dtype=f32) * 2.0 / HEAD_SIZE))
    angle = (both - start).astype(f32)[:, None] * freq[None, :]
    cos, sin = jnp.cos(angle), jnp.sin(angle)
    cos = jnp.concatenate([cos] * 4, axis=1)
    sin = jnp.concatenate([-sin, sin] * 2, axis=1)
    row, col = order_rel[None, :], order_rel[:, None]
    start_place = start[total:]

    h1, attn, q, k, v, wqkv = attn_fwd(
        places, x_pieces, w_pieces, gain_a, row, col, start_place[:, None],
        cos[:total], sin[:total], qh, kvh,
    )
    wo_pieces = ring(after(w_out, w_pieces[-1]), "dp")
    wo = put_in_order(d_of.astype(jnp.int32), wo_pieces, "wo").reshape(qw, MODEL_WIDTH)

    dy_own = after(cotangent[0], x_pieces[-1])
    pieces, dy_list = plane_gather(dy_own)
    routes_t = routes[0].T
    if pieces is None:
        routes_all = lax.all_gather(routes_t, ("expert", "context"), axis=0, tiled=False)
    else:
        pr = {0: routes_t}
        for axis, bit, off in (("expert", 1, 4), ("context", 2, 2), ("context", 1, 1)):
            for m in list(pr):
                pr[m | off] = flip(pr[m], axis, bit)
        routes_all = jnp.stack([pr[m] for m in range(8)])

    partial_far = dot(attn[2:].reshape(-1, qw), wo).astype(bf16).reshape(2, tok, MODEL_WIDTH)
    partial_near = dot(attn[:2].reshape(-1, qw), wo).astype(bf16).reshape(2, tok, MODEL_WIDTH)
    x_own = hidden[0].astype(f32)
    middle = x_own + ctx_sum([partial_near[0], partial_near[1], partial_far[0], partial_far[1]])
    r_b = lax.rsqrt(jnp.mean(middle * middle, axis=-1, keepdims=True) + NORM_EPS)
    h2 = (middle * r_b * gain_b).astype(bf16)
    _, h_list = plane_gather(h2)

    wg, wu, wd = w_gate[0], w_up[0], w_down[0]
    d_even, d_odd, y_even, y_odd, xs, deout, act, dgate, dup, coef = run_experts(
        my_expert.reshape(1).astype(jnp.int32), pieces, h_list, dy_list, routes_all,
        wg, wu, wd, wr, cap, experts, tok,
    )
    dh2 = plane_sum(d_even, d_odd)
    g_gate = dot(xs, dgate, TN).astype(bf16)
    g_up = dot(xs, dup, TN).astype(bf16)
    g_down = dot(act, deout, TN).astype(bf16)
    g_router = dot(xs, coef, TN)
    g_router = g_router[:, :experts] + g_router[:, LANES // 2 : LANES // 2 + experts]

    dy = cotangent[0].astype(f32)
    d_norm, g_gain_b = rms_back(dh2, middle, r_b, gain_b)
    d_middle = dy + d_norm
    db_pieces = ctx_gather(d_middle.astype(bf16))
    mixture = plane_sum(after(y_even, db_pieces[2]), after(y_odd, db_pieces[2]))
    output = (middle + mixture).astype(bf16)

    slab = MODEL_WIDTH // n_dp

    def rows_of(g):
        return lambda d: lax.dynamic_slice_in_dim(g, d * slab, slab, 0)

    sum_gate = ring_sum(rows_of(g_gate), "dp")
    sum_up = ring_sum(rows_of(g_up), "dp")
    sum_down = ring_sum(lambda d: lax.dynamic_slice_in_dim(g_down, d * slab, slab, 1), "dp")

    dqkv = attn_bwd(
        db_pieces, wo, attn, q, k, v, row, col, start_place[None, :],
        cos[total:], sin[total:], qh, kvh,
    )
    db_all = jnp.concatenate(db_pieces, axis=0)
    g_out = dot(attn.reshape(total, qw), db_all, TN).astype(bf16)
    dqkv_flat = dqkv.reshape(total, -1)
    g_qkv = dot(h1.reshape(total, MODEL_WIDTH), dqkv_flat, TN).astype(bf16)
    w_flat = wqkv.reshape(MODEL_WIDTH, -1)
    dh1_part = dot(dqkv_flat, w_flat, NT).astype(bf16).reshape(n_ctx, tok, MODEL_WIDTH)
    dh1 = ctx_sum([dh1_part[m] for m in range(n_ctx)])
    r_a = lax.rsqrt(jnp.mean(x_own * x_own, axis=-1, keepdims=True) + NORM_EPS)
    d_in, g_gain_a = rms_back(dh1, x_own, r_a, gain_a)
    grad_input = (d_middle + d_in).astype(bf16)

    def over_experts(part):
        if n_exp == 2:
            low = part.astype(bf16)
            return low.astype(f32) + flip(low, "expert", 1).astype(f32)
        return lax.psum(part.astype(bf16), "expert").astype(f32)

    width = qw + 2 * kw
    g4 = g_qkv.reshape(n_ctx, n_dp, rows, width)
    s_qkv = ring_sum(lambda d: lax.dynamic_index_in_dim(g4, d, 1, keepdims=False), "dp")
    s_qkv = over_experts(s_qkv).astype(bf16)
    s_out = over_experts(
        ring_sum(lambda d: lax.dynamic_slice_in_dim(g_out, d * rows, rows, 0), "dp")
    )
    back = [lax.dynamic_index_in_dim(s_qkv, cx, 0, keepdims=False)]
    for m in range(1, n_ctx):
        back.append(flip(lax.dynamic_index_in_dim(s_qkv, cx ^ m, 0, keepdims=False), "context", m))
    back = jnp.stack(back)[c_of]

    def columns(lo, hi):
        return back[:, :, lo:hi].transpose(1, 0, 2).reshape(rows, -1).astype(f32)

    sum_q, sum_k, sum_v = columns(0, qw), columns(qw, qw + kw), columns(qw + kw, width)
    tiny = jnp.concatenate([g_gain_a[None], g_gain_b[None], g_router.T], axis=0)
    tiny_rows = tiny.shape[0]
    if n_exp == 2:
        tiny = tiny + flip(tiny, "expert", 1)
    else:
        tiny = lax.psum(tiny, "expert")
    tiny = tiny.reshape(tiny_rows, n_ctx * n_dp, rows).transpose(1, 0, 2)
    tiny = lax.all_to_all(tiny, ("context", "dp"), split_axis=0, concat_axis=0, tiled=True)
    tiny = jnp.sum(tiny, axis=0)
    return (
        output[None], grad_input[None], tiny[0], sum_q, sum_k, sum_v, s_out,
        tiny[1], tiny[2:].T, sum_gate[None], sum_up[None], sum_down[None],
    )


def solution(mesh):
    tokens = P(("expert", "dp"), "context", None)
    group = P(("expert", "dp"), None)
    vec, mat = P(("context", "dp")), P(("context", "dp"), None)
    expert = P(("expert", "context"), None, None)
    by_rows = P(("expert", "context"), "dp", None)
    by_cols = P(("expert", "context"), None, "dp")
    return jax.shard_map(
        body,
        mesh=mesh,
        in_specs=(
            tokens, tokens, group, group, tokens, vec, mat, mat, mat, mat, vec, mat,
            expert, expert, expert,
        ),
        out_specs=(
            tokens, tokens, vec, mat, mat, mat, mat, vec, mat, by_rows, by_rows, by_cols,
        ),
        check_vma=False,
    )
```

```python
import functools

import jax
import jax.numpy as jnp
from jax import lax
from jax.experimental import pallas as pl
from jax.experimental.pallas import tpu as pltpu
from jax.sharding import PartitionSpec as P

MODEL_WIDTH = 1536
QUERY_HEADS = 24
KEY_VALUE_HEADS = 8
HEAD_SIZE = 64
MOST_LEN = 512
NORM_EPS = 1e-06
ROPE_BASE = 10000.0
MASKED = -1e30
QROWS = 128
LANES = 128
bf16 = jnp.bfloat16
f32 = jnp.float32
ANY = pl.BlockSpec(memory_space=pl.ANY)
VMEM = pl.BlockSpec(memory_space=pltpu.VMEM)
SMEM = pl.BlockSpec(memory_space=pltpu.SMEM)
NT = (((1,), (1,)), ((), ()))
TN = (((0,), (0,)), ((), ()))


def params(limit=56):
    return pltpu.CompilerParams(vmem_limit_bytes=limit * 1024 * 1024)


def cost(flops, nbytes):
    return pl.CostEstimate(flops=int(flops), bytes_accessed=int(nbytes), transcendentals=0)


def dot(a, b, dims=(((1,), (0,)), ((), ()))):
    return lax.dot_general(a, b, dims, preferred_element_type=f32)


def lane_iota(rows):
    return lax.broadcasted_iota(jnp.int32, (rows, LANES), 1)


def half_swap(v):
    lane = lane_iota(v.shape[0])
    low = lax.rem(lane, HEAD_SIZE) < HEAD_SIZE // 2
    up = pltpu.roll(v, LANES - HEAD_SIZE // 2, 1)
    down = pltpu.roll(v, HEAD_SIZE // 2, 1)
    return jnp.where(low, up, down)


def three_parts(v):
    hi = v.astype(bf16).astype(f32)
    mid = (v - hi).astype(bf16).astype(f32)
    return hi, mid, v - hi - mid


def norm_kernel(n_ctx, *refs):
    x_refs, (gain_ref, h1_ref, x_buf, sem) = refs[:n_ctx], refs[n_ctx:]
    tok = x_buf.shape[1]
    copies = [pltpu.make_async_copy(x_refs[m], x_buf.at[m], sem.at[m]) for m in range(n_ctx)]
    for c in copies:
        c.start()
    for c in copies:
        c.wait()
    step = 64

    def norm(i, carry):
        rows = pl.ds(pl.multiple_of(i % (tok // step) * step, step), step)
        x = x_buf[i // (tok // step), rows, :].astype(f32)
        r = lax.rsqrt(jnp.mean(x * x, axis=-1, keepdims=True) + NORM_EPS)
        h1_ref[i // (tok // step), rows, :] = (x * r * gain_ref[...]).astype(bf16)
        return carry

    lax.fori_loop(0, n_ctx * tok // step, norm, 0)


def norm_rows(x_pieces, gain):
    n_ctx, tok = len(x_pieces), x_pieces[0].shape[0]
    return pl.pallas_call(
        functools.partial(norm_kernel, n_ctx),
        out_shape=jax.ShapeDtypeStruct((n_ctx, tok, MODEL_WIDTH), bf16),
        in_specs=[ANY] * n_ctx + [VMEM],
        out_specs=VMEM,
        scratch_shapes=[
            pltpu.VMEM((n_ctx, tok, MODEL_WIDTH), bf16),
            pltpu.SemaphoreType.DMA((n_ctx,)),
        ],
        compiler_params=params(),
        cost_estimate=cost(3e9, 6e6),
        name="norm_rows",
    )(*x_pieces, gain)


def attn_fwd_kernel(n_ctx, n_w, qh, kvh, place_ref, *refs):
    w_refs, refs = refs[:n_w], refs[n_w:]
    (h1_ref, row_ref, col_ref, start_ref, cos_ref, sin_ref), refs = refs[:6], refs[6:]
    (near_ref, far_ref, q_ref, k_ref, v_ref, lse_ref, w_out), refs = refs[:7], refs[7:]
    w_ref, h1_buf, qkv_buf, sorted_buf, sem_w, sem_h, sem_out = refs
    tok = h1_buf.shape[1]
    total = n_ctx * tok
    group = qh // kvh
    part = w_refs[0].shape[1]
    w_copies = []
    for k in range(n_w):
        for m in range(n_ctx):
            i = k * n_ctx + m
            row0 = pl.multiple_of(place_ref[n_w * n_ctx + k] * part, 16)
            spot = w_ref.at[place_ref[i], pl.ds(row0, part), :]
            w_copies.append(pltpu.make_async_copy(w_refs[k].at[m], spot, sem_w.at[i]))
    h_copies = [pltpu.make_async_copy(h1_ref.at[m], h1_buf.at[m], sem_h.at[m]) for m in range(n_ctx)]
    for c in w_copies + h_copies:
        c.start()
    for c in w_copies + h_copies:
        c.wait()
    keep_w = pltpu.make_async_copy(w_ref, w_out, sem_out)
    keep_w.start()
    q_chunks = qh * HEAD_SIZE // LANES
    k_chunks = kvh * HEAD_SIZE // LANES

    def project(m, carry):
        w = w_ref[...].reshape(MODEL_WIDTH, w_ref.shape[2])
        qkv = dot(h1_buf[m], w)
        rows = pl.ds(m * tok, tok)
        cos, sin = cos_ref[rows, :], sin_ref[rows, :]
        out = []
        for j in range(q_chunks + 2 * k_chunks):
            piece = qkv[:, j * LANES : (j + 1) * LANES]
            if j < q_chunks + k_chunks:
                piece = piece * cos + half_swap(piece) * sin
                if j < q_chunks:
                    piece = piece * HEAD_SIZE**-0.5
            out.append(piece)
        qkv_buf[rows, :] = jnp.concatenate(out, axis=1).astype(bf16)
        return carry

    lax.fori_loop(0, n_ctx, project, 0)

    def arrange(b, carry):
        rows = pl.ds(b * tok, tok)
        place = lax.broadcasted_iota(jnp.int32, (tok, total), 0) + b * tok
        pick = (place == row_ref[...]).astype(f32).astype(bf16)
        s = dot(pick, qkv_buf[...])
        lane = lane_iota(tok)
        one = jnp.where(lane == HEAD_SIZE, 1.0, 0.0)
        for h in range(qh + 2 * kvh):
            piece = s[:, (h // 2) * LANES : (h // 2 + 1) * LANES]
            if h % 2:
                piece = pltpu.roll(piece, HEAD_SIZE, 1)
            fill = jnp.zeros_like(one) if h < qh + kvh else one
            piece = jnp.where(lane < HEAD_SIZE, piece, fill).astype(bf16)
            if h < qh:
                q_ref[h, rows, :] = piece
            elif h < qh + kvh:
                k_ref[h - qh, rows, :] = piece
            else:
                v_ref[h - qh - kvh, rows, :] = piece
        return carry

    lax.fori_loop(0, n_ctx, arrange, 0)
    window = min(MOST_LEN + QROWS, total)
    lse_ref[...] = jnp.zeros_like(lse_ref)

    def attend(b, carry):
        q0 = pl.multiple_of(b * QROWS, QROWS)
        k0 = pl.multiple_of(jnp.maximum(q0 + QROWS - window, 0), QROWS)
        rows, keys = pl.ds(q0, QROWS), pl.ds(k0, window)
        kidx = lax.broadcasted_iota(jnp.int32, (window, QROWS), 0) + k0
        qidx = lax.broadcasted_iota(jnp.int32, (window, QROWS), 1) + q0
        allowed = (kidx <= qidx) & (kidx >= start_ref[:, rows])
        for g in range(kvh):
            q = q_ref[g * group : (g + 1) * group, rows, :].reshape(group * QROWS, LANES)
            s = dot(k_ref[g, keys, :], q, NT)
            tops, exps = [], []
            for i in range(group):
                one = jnp.where(allowed, s[:, i * QROWS : (i + 1) * QROWS], MASKED)
                top = jnp.max(one, axis=0, keepdims=True)
                tops.append(top)
                exps.append(jnp.exp(one - top).astype(bf16))
            o = dot(v_ref[g, keys, :], jnp.concatenate(exps, axis=1), TN)
            total_e = o[HEAD_SIZE : HEAD_SIZE + 1, :]
            o = (o[:HEAD_SIZE, :] / total_e).astype(bf16)
            lse = jnp.log(total_e)
            for i in range(group):
                h = g * group + i
                cols = slice(i * QROWS, (i + 1) * QROWS)
                lse_ref[h : h + 1, rows] = tops[i] + lse[:, cols]
                sorted_buf[h * HEAD_SIZE : (h + 1) * HEAD_SIZE, rows] = o[:, cols]
        return carry

    lax.fori_loop(0, total // QROWS, attend, 0)

    def scatter(m, carry):
        place = lax.broadcasted_iota(jnp.int32, (tok, total), 1)
        pick = (place == col_ref[pl.ds(m * tok, tok), :]).astype(f32).astype(bf16)
        out = dot(pick, sorted_buf[...], NT).astype(bf16)

        @pl.when(m < n_ctx // 2)
        def _():
            near_ref[m] = out

        @pl.when(m >= n_ctx // 2)
        def _():
            far_ref[m - n_ctx // 2] = out

        return carry

    lax.fori_loop(0, n_ctx, scatter, 0)
    keep_w.wait()


def attn_fwd(places, w_pieces, n_dp, h1, row, col, start_row, cos, sin, qh, kvh):
    n_w = len(w_pieces)
    n_ctx, tok = h1.shape[:2]
    total = n_ctx * tok
    width = w_pieces[0].shape[2]
    rows = w_pieces[0].shape[1] * (n_w // n_dp)
    shape = jax.ShapeDtypeStruct
    return pl.pallas_call(
        functools.partial(attn_fwd_kernel, n_ctx, n_w, qh, kvh),
        out_shape=(
            shape((n_ctx // 2, tok, qh * HEAD_SIZE), bf16),
            shape((n_ctx // 2, tok, qh * HEAD_SIZE), bf16),
            shape((qh, total, LANES), bf16),
            shape((kvh, total, LANES), bf16),
            shape((kvh, total, LANES), bf16),
            shape((-(-qh // 8) * 8, total), f32),
            shape((n_ctx * n_dp, rows, width), bf16),
        ),
        in_specs=[SMEM] + [ANY] * (n_w + 1) + [VMEM] * 5,
        out_specs=(VMEM,) * 6 + (ANY,),
        scratch_shapes=[
            pltpu.VMEM((n_ctx * n_dp, rows, width), bf16),
            pltpu.VMEM((n_ctx, tok, MODEL_WIDTH), bf16),
            pltpu.VMEM((total, width), bf16),
            pltpu.VMEM((qh * HEAD_SIZE, total), bf16),
            pltpu.SemaphoreType.DMA((n_ctx * n_w,)),
            pltpu.SemaphoreType.DMA((n_ctx,)),
            pltpu.SemaphoreType.DMA,
        ],
        compiler_params=params(),
        cost_estimate=cost(20e9, 20e6),
        name="attn_fwd",
    )(places, *w_pieces, h1, row, col, start_row, cos, sin)


def attn_bwd_kernel(n_ctx, qh, kvh, *refs):
    db_refs, refs = refs[:n_ctx], refs[n_ctx:]
    (wo_ref, near_ref, far_ref, q_ref, k_ref, v_ref, lse_ref), refs = refs[:7], refs[7:]
    (row_ref, col_ref, start_ref, cos_ref, sin_ref, cos_t, sin_t), refs = refs[:7], refs[7:]
    out_ref, db_buf, dat_buf, del_buf, do_buf, dq_buf, dk_buf, dv_buf, kv_buf, sem = refs
    tok = db_buf.shape[1]
    total = n_ctx * tok
    group = qh // kvh
    k_chunks = kvh * HEAD_SIZE // LANES
    n_rows = lse_ref.shape[0]
    copies = [pltpu.make_async_copy(db_refs[m], db_buf.at[m], sem.at[m]) for m in range(n_ctx)]
    for c in copies:
        c.start()
    dk_buf[...] = jnp.zeros_like(dk_buf)
    dv_buf[...] = jnp.zeros_like(dv_buf)
    for c in copies:
        c.wait()
    q_width = qh * HEAD_SIZE
    head_of = lax.broadcasted_iota(jnp.int32, (n_rows, q_width), 1) // HEAD_SIZE
    ones = (head_of == lax.broadcasted_iota(jnp.int32, (n_rows, q_width), 0)).astype(f32).astype(bf16)

    def lift(m, carry):
        rows = pl.ds(pl.multiple_of(m * tok, tok), tok)
        low = dot(db_buf[m], wo_ref[...], NT).astype(bf16)
        dat_buf[rows, :] = low
        attn = jnp.where(m < n_ctx // 2, near_ref[m % (n_ctx // 2)], far_ref[m % (n_ctx // 2)])
        prod = low.astype(f32) * attn.astype(f32)
        hi = prod.astype(bf16)
        rest = (prod - hi.astype(f32)).astype(bf16)
        delta = dot(ones, hi, NT) + dot(ones, rest, NT)
        for i, v in enumerate(three_parts(delta)):
            del_buf[i * n_rows : (i + 1) * n_rows, rows] = v
        return carry

    lax.fori_loop(0, n_ctx, lift, 0)
    delta_parts = del_buf[...].astype(bf16)

    def arrange(b, carry):
        rows = pl.ds(pl.multiple_of(b * tok, tok), tok)
        place = lax.broadcasted_iota(jnp.int32, (tok, total), 0) + b * tok
        pick = (place == row_ref[...]).astype(f32).astype(bf16)
        s = dot(pick, dat_buf[...])
        lane = lane_iota(tok)
        for h in range(qh):
            piece = s[:, (h // 2) * LANES : (h // 2 + 1) * LANES]
            if h % 2:
                piece = pltpu.roll(piece, HEAD_SIZE, 1)
            do_buf[h, rows, :] = jnp.where(lane < HEAD_SIZE, piece, 0.0).astype(bf16)
        d = dot(delta_parts, pick, NT)
        del_buf[:n_rows, rows] = d[:n_rows] + d[n_rows : 2 * n_rows] + d[2 * n_rows :]
        return carry

    lax.fori_loop(0, n_ctx, arrange, 0)
    window = min(MOST_LEN + QROWS, total)

    def attend(b, carry):
        q0 = pl.multiple_of(b * QROWS, QROWS)
        k0 = pl.multiple_of(jnp.maximum(q0 + QROWS - window, 0), QROWS)
        rows, keys = pl.ds(q0, QROWS), pl.ds(k0, window)
        kidx = lax.broadcasted_iota(jnp.int32, (window, QROWS), 0) + k0
        qidx = lax.broadcasted_iota(jnp.int32, (window, QROWS), 1) + q0
        allowed = (kidx <= qidx) & (kidx >= start_ref[:, rows])
        for g in range(kvh):
            heads = slice(g * group, (g + 1) * group)
            q = q_ref[heads, rows, :].reshape(group * QROWS, LANES)
            do = do_buf[heads, rows, :].reshape(group * QROWS, LANES)
            k, v = k_ref[g, keys, :], v_ref[g, keys, :]
            s, dp = dot(k, q, NT), dot(v, do, NT)
            probs, grads = [], []
            for i in range(group):
                h = g * group + i
                cols = slice(i * QROWS, (i + 1) * QROWS)
                p = jnp.where(allowed, jnp.exp(s[:, cols] - lse_ref[h : h + 1, rows]), 0.0)
                probs.append(p.astype(bf16))
                grads.append((p * (dp[:, cols] - del_buf[h : h + 1, rows])).astype(bf16))
            p, ds = jnp.concatenate(probs, axis=1), jnp.concatenate(grads, axis=1)
            dv_buf[g, keys, :] += dot(p, do)
            dk_buf[g, keys, :] += dot(ds, q)
            dq = dot(k, ds, TN)
            for i in range(group):
                h = g * group + i
                turned = dq[:HEAD_SIZE, i * QROWS : (i + 1) * QROWS] * HEAD_SIZE**-0.5
                half = HEAD_SIZE // 2
                low, high = turned[:half], turned[half:]
                cos, sin = cos_t[:, rows], sin_t[:, rows]
                turned = jnp.concatenate([low * cos + high * sin, high * cos - low * sin], axis=0)
                dq_buf[h * HEAD_SIZE : (h + 1) * HEAD_SIZE, rows] = turned.astype(bf16)
        return carry

    lax.fori_loop(0, total // QROWS, attend, 0)

    def turn_back(b, carry):
        rows = pl.ds(b * tok, tok)
        cos, sin = cos_ref[rows, :], sin_ref[rows, :]
        lane = lane_iota(tok)
        heads = [dk_buf[h, rows, :] for h in range(kvh)] + [dv_buf[h, rows, :] for h in range(kvh)]
        for j in range(2 * k_chunks):
            pair = jnp.where(lane < HEAD_SIZE, heads[2 * j], pltpu.roll(heads[2 * j + 1], HEAD_SIZE, 1))
            if j < k_chunks:
                pair = pair * cos - half_swap(pair) * sin
            kv_buf[rows, j * LANES : (j + 1) * LANES] = pair.astype(bf16)
        return carry

    lax.fori_loop(0, n_ctx, turn_back, 0)

    def scatter(m, carry):
        place = lax.broadcasted_iota(jnp.int32, (tok, total), 1)
        pick = (place == col_ref[pl.ds(m * tok, tok), :]).astype(f32).astype(bf16)
        out_ref[m, :, :q_width] = dot(pick, dq_buf[...], NT).astype(bf16)
        out_ref[m, :, q_width:] = dot(pick, kv_buf[...]).astype(bf16)
        return carry

    lax.fori_loop(0, n_ctx, scatter, 0)


def attn_bwd(db_pieces, wo, near, far, q, k, v, lse, row, col, start_row, tables, qh, kvh):
    n_ctx = len(db_pieces)
    tok = db_pieces[0].shape[0]
    total = n_ctx * tok
    width = (qh + 2 * kvh) * HEAD_SIZE
    return pl.pallas_call(
        functools.partial(attn_bwd_kernel, n_ctx, qh, kvh),
        out_shape=jax.ShapeDtypeStruct((n_ctx, tok, width), bf16),
        in_specs=[ANY] * n_ctx + [VMEM] * 14,
        out_specs=VMEM,
        scratch_shapes=[
            pltpu.VMEM((n_ctx, tok, MODEL_WIDTH), bf16),
            pltpu.VMEM((total, qh * HEAD_SIZE), bf16),
            pltpu.VMEM((3 * lse.shape[0], total), f32),
            pltpu.VMEM((qh, total, LANES), bf16),
            pltpu.VMEM((qh * HEAD_SIZE, total), bf16),
            pltpu.VMEM((kvh, total, LANES), f32),
            pltpu.VMEM((kvh, total, LANES), f32),
            pltpu.VMEM((total, 2 * kvh * HEAD_SIZE), bf16),
            pltpu.SemaphoreType.DMA((n_ctx,)),
        ],
        compiler_params=params(),
        cost_estimate=cost(25e9, 20e6),
        name="attn_bwd",
    )(*db_pieces, wo, near, far, q, k, v, lse, row, col, start_row, *tables)


def pick_rows(e, cap, routes):
    tok = routes.shape[1]
    before = lax.broadcasted_iota(jnp.int32, (tok, tok), 0) < lax.broadcasted_iota(
        jnp.int32, (tok, tok), 1
    )
    names = lax.broadcasted_iota(jnp.int32, (LANES, tok), 0)
    slots = lax.broadcasted_iota(jnp.int32, (cap, tok), 0).astype(f32)
    hit = jnp.zeros((1, tok), f32)
    named = jnp.zeros((LANES, tok), f32)
    for j in range(routes.shape[0]):
        hit = hit + jnp.where(routes[j : j + 1] == e, 1.0, 0.0)
        named = named + jnp.where(names == routes[j : j + 1], 1.0, 0.0)
    hits = jnp.broadcast_to(hit, (8, tok)).astype(bf16)
    slot = dot(hits, before.astype(f32).astype(bf16))[0:1]
    pick = jnp.where((slots == slot) & (hit > 0.5), 1.0, 0.0).astype(bf16)
    return pick, dot(pick, named.astype(bf16), NT)


TILE = 512


def expert_kernel(by_hand, cap, who_ref, *refs):
    n_in = len(PIECES) if by_hand else 1
    h_refs, dy_refs, refs = refs[:n_in], refs[n_in : 2 * n_in], refs[2 * n_in :]
    (routes_ref, wc_ref, wd_ref), refs = refs[:3], refs[3:]
    n_rows = 4 if by_hand else 2
    row_refs, refs = refs[:n_rows], refs[n_rows:]
    (xs_ref, deout_ref, act_ref, dgate_ref, dup_ref, coef_ref), refs = refs[:6], refs[6:]
    dcat, drow, yrow, refs = *refs[:3], refs[3:]
    step = pl.program_id(0)
    core = who_ref[1]
    e = who_ref[0]
    ff = wd_ref.shape[0]
    if by_hand:
        h_buf, dy_buf, sem = refs

        def copies(chip):
            got = []
            for n, (j, sib) in enumerate(PIECES):
                if j != chip:
                    continue
                col = pl.multiple_of((core + sib) % 2 * HALF, HALF)
                for i in range(2):
                    spot = (2 * j + (i ^ sib), slice(None), pl.ds(col, HALF))
                    for k, (src, buf) in enumerate(((h_refs, h_buf), (dy_refs, dy_buf))):
                        got.append(
                            pltpu.make_async_copy(src[n].at[i], buf.at[spot], sem.at[k, n, i])
                        )
            return got

        @pl.when(step == 0)
        def _():
            for j in range(4):
                for c in copies(j):
                    c.start()

        for j in range(4):

            @pl.when(step == j)
            def _():
                for c in copies(j):
                    c.wait()

        def load(buf, i, cols):
            return buf[2 * step + i, :, cols]

    else:
        h_buf, dy_buf = h_refs[0], dy_refs[0]

        def load(buf, i, cols):
            return buf[i, :, cols]

    picks, masks = [], []
    for i in range(2):
        pick, mask = pick_rows(e, cap, routes_ref[2 * step + i])
        picks.append(pick)
        masks.append(mask)
    mask = jnp.concatenate(masks, axis=0) > 0.5
    tiles = [slice(t, t + TILE) for t in range(0, MODEL_WIDTH, TILE)]
    for cols in tiles:
        for i in range(2):
            rows = slice(i * cap, (i + 1) * cap)
            xs_ref[rows, cols] = dot(picks[i], load(h_buf, i, cols)).astype(bf16)
            deout_ref[rows, cols] = dot(picks[i], load(dy_buf, i, cols)).astype(bf16)
    xs = xs_ref[...]
    logits = jnp.where(mask, dot(xs, wc_ref[:, 2 * ff :]), MASKED)
    ex = jnp.where(mask, jnp.exp(logits - jnp.max(logits, axis=1, keepdims=True)), 0.0)
    lane = lax.broadcasted_iota(jnp.int32, ex.shape, 1)
    own = lane == e
    denom = jnp.sum(ex, axis=1, keepdims=True)
    probs = ex / jnp.where(denom > 0.0, denom, 1.0)
    gp = jnp.sum(jnp.where(own, probs, 0.0), axis=1, keepdims=True)
    gate = dot(xs, wc_ref[:, :ff])
    up = dot(xs, wc_ref[:, ff : 2 * ff])
    sig = jax.nn.sigmoid(gate)
    silu = gate * sig
    act = (silu * up).astype(bf16)
    act_ref[...] = act
    dgp = jnp.zeros((2 * cap, LANES), f32)
    for cols in tiles:
        eout = dot(act, wd_ref[:, cols]).astype(bf16).astype(f32)
        dys = deout_ref[:, cols].astype(f32)
        both = dys * eout
        for c in range(0, TILE, LANES):
            dgp = dgp + both[:, c : c + LANES]
        deout_ref[:, cols] = (gp * dys).astype(bf16)
        yrow[:, cols] = (gp * eout).astype(bf16)
    dgp = jnp.sum(dgp, axis=1, keepdims=True)
    coef = gp * dgp * (jnp.where(own, 1.0, 0.0) - probs)
    hi = coef.astype(bf16).astype(f32)
    low = pltpu.roll(coef - hi, LANES // 2, 1)
    coef = jnp.where(lane < LANES // 2, hi, low).astype(bf16)
    coef_ref[...] = coef
    dact = dot(deout_ref[...], wd_ref[...], NT)
    dgate = (dact * up * sig * (1.0 + gate * (1.0 - sig))).astype(bf16)
    dup = (dact * silu).astype(bf16)
    dgate_ref[...] = dgate
    dup_ref[...] = dup
    dcat[:, :ff] = dgate
    dcat[:, ff : 2 * ff] = dup
    dcat[:, 2 * ff :] = coef
    for cols in tiles:
        drow[:, cols] = dot(dcat[...], wc_ref[cols, :], NT).astype(bf16)
    for k, buf in enumerate((drow, yrow)):
        for i in range(2):
            rows = slice(i * cap, (i + 1) * cap)
            if by_hand:
                mine = pl.multiple_of(core * HALF, HALF)
                other = pl.multiple_of((1 - core) * HALF, HALF)
                for ref, at, col in ((row_refs[2 * k], i, mine), (row_refs[2 * k + 1], 1 - i, other)):
                    ref[0, at] = dot(picks[i], buf[rows, pl.ds(col, HALF)], TN).astype(bf16)
            else:
                row_refs[k][0, i] = dot(picks[i], buf[rows, :], TN).astype(bf16)


def run_experts(who, by_hand, h_list, dy_list, routes_t, wc, wd, cap, tok):
    n_blocks = routes_t.shape[0]
    steps = n_blocks // 2
    ff = wd.shape[0]
    rows = 2 * cap
    shape = jax.ShapeDtypeStruct
    out_w = HALF if by_hand else MODEL_WIDTH
    block = pl.BlockSpec((1, 2, tok, out_w), lambda i, *_: (i, 0, 0, 0))
    other = pl.BlockSpec((1, 2, tok, out_w), lambda i, *_: (i // 2 + i % 2 * 2, 0, 0, 0))
    wide = pl.BlockSpec((rows, MODEL_WIDTH), lambda i, *_: (i, 0))
    thin = pl.BlockSpec((rows, ff), lambda i, *_: (i, 0))
    edge = pl.BlockSpec((rows, LANES), lambda i, *_: (i, 0))
    whole = pl.BlockSpec((2, tok, MODEL_WIDTH), lambda i, *_: (i, 0, 0))
    n_in = len(h_list)
    scratch = [
        pltpu.VMEM((rows, wc.shape[1]), bf16),
        pltpu.VMEM((rows, MODEL_WIDTH), bf16),
        pltpu.VMEM((rows, MODEL_WIDTH), bf16),
    ]
    if by_hand:
        scratch += [
            pltpu.VMEM((n_blocks, tok, MODEL_WIDTH), bf16),
            pltpu.VMEM((n_blocks, tok, MODEL_WIDTH), bf16),
            pltpu.SemaphoreType.DMA((2, n_in, 2)),
        ]
    row_specs = [block, other] * 2 if by_hand else [block] * 2
    grid_spec = pltpu.PrefetchScalarGridSpec(
        num_scalar_prefetch=1,
        grid=(steps,),
        in_specs=[ANY if by_hand else whole] * (2 * n_in) + [VMEM] * 3,
        out_specs=row_specs + [wide] * 2 + [thin] * 3 + [edge],
        scratch_shapes=scratch,
    )
    return pl.pallas_call(
        functools.partial(expert_kernel, by_hand, cap),
        out_shape=[shape((steps, 2, tok, out_w), bf16)] * len(row_specs)
        + [shape((steps * rows, MODEL_WIDTH), bf16)] * 2
        + [shape((steps * rows, ff), bf16)] * 3
        + [shape((steps * rows, LANES), bf16)],
        grid_spec=grid_spec,
        compiler_params=params(60),
        cost_estimate=cost(30e9, 30e6),
        name="experts",
    )(who, *h_list, *dy_list, routes_t, wc, wd)


def flip(v, axis, bit):
    n = lax.axis_size(axis)
    return lax.ppermute(v, axis, [(i, i ^ bit) for i in range(n)])


def step_up(v, axis):
    n = lax.axis_size(axis)
    return lax.ppermute(v, axis, [(i, (i + 1) % n) for i in range(n)])


def ctx_gather(v):
    n = lax.axis_size("context")
    pieces = {0: v}
    bit = n // 2
    while bit:
        for m in list(pieces):
            pieces[m | bit] = flip(pieces[m], "context", bit)
        bit //= 2
    return [pieces[m] for m in range(n)]


def add_low(a, b):
    return (a.astype(f32) + b.astype(f32)).astype(bf16)


def ring(v, axis, deps=()):
    pieces = [v]
    for i in range(lax.axis_size(axis) - 1):
        sent = after(pieces[-1], *deps[i]) if i < len(deps) else pieces[-1]
        pieces.append(step_up(sent, axis))
    return pieces


def send_all(v, axis):
    n = lax.axis_size(axis)
    return [v] + [
        lax.ppermute(v, axis, [(i, (i + k) % n) for i in range(n)]) for k in range(1, n)
    ]


def ring_sum(chunk, axis):
    n, d = lax.axis_size(axis), lax.axis_index(axis)
    part = chunk(lax.rem(d + n - 1, n)).astype(bf16)
    for hop in range(n - 1):
        got = step_up(part, axis)
        own = chunk(lax.rem(d + 2 * n - 2 - hop, n))
        part = (got.astype(f32) + own.astype(f32)).astype(bf16)
    return part


def direct_sum(chunk, axis, *deps):
    n, d = lax.axis_size(axis), lax.axis_index(axis)
    total = chunk(d).astype(f32)
    if deps:
        total = after(total, *deps)
    for k in range(1, n):
        sent = chunk(lax.rem(d + k, n)).astype(bf16)
        got = lax.ppermute(sent, axis, [(i, (i + k) % n) for i in range(n)])
        total = total + got.astype(f32)
    return total


def after(v, *deps):
    return lax.optimization_barrier((v, *deps))[0]


HALF = MODEL_WIDTH // 2
PLANE = ("expert", "context")
PIECES = ((0, 0), (1, 0), (2, 0), (3, 0), (0, 1), (2, 1), (1, 1), (3, 1))


def small_plane():
    return lax.axis_size("expert") == 2 and lax.axis_size("context") == 4


def hop_plane(v, second):
    pairs = []
    for i in range(8):
        along_context = (i % 2 == 0) != second
        pairs.append((i, i ^ 2 if along_context else i ^ 4))
    return lax.ppermute(v, PLANE, pairs)


def halves(v, core):
    left, right = v[..., :HALF], v[..., HALF:]
    return jnp.where(core == 0, left, right), jnp.where(core == 0, right, left)


def sync(*values):
    return lax.optimization_barrier(values)


def plane_near(v):
    core = lax.axis_index("context") % 2
    mine, given = halves(v, core)
    return jnp.stack([mine, flip(given, "context", 1)])


def plane_far(u0, u1):
    return hop_plane(u0, True), hop_plane(u1, True)


def plane_share(own):
    return list(own) + [flip(u, "context", 1) for u in own]


def plane_gather(v):
    if not small_plane():
        return [lax.all_gather(v, PLANE, axis=0, tiled=False)]
    u0 = plane_near(v)
    u1 = hop_plane(u0, False)
    return plane_share((u0, u1) + plane_far(u0, u1))


class PlaneSum:
    def __init__(self, rows):
        self.small = small_plane()
        self.rows = rows
        if self.small:
            self.keep, give = rows
            self.got = flip(give, "context", 1)
            self.far = add_low(self.keep[2:], self.got[2:])

    def first(self):
        if self.small:
            self.got2 = hop_plane(self.far, True)

    def second(self):
        if self.small:
            near = self.keep[:2].astype(f32) + self.got[:2].astype(f32) + self.got2.astype(f32)
            self.near = near[0]
            self.got1 = hop_plane(near[1].astype(bf16), False)

    def finish(self):
        if not self.small:
            (both,) = self.rows
            flat = both.reshape(-1, both.shape[-1])
            return lax.psum_scatter(flat, PLANE, scatter_dimension=0, tiled=True).astype(f32)
        core = lax.axis_index("context") % 2
        whole = self.near + self.got1.astype(f32)
        other = flip(whole[1].astype(bf16), "context", 1).astype(f32)
        left = jnp.where(core == 0, whole[0], other)
        right = jnp.where(core == 0, other, whole[0])
        return jnp.concatenate([left, right], axis=1)


def ctx_sum(p):
    far = add_low(p[2], flip(p[3], "context", 1))
    own = p[0].astype(f32) + flip(p[1], "context", 1).astype(f32)
    return own + flip(far, "context", 2).astype(f32)


def put_in_order(places, pieces, name):
    n = len(pieces)
    rows, width = pieces[0].shape

    def kernel(place_ref, *refs):
        out_ref, sem = refs[n:]
        copies = [
            pltpu.make_async_copy(refs[k], out_ref.at[place_ref[k]], sem.at[k]) for k in range(n)
        ]
        for c in copies:
            c.start()
        for c in copies:
            c.wait()

    return pl.pallas_call(
        kernel,
        out_shape=jax.ShapeDtypeStruct((n, rows, width), pieces[0].dtype),
        in_specs=[SMEM] + [ANY] * n,
        out_specs=VMEM,
        scratch_shapes=[pltpu.SemaphoreType.DMA((n,))],
        cost_estimate=cost(0, 2 * n * rows * width * 2),
        name=name,
    )(places, *pieces)


def columns_of(spots, near, far, qw, kw):
    n_ctx, part, width = near.shape

    def kernel(spot_ref, near_ref, far_ref, *outs):
        for k, ref in enumerate((near_ref, far_ref)):
            row = pl.multiple_of(spot_ref[n_ctx + k] * part, 16)
            for m in range(n_ctx):
                v = ref[m].astype(f32)
                lo = 0
                for out, w in zip(outs, (qw, kw, kw)):
                    col = pl.multiple_of(spot_ref[m] * w, LANES)
                    out[pl.ds(row, part), pl.ds(col, w)] = v[:, lo : lo + w]
                    lo += w

    shape = jax.ShapeDtypeStruct
    return pl.pallas_call(
        kernel,
        out_shape=tuple(shape((2 * part, n_ctx * w), f32) for w in (qw, kw, kw)),
        in_specs=[SMEM, VMEM, VMEM],
        out_specs=(VMEM,) * 3,
        cost_estimate=cost(0, 2e6),
        name="columns_of",
    )(spots, near, far)


def rms_back(dh, v, r, gain):
    inner = jnp.sum(gain * dh * v, axis=-1, keepdims=True)
    dv = r * gain * dh - v * (r * r * r) * (inner / MODEL_WIDTH)
    return dv, jnp.sum(dh * v * r, axis=0)


def body(
    hidden, cotangent, token_order, lengths, routes, attn_gain, w_query, key_weight,
    value_weight, w_out, ffn_gain, w_router, w_gate, w_up, w_down,
):
    tok, top = hidden.shape[1], routes.shape[2]
    n_exp, n_ctx, n_dp = (lax.axis_size(a) for a in ("expert", "context", "dp"))
    experts = n_exp * n_ctx
    cap = -(-(9 * tok * top // (8 * experts)) // 16) * 16
    qh, kvh = QUERY_HEADS // n_ctx, KEY_VALUE_HEADS // n_ctx
    qw, kw = qh * HEAD_SIZE, kvh * HEAD_SIZE
    rows = w_query.shape[0]
    ex, cx, dx = (lax.axis_index(a) for a in ("expert", "context", "dp"))
    my_expert = ex * n_ctx + cx
    total = n_ctx * tok

    def for_context(c):
        return jnp.concatenate(
            [
                lax.dynamic_slice_in_dim(w_query, c * qw, qw, 1),
                lax.dynamic_slice_in_dim(key_weight, c * kw, kw, 1),
                lax.dynamic_slice_in_dim(value_weight, c * kw, kw, 1),
            ],
            axis=1,
        )

    params_t = jnp.concatenate([attn_gain[None], ffn_gain[None], w_router.T], axis=0)
    p_rows = params_t.shape[0]
    params_t = jnp.pad(params_t, ((0, 0), (0, tok - rows)))
    note = jnp.concatenate([routes[0].T.astype(bf16), params_t], axis=0)
    k_of = jnp.arange(n_dp, dtype=jnp.int32)
    d_of = lax.rem(dx - k_of + n_dp, n_dp)
    c_of = cx ^ jnp.arange(n_ctx, dtype=jnp.int32)
    places = (c_of[None, :] * n_dp + d_of[:, None]).reshape(-1).astype(jnp.int32)

    def own_params(stack):
        stack = stack.reshape(n_dp * n_ctx, p_rows, -1)[:, :, :rows]
        at = d_of[None, :] * n_ctx + (cx ^ jnp.arange(n_ctx, dtype=jnp.int32))[:, None]
        flat = stack[at.reshape(-1)].transpose(1, 0, 2).reshape(p_rows, MODEL_WIDTH)
        router = jnp.pad(flat[2:].T, ((0, 0), (0, LANES // 2 - experts)))
        return flat[0:1].astype(f32), flat[1:2].astype(f32), router

    def own_routes(stack):
        return stack.reshape(experts, top, tok).astype(jnp.int32)

    def positions(order_row, lengths_row):
        order_rel = order_row.reshape(n_ctx, tok)[c_of].reshape(-1)
        both = jnp.concatenate([order_rel, jnp.arange(total, dtype=jnp.int32)])
        end = jnp.zeros((), jnp.int32)
        start = jnp.zeros_like(both)
        for j in range(lengths_row.shape[0]):
            end = end + lengths_row[j]
            start = start + jnp.where(both >= end, lengths_row[j], 0)
        lane = jnp.arange(LANES, dtype=jnp.int32) % HEAD_SIZE
        half = HEAD_SIZE // 2
        freq = ROPE_BASE ** (-((lane % half).astype(f32) * 2.0 / HEAD_SIZE))

        def tables(places):
            angle = places.astype(f32)[:, None] * freq[None, :]
            return jnp.cos(angle), jnp.where(lane < half, -1.0, 1.0)[None] * jnp.sin(angle)

        places_s = (both - start)[total:]
        turned = freq[:half, None] * places_s.astype(f32)[None, :]
        placed = (*tables(places_s), jnp.cos(turned), jnp.sin(turned))
        dealt = tables((both - start)[:total])
        return (order_rel[None, :], order_rel[:, None], start[None, total:], *dealt, *placed)

    order_row, ends_in = token_order[0], lengths[0]

    def gather_plane(v):
        return lax.all_gather(v, PLANE, axis=0, tiled=False)

    def gather_out(v):
        return lax.all_gather(v, "dp", axis=0, tiled=True)

    x_own, dy_own = hidden[0], cotangent[0]
    if small_plane():
        part = rows // 2

        def half_for(c):
            return lax.dynamic_slice_in_dim(for_context(c), ex * part, part, 0)

        got = [half_for(cx)] + [flip(half_for(cx ^ m), "context", m) for m in range(1, n_ctx)]
        note2 = jnp.stack([note, flip(note, "context", 2)])
        x2 = flip(x_own, "context", 2)
        dy0 = plane_near(dy_own)
        w0, note2, dy0 = sync(jnp.stack(got), note2, dy0)
        mine, theirs = [w0], []
        for k in range(n_dp - 1):
            nxt, other = step_up(mine[-1], "dp"), flip(mine[-1], "expert", 1)
            if k == 0:
                near = flip(note2, "context", 1)
                note4 = jnp.stack([note2[0], near[0], note2[1], near[1]])
                nxt, other, note4, order_row, ends_in = sync(nxt, other, note4, order_row, ends_in)
            elif k == 1:
                shards = send_all(note4[:, top:], "dp")
                routes_far = flip(note4[:, :top], "expert", 1)
                nxt, other, x2, routes_far, *shards = sync(nxt, other, x2, routes_far, *shards)
                x1, x3 = flip(x_own, "context", 1), flip(x2, "context", 1)
                gain_a, gain_b, router = own_params(jnp.stack(shards))
                where = positions(order_row, ends_in)
            elif k == 2:
                nxt, other, gain_a, *where = sync(nxt, other, gain_a, *where)
                h1 = norm_rows([x_own, x1, x2, x3], gain_a)
                dy1 = hop_plane(after(dy0, x2), False)
            mine.append(nxt)
            theirs.append(other)
        theirs.append(flip(mine[-1], "expert", 1))
        c = lax.rem(cx, 2)
        routes_rel = jnp.stack([note4[:, :top], routes_far]).reshape(8, top, tok)
        even = jnp.array([0, 1, 2, 3, 4, 5, 6, 7], jnp.int32)
        odd = jnp.array([0, 1, 4, 5, 2, 3, 6, 7], jnp.int32)
        routes_all = own_routes(routes_rel[jnp.where(c == 0, even, odd)])
        theirs[-1], router, h1, routes_all, dy1 = sync(theirs[-1], router, h1, routes_all, dy1)
        wo = gather_out(after(w_out, mine[-1]))
        dy2, dy3 = plane_far(dy0, dy1)
        w_pieces = mine + theirs
        spots = jnp.concatenate(
            [places, places, jnp.broadcast_to(ex, (n_dp,)), jnp.broadcast_to(1 - ex, (n_dp,))]
        ).astype(jnp.int32)
    else:
        got = [for_context(cx)]
        for m in range(1, n_ctx):
            got.append(flip(for_context(cx ^ m), "context", m))
        w_pieces = ring(jnp.stack(got), "dp")
        note4 = jnp.stack(ctx_gather(note))
        gain_a, gain_b, router = own_params(jnp.stack(send_all(note4[:, top:], "dp")))
        routes_all = own_routes(lax.all_gather(note[:top], PLANE, axis=0, tiled=False))
        h1 = norm_rows(ctx_gather(x_own), gain_a)
        dy_all, wo = gather_plane(cotangent[0]), gather_out(w_out)
        spots = jnp.concatenate([places, jnp.zeros((n_dp,), jnp.int32)])
        where = positions(order_row, ends_in)
    row, col, start_row, cos_d, sin_d, *placed = where
    near, far, q, k, v, lse, wqkv = attn_fwd(
        spots, w_pieces, n_dp, h1, row, col, start_row, cos_d, sin_d, qh, kvh
    )
    if small_plane():
        near, wo, dy2, dy3 = sync(near, wo, dy2, dy3)
        dy_list = plane_share((dy0, dy1, dy2, dy3))
    else:
        dy_list = [dy_all]
    partial_far = dot(far.reshape(-1, qw), wo).astype(bf16).reshape(-1, tok, MODEL_WIDTH)
    partial_near = dot(near.reshape(-1, qw), wo).astype(bf16).reshape(-1, tok, MODEL_WIDTH)
    late_gate = after(w_gate[0], partial_near)
    w_cat = jnp.concatenate([late_gate, w_up[0], router, router], axis=1)
    branch = ctx_sum([partial_near[0], partial_near[1], partial_far[0], partial_far[1]])
    branch, w_cat, *dy_list = sync(branch, w_cat, *dy_list)
    x_own = x_own.astype(f32)
    middle = x_own + branch
    r_b = lax.rsqrt(jnp.mean(middle * middle, axis=-1, keepdims=True) + NORM_EPS)
    h2 = (middle * r_b * gain_b).astype(bf16)
    h_list = plane_gather(h2)

    by_hand = small_plane()
    who = jnp.stack([my_expert, cx % 2]).astype(jnp.int32)
    out = run_experts(
        who, by_hand, h_list, dy_list, routes_all, w_cat, w_down[0], cap, tok
    )
    n_rows = 2 if by_hand else 1
    d_rows, y_rows, (xs, deout, act, dgate, dup, coef) = (
        out[:n_rows], out[n_rows : 2 * n_rows], out[2 * n_rows :],
    )
    d_sum, y_sum = PlaneSum(d_rows), PlaneSum(y_rows)
    small = small_plane()
    xs_late, deout_late = (after(xs, d_sum.far), after(deout, d_sum.far)) if small else (xs, deout)
    g_gate = dot(xs_late, dgate, TN).astype(bf16)
    g_up = dot(xs_late, dup, TN).astype(bf16)
    g_down = dot(deout_late, act, TN).astype(bf16)
    g_router = dot(xs_late, coef, TN)
    g_router = g_router[:, :experts] + g_router[:, LANES // 2 : LANES // 2 + experts]

    def over_dp(g, dim):
        return lax.psum_scatter(g, "dp", scatter_dimension=dim, tiled=True).astype(f32)

    if small:
        d_sum.first()
        sum_gate, sum_up, sum_down = over_dp(g_gate, 0), over_dp(g_up, 0), over_dp(g_down, 0)
        d_sum.got2, y_sum.far, g_gate, g_up, g_down, g_router = sync(
            d_sum.got2, y_sum.far, g_gate, g_up, g_down, g_router
        )
        d_sum.second()
    else:
        sum_gate, sum_up, sum_down = over_dp(g_gate, 0), over_dp(g_up, 0), over_dp(g_down, 0)
    dh2 = d_sum.finish()
    dy = dy_own.astype(f32)
    d_norm, g_gain_b = rms_back(dh2, middle, r_b, gain_b)
    d_middle = dy + d_norm
    if small:
        b0 = d_middle.astype(bf16)
        b2, b1 = flip(b0, "context", 2), flip(b0, "context", 1)
        b2, b1 = sync(b2, b1)
        db_pieces = [b0, b1, b2, flip(b2, "context", 1)]
        y_sum.far = after(y_sum.far, b2)
        y_sum.first()
    else:
        db_pieces = ctx_gather(d_middle.astype(bf16))
    db_all = jnp.concatenate(db_pieces, axis=0)
    attn = jnp.concatenate([near, far], axis=0).reshape(total, qw)
    g_out = dot(attn, db_all, TN).astype(bf16)
    db_last = after(db_pieces[-1], g_out, sum_gate)

    dqkv = attn_bwd(
        db_pieces[:-1] + [db_last], wo, near, far, q, k, v, lse, row, col, start_row, placed, qh, kvh
    )
    dqkv, sum_up = sync(dqkv, sum_up)
    dqkv_flat = dqkv.reshape(total, -1)
    h1_flat = h1.reshape(total, MODEL_WIDTH)
    g_qkv = dot(h1_flat, dqkv_flat, TN).astype(bf16)
    w_flat = wqkv.reshape(MODEL_WIDTH, -1)
    if small:
        part = rows // 2
        g5 = g_qkv.reshape(n_ctx * n_dp, 2, part, -1)
        theirs = lax.dynamic_index_in_dim(g5, 1 - ex, 1, keepdims=False)
        mine = lax.dynamic_index_in_dim(g5, ex, 1, keepdims=False)
        got = flip(theirs, "expert", 1)
        dh1_in = after(dqkv_flat, theirs, mine)
    else:
        dh1_in = dqkv_flat
    dh1_part = dot(dh1_in, w_flat, NT).astype(bf16)
    g_gain_a = jnp.sum(dh1_part.astype(f32) * h1_flat.astype(f32), axis=0) / gain_a[0]
    dh1_part = dh1_part.reshape(n_ctx, tok, MODEL_WIDTH)
    r_a = lax.rsqrt(jnp.mean(x_own * x_own, axis=-1, keepdims=True) + NORM_EPS)

    width = qw + 2 * kw
    s_out = lax.psum_scatter(g_out, "dp", scatter_dimension=0, tiled=True)

    def exchange(s):
        back = [lax.dynamic_index_in_dim(s, cx, 0, keepdims=False)]
        for m in range(1, n_ctx):
            one = lax.dynamic_index_in_dim(s, cx ^ m, 0, keepdims=False)
            back.append(flip(one, "context", m))
        return jnp.stack(back)

    tiny = jnp.concatenate([g_gain_a[None], g_gain_b[None], g_router.T], axis=0)

    def finish_rows(dh1):
        return (d_middle + rms_back(dh1, x_own, r_a, gain_a)[0]).astype(bf16)

    def spread(tiny):
        tiny = tiny.reshape(-1, n_ctx * n_dp, rows).transpose(1, 0, 2)
        tiny = lax.all_to_all(tiny, ("context", "dp"), split_axis=0, concat_axis=0, tiled=True)
        return jnp.sum(tiny, axis=0)

    if small:
        h3 = flip(dh1_part[3], "context", 1)
        hop = flip(add_low(dh1_part[2], h3), "context", 2)
        h1p = flip(dh1_part[1], "context", 1)
        dh1 = dh1_part[0].astype(f32) + h1p.astype(f32)
        y_sum.got2 = after(y_sum.got2, dqkv)
        got, hop, dh1, y_sum.got2, sum_down, s_out, tiny = sync(
            got, hop, dh1, y_sum.got2, sum_down, s_out, tiny
        )
        both_g = add_low(mine, got).reshape(n_ctx, n_dp, part, width)
        s_qkv = ring_sum(lambda d: lax.dynamic_index_in_dim(both_g, d, 1, keepdims=False), "dp")
        y_sum.got2 = after(y_sum.got2, both_g)
        y_sum.second()
        tiny = after(tiny, both_g)
        tiny = spread(tiny + flip(tiny, "expert", 1))
        grad_input = finish_rows(after(dh1, both_g) + hop.astype(f32))
        out_low = s_out.astype(bf16)
        s_qkv, out_low, y_sum.got1, grad_input, tiny = sync(
            s_qkv, out_low, y_sum.got1, grad_input, tiny
        )
        out_far = flip(out_low, "expert", 1)
        output = (middle + y_sum.finish()).astype(bf16)
        s_out = out_low.astype(f32) + out_far.astype(f32)
        near = exchange(s_qkv.astype(bf16))
        far = flip(near, "expert", 1)
        spots = jnp.concatenate([c_of, ex[None], 1 - ex[None]]).astype(jnp.int32)
        sum_q, sum_k, sum_v = columns_of(spots, near, far, qw, kw)
    else:
        dh1 = ctx_sum([dh1_part[m] for m in range(n_ctx)])
        grad_input = finish_rows(dh1)
        tiny = spread(lax.psum(tiny, "expert"))
        g4 = g_qkv.reshape(n_ctx, n_dp, rows, width)
        s_qkv = direct_sum(lambda d: lax.dynamic_index_in_dim(g4, d, 1, keepdims=False), "dp")
        s_qkv = lax.psum(s_qkv.astype(bf16), "expert")
        s_out = lax.psum(s_out.astype(bf16), "expert").astype(f32)
        back = exchange(s_qkv)[c_of]

        def columns(lo, hi):
            return back[:, :, lo:hi].transpose(1, 0, 2).reshape(rows, -1).astype(f32)

        sum_q, sum_k, sum_v = columns(0, qw), columns(qw, qw + kw), columns(qw + kw, width)
        output = (middle + y_sum.finish()).astype(bf16)

    return (
        output[None], grad_input[None], tiny[0], sum_q, sum_k, sum_v, s_out,
        tiny[1], tiny[2:].T, sum_gate[None], sum_up[None], sum_down.T[None],
    )


def solution(mesh):
    tokens = P(("expert", "dp"), "context", None)
    group = P(("expert", "dp"), None)
    vec, mat = P(("context", "dp")), P(("context", "dp"), None)
    expert = P(("expert", "context"), None, None)
    by_rows = P(("expert", "context"), "dp", None)
    by_cols = P(("expert", "context"), None, "dp")
    return jax.shard_map(
        body,
        mesh=mesh,
        in_specs=(
            tokens, tokens, group, group, tokens, vec, mat, mat, mat, mat, vec, mat,
            expert, expert, expert,
        ),
        out_specs=(
            tokens, tokens, vec, mat, mat, mat, mat, vec, mat, by_rows, by_rows, by_cols,
        ),
        check_vma=False,
    )
```

```python
import functools

import jax
import jax.numpy as jnp
from jax import lax
from jax.experimental import pallas as pl
from jax.experimental.pallas import tpu as pltpu
from jax.sharding import PartitionSpec as P

MODEL_WIDTH = 1536
QUERY_HEADS = 24
KEY_VALUE_HEADS = 8
HEAD_SIZE = 64
MOST_LEN = 512
NORM_EPS = 1e-06
ROPE_BASE = 10000.0
MASKED = -1e30
QROWS = 128
LANES = 128
bf16 = jnp.bfloat16
f32 = jnp.float32
ANY = pl.BlockSpec(memory_space=pl.ANY)
VMEM = pl.BlockSpec(memory_space=pltpu.VMEM)
SMEM = pl.BlockSpec(memory_space=pltpu.SMEM)
NT = (((1,), (1,)), ((), ()))
TN = (((0,), (0,)), ((), ()))


def params(limit=56):
    return pltpu.CompilerParams(vmem_limit_bytes=limit * 1024 * 1024)


def cost(flops, nbytes):
    return pl.CostEstimate(flops=int(flops), bytes_accessed=int(nbytes), transcendentals=0)


def dot(a, b, dims=(((1,), (0,)), ((), ()))):
    return lax.dot_general(a, b, dims, preferred_element_type=f32)


def lane_iota(rows):
    return lax.broadcasted_iota(jnp.int32, (rows, LANES), 1)


def half_swap(v):
    lane = lane_iota(v.shape[0])
    low = lax.rem(lane, HEAD_SIZE) < HEAD_SIZE // 2
    up = pltpu.roll(v, LANES - HEAD_SIZE // 2, 1)
    down = pltpu.roll(v, HEAD_SIZE // 2, 1)
    return jnp.where(low, up, down)


def three_parts(v):
    hi = v.astype(bf16).astype(f32)
    mid = (v - hi).astype(bf16).astype(f32)
    return hi, mid, v - hi - mid


def norm_kernel(n_ctx, *refs):
    x_refs, (gain_ref, h1_ref, x_buf, sem) = refs[:n_ctx], refs[n_ctx:]
    tok = x_buf.shape[1]
    copies = [pltpu.make_async_copy(x_refs[m], x_buf.at[m], sem.at[m]) for m in range(n_ctx)]
    for c in copies:
        c.start()
    for c in copies:
        c.wait()
    step = 64

    def norm(i, carry):
        rows = pl.ds(pl.multiple_of(i % (tok // step) * step, step), step)
        x = x_buf[i // (tok // step), rows, :].astype(f32)
        r = lax.rsqrt(jnp.mean(x * x, axis=-1, keepdims=True) + NORM_EPS)
        h1_ref[i // (tok // step), rows, :] = (x * r * gain_ref[...]).astype(bf16)
        return carry

    lax.fori_loop(0, n_ctx * tok // step, norm, 0)


def norm_rows(x_pieces, gain):
    n_ctx, tok = len(x_pieces), x_pieces[0].shape[0]
    return pl.pallas_call(
        functools.partial(norm_kernel, n_ctx),
        out_shape=jax.ShapeDtypeStruct((n_ctx, tok, MODEL_WIDTH), bf16),
        in_specs=[ANY] * n_ctx + [VMEM],
        out_specs=VMEM,
        scratch_shapes=[
            pltpu.VMEM((n_ctx, tok, MODEL_WIDTH), bf16),
            pltpu.SemaphoreType.DMA((n_ctx,)),
        ],
        compiler_params=params(),
        cost_estimate=cost(7e9, 6e6),
        name="norm_rows",
    )(*x_pieces, gain)


def attn_fwd_kernel(n_ctx, n_w, qh, kvh, place_ref, *refs):
    w_refs, refs = refs[:n_w], refs[n_w:]
    (h1_ref, row_ref, col_ref, start_ref, cos_ref, sin_ref), refs = refs[:6], refs[6:]
    (near_ref, far_ref, q_ref, k_ref, v_ref, lse_ref, w_out), refs = refs[:7], refs[7:]
    w_ref, h1_buf, qkv_buf, sorted_buf, sem_w, sem_h, sem_out = refs
    tok = h1_buf.shape[1]
    total = n_ctx * tok
    group = qh // kvh
    part = w_refs[0].shape[1]
    w_copies = []
    for k in range(n_w):
        for m in range(n_ctx):
            i = k * n_ctx + m
            row0 = pl.multiple_of(place_ref[n_w * n_ctx + k] * part, 16)
            spot = w_ref.at[place_ref[i], pl.ds(row0, part), :]
            w_copies.append(pltpu.make_async_copy(w_refs[k].at[m], spot, sem_w.at[i]))
    h_copies = [pltpu.make_async_copy(h1_ref.at[m], h1_buf.at[m], sem_h.at[m]) for m in range(n_ctx)]
    for c in w_copies + h_copies:
        c.start()
    for c in w_copies + h_copies:
        c.wait()
    keep_w = pltpu.make_async_copy(w_ref, w_out, sem_out)
    keep_w.start()
    q_chunks = qh * HEAD_SIZE // LANES
    k_chunks = kvh * HEAD_SIZE // LANES

    def project(m, carry):
        w = w_ref[...].reshape(MODEL_WIDTH, w_ref.shape[2])
        qkv = dot(h1_buf[m], w)
        rows = pl.ds(m * tok, tok)
        cos, sin = cos_ref[rows, :], sin_ref[rows, :]
        out = []
        for j in range(q_chunks + 2 * k_chunks):
            piece = qkv[:, j * LANES : (j + 1) * LANES]
            if j < q_chunks + k_chunks:
                piece = piece * cos + half_swap(piece) * sin
                if j < q_chunks:
                    piece = piece * HEAD_SIZE**-0.5
            out.append(piece)
        qkv_buf[rows, :] = jnp.concatenate(out, axis=1).astype(bf16)
        return carry

    lax.fori_loop(0, n_ctx, project, 0)

    def arrange(b, carry):
        rows = pl.ds(b * tok, tok)
        place = lax.broadcasted_iota(jnp.int32, (tok, total), 0) + b * tok
        pick = (place == row_ref[...]).astype(f32).astype(bf16)
        s = dot(pick, qkv_buf[...])
        lane = lane_iota(tok)
        one = jnp.where(lane == HEAD_SIZE, 1.0, 0.0)
        for h in range(qh + 2 * kvh):
            piece = s[:, (h // 2) * LANES : (h // 2 + 1) * LANES]
            if h % 2:
                piece = pltpu.roll(piece, HEAD_SIZE, 1)
            fill = jnp.zeros_like(one) if h < qh + kvh else one
            piece = jnp.where(lane < HEAD_SIZE, piece, fill).astype(bf16)
            if h < qh:
                q_ref[h, rows, :] = piece
            elif h < qh + kvh:
                k_ref[h - qh, rows, :] = piece
            else:
                v_ref[h - qh - kvh, rows, :] = piece
        return carry

    lax.fori_loop(0, n_ctx, arrange, 0)
    window = min(MOST_LEN + QROWS, total)
    lse_ref[...] = jnp.zeros_like(lse_ref)

    def attend(b, carry):
        q0 = pl.multiple_of(b * QROWS, QROWS)
        k0 = pl.multiple_of(jnp.maximum(q0 + QROWS - window, 0), QROWS)
        rows, keys = pl.ds(q0, QROWS), pl.ds(k0, window)
        kidx = lax.broadcasted_iota(jnp.int32, (window, QROWS), 0) + k0
        qidx = lax.broadcasted_iota(jnp.int32, (window, QROWS), 1) + q0
        allowed = (kidx <= qidx) & (kidx >= start_ref[:, rows])
        for g in range(kvh):
            q = q_ref[g * group : (g + 1) * group, rows, :].reshape(group * QROWS, LANES)
            s = dot(k_ref[g, keys, :], q, NT)
            tops, exps = [], []
            for i in range(group):
                one = jnp.where(allowed, s[:, i * QROWS : (i + 1) * QROWS], MASKED)
                top = jnp.max(one, axis=0, keepdims=True)
                tops.append(top)
                exps.append(jnp.exp(one - top).astype(bf16))
            o = dot(v_ref[g, keys, :], jnp.concatenate(exps, axis=1), TN)
            total_e = o[HEAD_SIZE : HEAD_SIZE + 1, :]
            o = (o[:HEAD_SIZE, :] / total_e).astype(bf16)
            lse = jnp.log(total_e)
            for i in range(group):
                h = g * group + i
                cols = slice(i * QROWS, (i + 1) * QROWS)
                lse_ref[h : h + 1, rows] = tops[i] + lse[:, cols]
                sorted_buf[h * HEAD_SIZE : (h + 1) * HEAD_SIZE, rows] = o[:, cols]
        return carry

    lax.fori_loop(0, total // QROWS, attend, 0)

    def scatter(m, carry):
        place = lax.broadcasted_iota(jnp.int32, (tok, total), 1)
        pick = (place == col_ref[pl.ds(m * tok, tok), :]).astype(f32).astype(bf16)
        out = dot(pick, sorted_buf[...], NT).astype(bf16)

        @pl.when(m < n_ctx // 2)
        def _():
            near_ref[m] = out

        @pl.when(m >= n_ctx // 2)
        def _():
            far_ref[m - n_ctx // 2] = out

        return carry

    lax.fori_loop(0, n_ctx, scatter, 0)
    keep_w.wait()


def attn_fwd(places, w_pieces, n_dp, h1, row, col, start_row, cos, sin, qh, kvh):
    n_w = len(w_pieces)
    n_ctx, tok = h1.shape[:2]
    total = n_ctx * tok
    width = w_pieces[0].shape[2]
    rows = w_pieces[0].shape[1] * (n_w // n_dp)
    shape = jax.ShapeDtypeStruct
    return pl.pallas_call(
        functools.partial(attn_fwd_kernel, n_ctx, n_w, qh, kvh),
        out_shape=(
            shape((n_ctx // 2, tok, qh * HEAD_SIZE), bf16),
            shape((n_ctx // 2, tok, qh * HEAD_SIZE), bf16),
            shape((qh, total, LANES), bf16),
            shape((kvh, total, LANES), bf16),
            shape((kvh, total, LANES), bf16),
            shape((-(-qh // 8) * 8, total), f32),
            shape((n_ctx * n_dp, rows, width), bf16),
        ),
        in_specs=[SMEM] + [ANY] * (n_w + 1) + [VMEM] * 5,
        out_specs=(VMEM,) * 6 + (ANY,),
        scratch_shapes=[
            pltpu.VMEM((n_ctx * n_dp, rows, width), bf16),
            pltpu.VMEM((n_ctx, tok, MODEL_WIDTH), bf16),
            pltpu.VMEM((total, width), bf16),
            pltpu.VMEM((qh * HEAD_SIZE, total), bf16),
            pltpu.SemaphoreType.DMA((n_ctx * n_w,)),
            pltpu.SemaphoreType.DMA((n_ctx,)),
            pltpu.SemaphoreType.DMA,
        ],
        compiler_params=params(),
        cost_estimate=cost(20e9, 20e6),
        name="attn_fwd",
    )(places, *w_pieces, h1, row, col, start_row, cos, sin)


def attn_bwd_kernel(n_ctx, qh, kvh, *refs):
    db_refs, refs = refs[:n_ctx], refs[n_ctx:]
    (wo_ref, near_ref, far_ref, q_ref, k_ref, v_ref, lse_ref), refs = refs[:7], refs[7:]
    (row_ref, col_ref, start_ref, cos_ref, sin_ref, cos_t, sin_t), refs = refs[:7], refs[7:]
    out_ref, db_buf, dat_buf, del_buf, do_buf, dq_buf, dk_buf, dv_buf, kv_buf, sem = refs
    tok = db_buf.shape[1]
    total = n_ctx * tok
    group = qh // kvh
    k_chunks = kvh * HEAD_SIZE // LANES
    n_rows = lse_ref.shape[0]
    copies = [pltpu.make_async_copy(db_refs[m], db_buf.at[m], sem.at[m]) for m in range(n_ctx)]
    for c in copies:
        c.start()
    dk_buf[...] = jnp.zeros_like(dk_buf)
    dv_buf[...] = jnp.zeros_like(dv_buf)
    for c in copies:
        c.wait()
    q_width = qh * HEAD_SIZE
    head_of = lax.broadcasted_iota(jnp.int32, (n_rows, q_width), 1) // HEAD_SIZE
    ones = (head_of == lax.broadcasted_iota(jnp.int32, (n_rows, q_width), 0)).astype(f32).astype(bf16)

    def lift(m, carry):
        rows = pl.ds(pl.multiple_of(m * tok, tok), tok)
        low = dot(db_buf[m], wo_ref[...], NT).astype(bf16)
        dat_buf[rows, :] = low
        attn = jnp.where(m < n_ctx // 2, near_ref[m % (n_ctx // 2)], far_ref[m % (n_ctx // 2)])
        prod = low.astype(f32) * attn.astype(f32)
        hi = prod.astype(bf16)
        rest = (prod - hi.astype(f32)).astype(bf16)
        delta = dot(ones, hi, NT) + dot(ones, rest, NT)
        for i, v in enumerate(three_parts(delta)):
            del_buf[i * n_rows : (i + 1) * n_rows, rows] = v
        return carry

    lax.fori_loop(0, n_ctx, lift, 0)
    delta_parts = del_buf[...].astype(bf16)

    def arrange(b, carry):
        rows = pl.ds(pl.multiple_of(b * tok, tok), tok)
        place = lax.broadcasted_iota(jnp.int32, (tok, total), 0) + b * tok
        pick = (place == row_ref[...]).astype(f32).astype(bf16)
        s = dot(pick, dat_buf[...])
        lane = lane_iota(tok)
        for h in range(qh):
            piece = s[:, (h // 2) * LANES : (h // 2 + 1) * LANES]
            if h % 2:
                piece = pltpu.roll(piece, HEAD_SIZE, 1)
            do_buf[h, rows, :] = jnp.where(lane < HEAD_SIZE, piece, 0.0).astype(bf16)
        d = dot(delta_parts, pick, NT)
        del_buf[:n_rows, rows] = d[:n_rows] + d[n_rows : 2 * n_rows] + d[2 * n_rows :]
        return carry

    lax.fori_loop(0, n_ctx, arrange, 0)
    window = min(MOST_LEN + QROWS, total)

    def attend(b, carry):
        q0 = pl.multiple_of(b * QROWS, QROWS)
        k0 = pl.multiple_of(jnp.maximum(q0 + QROWS - window, 0), QROWS)
        rows, keys = pl.ds(q0, QROWS), pl.ds(k0, window)
        kidx = lax.broadcasted_iota(jnp.int32, (window, QROWS), 0) + k0
        qidx = lax.broadcasted_iota(jnp.int32, (window, QROWS), 1) + q0
        allowed = (kidx <= qidx) & (kidx >= start_ref[:, rows])
        for g in range(kvh):
            heads = slice(g * group, (g + 1) * group)
            q = q_ref[heads, rows, :].reshape(group * QROWS, LANES)
            do = do_buf[heads, rows, :].reshape(group * QROWS, LANES)
            k, v = k_ref[g, keys, :], v_ref[g, keys, :]
            s, dp = dot(k, q, NT), dot(v, do, NT)
            probs, grads = [], []
            for i in range(group):
                h = g * group + i
                cols = slice(i * QROWS, (i + 1) * QROWS)
                p = jnp.where(allowed, jnp.exp(s[:, cols] - lse_ref[h : h + 1, rows]), 0.0)
                probs.append(p.astype(bf16))
                grads.append((p * (dp[:, cols] - del_buf[h : h + 1, rows])).astype(bf16))
            p, ds = jnp.concatenate(probs, axis=1), jnp.concatenate(grads, axis=1)
            dv_buf[g, keys, :] += dot(p, do)
            dk_buf[g, keys, :] += dot(ds, q)
            dq = dot(k, ds, TN)
            for i in range(group):
                h = g * group + i
                turned = dq[:HEAD_SIZE, i * QROWS : (i + 1) * QROWS] * HEAD_SIZE**-0.5
                half = HEAD_SIZE // 2
                low, high = turned[:half], turned[half:]
                cos, sin = cos_t[:, rows], sin_t[:, rows]
                turned = jnp.concatenate([low * cos + high * sin, high * cos - low * sin], axis=0)
                dq_buf[h * HEAD_SIZE : (h + 1) * HEAD_SIZE, rows] = turned.astype(bf16)
        return carry

    lax.fori_loop(0, total // QROWS, attend, 0)

    def turn_back(b, carry):
        rows = pl.ds(b * tok, tok)
        cos, sin = cos_ref[rows, :], sin_ref[rows, :]
        lane = lane_iota(tok)
        heads = [dk_buf[h, rows, :] for h in range(kvh)] + [dv_buf[h, rows, :] for h in range(kvh)]
        for j in range(2 * k_chunks):
            pair = jnp.where(lane < HEAD_SIZE, heads[2 * j], pltpu.roll(heads[2 * j + 1], HEAD_SIZE, 1))
            if j < k_chunks:
                pair = pair * cos - half_swap(pair) * sin
            kv_buf[rows, j * LANES : (j + 1) * LANES] = pair.astype(bf16)
        return carry

    lax.fori_loop(0, n_ctx, turn_back, 0)

    def scatter(m, carry):
        place = lax.broadcasted_iota(jnp.int32, (tok, total), 1)
        pick = (place == col_ref[pl.ds(m * tok, tok), :]).astype(f32).astype(bf16)
        out_ref[m, :, :q_width] = dot(pick, dq_buf[...], NT).astype(bf16)
        out_ref[m, :, q_width:] = dot(pick, kv_buf[...]).astype(bf16)
        return carry

    lax.fori_loop(0, n_ctx, scatter, 0)


def attn_bwd(db_pieces, wo, near, far, q, k, v, lse, row, col, start_row, tables, qh, kvh):
    n_ctx = len(db_pieces)
    tok = db_pieces[0].shape[0]
    total = n_ctx * tok
    width = (qh + 2 * kvh) * HEAD_SIZE
    return pl.pallas_call(
        functools.partial(attn_bwd_kernel, n_ctx, qh, kvh),
        out_shape=jax.ShapeDtypeStruct((n_ctx, tok, width), bf16),
        in_specs=[ANY] * n_ctx + [VMEM] * 14,
        out_specs=VMEM,
        scratch_shapes=[
            pltpu.VMEM((n_ctx, tok, MODEL_WIDTH), bf16),
            pltpu.VMEM((total, qh * HEAD_SIZE), bf16),
            pltpu.VMEM((3 * lse.shape[0], total), f32),
            pltpu.VMEM((qh, total, LANES), bf16),
            pltpu.VMEM((qh * HEAD_SIZE, total), bf16),
            pltpu.VMEM((kvh, total, LANES), f32),
            pltpu.VMEM((kvh, total, LANES), f32),
            pltpu.VMEM((total, 2 * kvh * HEAD_SIZE), bf16),
            pltpu.SemaphoreType.DMA((n_ctx,)),
        ],
        compiler_params=params(),
        cost_estimate=cost(25e9, 20e6),
        name="attn_bwd",
    )(*db_pieces, wo, near, far, q, k, v, lse, row, col, start_row, *tables)


def pick_rows(e, cap, routes):
    tok = routes.shape[1]
    before = lax.broadcasted_iota(jnp.int32, (tok, tok), 0) < lax.broadcasted_iota(
        jnp.int32, (tok, tok), 1
    )
    names = lax.broadcasted_iota(jnp.int32, (LANES, tok), 0)
    slots = lax.broadcasted_iota(jnp.int32, (cap, tok), 0).astype(f32)
    hit = jnp.zeros((1, tok), f32)
    named = jnp.zeros((LANES, tok), f32)
    for j in range(routes.shape[0]):
        hit = hit + jnp.where(routes[j : j + 1] == e, 1.0, 0.0)
        named = named + jnp.where(names == routes[j : j + 1], 1.0, 0.0)
    hits = jnp.broadcast_to(hit, (8, tok)).astype(bf16)
    slot = dot(hits, before.astype(f32).astype(bf16))[0:1]
    pick = jnp.where((slots == slot) & (hit > 0.5), 1.0, 0.0).astype(bf16)
    return pick, dot(pick, named.astype(bf16), NT)


TILE = 512


def expert_kernel(by_hand, cap, who_ref, *refs):
    n_in = len(PIECES) if by_hand else 1
    h_refs, dy_refs, refs = refs[:n_in], refs[n_in : 2 * n_in], refs[2 * n_in :]
    (routes_ref, wc_ref, wd_ref), refs = refs[:3], refs[3:]
    n_rows = 4 if by_hand else 2
    row_refs, refs = refs[:n_rows], refs[n_rows:]
    (xs_ref, deout_ref, act_ref, dgate_ref, dup_ref, coef_ref), refs = refs[:6], refs[6:]
    dcat, drow, yrow, refs = *refs[:3], refs[3:]
    step = pl.program_id(0)
    core = who_ref[1]
    e = who_ref[0]
    ff = wd_ref.shape[0]
    if by_hand:
        h_buf, dy_buf, sem = refs

        def copies(chip):
            got = []
            for n, (j, sib) in enumerate(PIECES):
                if j != chip:
                    continue
                col = pl.multiple_of((core + sib) % 2 * HALF, HALF)
                for i in range(2):
                    spot = (2 * j + (i ^ sib), slice(None), pl.ds(col, HALF))
                    for k, (src, buf) in enumerate(((h_refs, h_buf), (dy_refs, dy_buf))):
                        got.append(
                            pltpu.make_async_copy(src[n].at[i], buf.at[spot], sem.at[k, n, i])
                        )
            return got

        @pl.when(step == 0)
        def _():
            for j in range(4):
                for c in copies(j):
                    c.start()

        for j in range(4):

            @pl.when(step == j)
            def _():
                for c in copies(j):
                    c.wait()

        def load(buf, i, cols):
            return buf[2 * step + i, :, cols]

    else:
        h_buf, dy_buf = h_refs[0], dy_refs[0]

        def load(buf, i, cols):
            return buf[i, :, cols]

    picks, masks = [], []
    for i in range(2):
        pick, mask = pick_rows(e, cap, routes_ref[2 * step + i])
        picks.append(pick)
        masks.append(mask)
    mask = jnp.concatenate(masks, axis=0) > 0.5
    tiles = [slice(t, t + TILE) for t in range(0, MODEL_WIDTH, TILE)]
    for cols in tiles:
        for i in range(2):
            rows = slice(i * cap, (i + 1) * cap)
            xs_ref[rows, cols] = dot(picks[i], load(h_buf, i, cols)).astype(bf16)
            deout_ref[rows, cols] = dot(picks[i], load(dy_buf, i, cols)).astype(bf16)
    xs = xs_ref[...]
    logits = jnp.where(mask, dot(xs, wc_ref[:, 2 * ff :]), MASKED)
    ex = jnp.where(mask, jnp.exp(logits - jnp.max(logits, axis=1, keepdims=True)), 0.0)
    lane = lax.broadcasted_iota(jnp.int32, ex.shape, 1)
    own = lane == e
    denom = jnp.sum(ex, axis=1, keepdims=True)
    probs = ex / jnp.where(denom > 0.0, denom, 1.0)
    gp = jnp.sum(jnp.where(own, probs, 0.0), axis=1, keepdims=True)
    gate = dot(xs, wc_ref[:, :ff])
    up = dot(xs, wc_ref[:, ff : 2 * ff])
    sig = jax.nn.sigmoid(gate)
    silu = gate * sig
    act = (silu * up).astype(bf16)
    act_ref[...] = act
    dgp = jnp.zeros((2 * cap, LANES), f32)
    for cols in tiles:
        eout = dot(act, wd_ref[:, cols]).astype(bf16).astype(f32)
        dys = deout_ref[:, cols].astype(f32)
        both = dys * eout
        for c in range(0, TILE, LANES):
            dgp = dgp + both[:, c : c + LANES]
        deout_ref[:, cols] = (gp * dys).astype(bf16)
        yrow[:, cols] = (gp * eout).astype(bf16)
    dgp = jnp.sum(dgp, axis=1, keepdims=True)
    coef = gp * dgp * (jnp.where(own, 1.0, 0.0) - probs)
    hi = coef.astype(bf16).astype(f32)
    low = pltpu.roll(coef - hi, LANES // 2, 1)
    coef = jnp.where(lane < LANES // 2, hi, low).astype(bf16)
    coef_ref[...] = coef
    dact = dot(deout_ref[...], wd_ref[...], NT)
    dgate = (dact * up * sig * (1.0 + gate * (1.0 - sig))).astype(bf16)
    dup = (dact * silu).astype(bf16)
    dgate_ref[...] = dgate
    dup_ref[...] = dup
    dcat[:, :ff] = dgate
    dcat[:, ff : 2 * ff] = dup
    dcat[:, 2 * ff :] = coef
    for cols in tiles:
        drow[:, cols] = dot(dcat[...], wc_ref[cols, :], NT).astype(bf16)
    for k, buf in enumerate((drow, yrow)):
        for i in range(2):
            rows = slice(i * cap, (i + 1) * cap)
            if by_hand:
                mine = pl.multiple_of(core * HALF, HALF)
                other = pl.multiple_of((1 - core) * HALF, HALF)
                for ref, at, col in ((row_refs[2 * k], i, mine), (row_refs[2 * k + 1], 1 - i, other)):
                    ref[0, at] = dot(picks[i], buf[rows, pl.ds(col, HALF)], TN).astype(bf16)
            else:
                row_refs[k][0, i] = dot(picks[i], buf[rows, :], TN).astype(bf16)


def run_experts(who, by_hand, h_list, dy_list, routes_t, wc, wd, cap, tok):
    n_blocks = routes_t.shape[0]
    steps = n_blocks // 2
    ff = wd.shape[0]
    rows = 2 * cap
    shape = jax.ShapeDtypeStruct
    out_w = HALF if by_hand else MODEL_WIDTH
    block = pl.BlockSpec((1, 2, tok, out_w), lambda i, *_: (i, 0, 0, 0))
    other = pl.BlockSpec((1, 2, tok, out_w), lambda i, *_: (i // 2 + i % 2 * 2, 0, 0, 0))
    wide = pl.BlockSpec((rows, MODEL_WIDTH), lambda i, *_: (i, 0))
    thin = pl.BlockSpec((rows, ff), lambda i, *_: (i, 0))
    edge = pl.BlockSpec((rows, LANES), lambda i, *_: (i, 0))
    whole = pl.BlockSpec((2, tok, MODEL_WIDTH), lambda i, *_: (i, 0, 0))
    n_in = len(h_list)
    scratch = [
        pltpu.VMEM((rows, wc.shape[1]), bf16),
        pltpu.VMEM((rows, MODEL_WIDTH), bf16),
        pltpu.VMEM((rows, MODEL_WIDTH), bf16),
    ]
    if by_hand:
        scratch += [
            pltpu.VMEM((n_blocks, tok, MODEL_WIDTH), bf16),
            pltpu.VMEM((n_blocks, tok, MODEL_WIDTH), bf16),
            pltpu.SemaphoreType.DMA((2, n_in, 2)),
        ]
    row_specs = [block, other] * 2 if by_hand else [block] * 2
    grid_spec = pltpu.PrefetchScalarGridSpec(
        num_scalar_prefetch=1,
        grid=(steps,),
        in_specs=[ANY if by_hand else whole] * (2 * n_in) + [VMEM] * 3,
        out_specs=row_specs + [wide] * 2 + [thin] * 3 + [edge],
        scratch_shapes=scratch,
    )
    return pl.pallas_call(
        functools.partial(expert_kernel, by_hand, cap),
        out_shape=[shape((steps, 2, tok, out_w), bf16)] * len(row_specs)
        + [shape((steps * rows, MODEL_WIDTH), bf16)] * 2
        + [shape((steps * rows, ff), bf16)] * 3
        + [shape((steps * rows, LANES), bf16)],
        grid_spec=grid_spec,
        compiler_params=params(60),
        cost_estimate=cost(30e9, 30e6),
        name="experts",
    )(who, *h_list, *dy_list, routes_t, wc, wd)


def flip(v, axis, bit):
    n = lax.axis_size(axis)
    return lax.ppermute(v, axis, [(i, i ^ bit) for i in range(n)])


def step_up(v, axis):
    n = lax.axis_size(axis)
    return lax.ppermute(v, axis, [(i, (i + 1) % n) for i in range(n)])


def ctx_gather(v):
    n = lax.axis_size("context")
    pieces = {0: v}
    bit = n // 2
    while bit:
        for m in list(pieces):
            pieces[m | bit] = flip(pieces[m], "context", bit)
        bit //= 2
    return [pieces[m] for m in range(n)]


def add_low(a, b):
    return (a.astype(f32) + b.astype(f32)).astype(bf16)


def ring(v, axis, deps=()):
    pieces = [v]
    for i in range(lax.axis_size(axis) - 1):
        sent = after(pieces[-1], *deps[i]) if i < len(deps) else pieces[-1]
        pieces.append(step_up(sent, axis))
    return pieces


def send_all(v, axis):
    n = lax.axis_size(axis)
    return [v] + [
        lax.ppermute(v, axis, [(i, (i + k) % n) for i in range(n)]) for k in range(1, n)
    ]


def ring_sum(chunk, axis, deps=()):
    n, d = lax.axis_size(axis), lax.axis_index(axis)
    part = chunk(lax.rem(d + n - 1, n)).astype(bf16)
    for hop in range(n - 1):
        got = step_up(part, axis)
        own = chunk(lax.rem(d + 2 * n - 2 - hop, n))
        if hop < len(deps):
            own = after(own, *deps[hop])
        part = (got.astype(f32) + own.astype(f32)).astype(bf16)
    return part


def direct_sum(chunk, axis, *deps):
    n, d = lax.axis_size(axis), lax.axis_index(axis)
    total = chunk(d).astype(f32)
    if deps:
        total = after(total, *deps)
    for k in range(1, n):
        sent = chunk(lax.rem(d + k, n)).astype(bf16)
        got = lax.ppermute(sent, axis, [(i, (i + k) % n) for i in range(n)])
        total = total + got.astype(f32)
    return total


def after(v, *deps):
    return lax.optimization_barrier((v, *deps))[0]


HALF = MODEL_WIDTH // 2
PLANE = ("expert", "context")
PIECES = ((0, 0), (1, 0), (2, 0), (3, 0), (0, 1), (2, 1), (1, 1), (3, 1))


def small_plane():
    return lax.axis_size("expert") == 2 and lax.axis_size("context") == 4


def hop_plane(v, second):
    pairs = []
    for i in range(8):
        along_context = (i % 2 == 0) != second
        pairs.append((i, i ^ 2 if along_context else i ^ 4))
    return lax.ppermute(v, PLANE, pairs)


def halves(v, core):
    left, right = v[..., :HALF], v[..., HALF:]
    return jnp.where(core == 0, left, right), jnp.where(core == 0, right, left)


def sync(*values):
    return lax.optimization_barrier(values)


def plane_near(v):
    core = lax.axis_index("context") % 2
    mine, given = halves(v, core)
    return jnp.stack([mine, flip(given, "context", 1)])


def plane_far(u0, u1):
    return hop_plane(u0, True), hop_plane(u1, True)


def plane_share(own):
    return list(own) + [flip(u, "context", 1) for u in own]


def plane_gather(v):
    if not small_plane():
        return [lax.all_gather(v, PLANE, axis=0, tiled=False)]
    u0 = plane_near(v)
    u1 = hop_plane(u0, False)
    return plane_share((u0, u1) + plane_far(u0, u1))


class PlaneSum:
    def __init__(self, rows):
        self.small = small_plane()
        self.rows = rows
        if self.small:
            self.keep, give = rows
            self.got = flip(give, "context", 1)
            self.far = add_low(self.keep[2:], self.got[2:])

    def first(self):
        if self.small:
            self.got2 = hop_plane(self.far, True)

    def second(self):
        if self.small:
            near = self.keep[:2].astype(f32) + self.got[:2].astype(f32) + self.got2.astype(f32)
            self.near = near[0]
            self.got1 = hop_plane(near[1].astype(bf16), False)

    def finish(self):
        if not self.small:
            (both,) = self.rows
            flat = both.reshape(-1, both.shape[-1])
            return lax.psum_scatter(flat, PLANE, scatter_dimension=0, tiled=True).astype(f32)
        core = lax.axis_index("context") % 2
        whole = self.near + self.got1.astype(f32)
        other = flip(whole[1].astype(bf16), "context", 1).astype(f32)
        left = jnp.where(core == 0, whole[0], other)
        right = jnp.where(core == 0, other, whole[0])
        return jnp.concatenate([left, right], axis=1)


def ctx_sum(p):
    far = add_low(p[2], flip(p[3], "context", 1))
    own = p[0].astype(f32) + flip(p[1], "context", 1).astype(f32)
    return own + flip(far, "context", 2).astype(f32)


def put_in_order(places, pieces, name):
    n = len(pieces)
    rows, width = pieces[0].shape

    def kernel(place_ref, *refs):
        out_ref, sem = refs[n:]
        copies = [
            pltpu.make_async_copy(refs[k], out_ref.at[place_ref[k]], sem.at[k]) for k in range(n)
        ]
        for c in copies:
            c.start()
        for c in copies:
            c.wait()

    return pl.pallas_call(
        kernel,
        out_shape=jax.ShapeDtypeStruct((n, rows, width), pieces[0].dtype),
        in_specs=[SMEM] + [ANY] * n,
        out_specs=VMEM,
        scratch_shapes=[pltpu.SemaphoreType.DMA((n,))],
        cost_estimate=cost(0, 2 * n * rows * width * 2),
        name=name,
    )(places, *pieces)


def columns_of(spots, near, far, qw, kw):
    n_ctx, part, width = near.shape

    def kernel(spot_ref, near_ref, far_ref, *outs):
        for k, ref in enumerate((near_ref, far_ref)):
            row = pl.multiple_of(spot_ref[n_ctx + k] * part, 16)
            for m in range(n_ctx):
                v = ref[m].astype(f32)
                lo = 0
                for out, w in zip(outs, (qw, kw, kw)):
                    col = pl.multiple_of(spot_ref[m] * w, LANES)
                    out[pl.ds(row, part), pl.ds(col, w)] = v[:, lo : lo + w]
                    lo += w

    shape = jax.ShapeDtypeStruct
    return pl.pallas_call(
        kernel,
        out_shape=tuple(shape((2 * part, n_ctx * w), f32) for w in (qw, kw, kw)),
        in_specs=[SMEM, VMEM, VMEM],
        out_specs=(VMEM,) * 3,
        cost_estimate=cost(0, 2e6),
        name="columns_of",
    )(spots, near, far)


def position_tables(lengths_row, row, freq):
    total = row.shape[1]
    half = HEAD_SIZE // 2

    def kernel(len_ref, row_ref, freq_ref, *outs):
        cos_d, sin_d, cos_s, sin_s, cos_t, sin_t, start_ref = outs

        def start_of(place):
            end, start = 0, jnp.zeros_like(place)
            for j in range(lengths_row.shape[0]):
                end = end + len_ref[j]
                start = start + jnp.where(place >= end, len_ref[j], 0)
            return start

        dealt = row_ref[...]
        placed = lax.broadcasted_iota(jnp.int32, (1, total), 1)
        start_ref[...] = start_of(placed)
        for place, cos_ref, sin_ref in ((dealt, cos_d, sin_d), (placed, cos_s, sin_s)):
            angle = freq_ref[...] * (place - start_of(place)).astype(f32)
            cos, sin = jnp.cos(angle), jnp.sin(angle)
            cos_ref[...] = jnp.concatenate([cos] * 4, axis=0).T
            sin_ref[...] = jnp.concatenate([-sin, sin] * 2, axis=0).T
        cos_t[...] = cos
        sin_t[...] = sin

    shape = jax.ShapeDtypeStruct
    wide, thin = shape((total, LANES), f32), shape((half, total), f32)
    return pl.pallas_call(
        kernel,
        out_shape=(wide, wide, wide, wide, thin, thin, shape((1, total), jnp.int32)),
        in_specs=[SMEM, VMEM, VMEM],
        out_specs=(VMEM,) * 7,
        compiler_params=params(),
        cost_estimate=cost(0, 0),
        name="position_tables",
    )(lengths_row, row, freq)


def widen(gate, up, down):
    def kernel(a_ref, b_ref, c_ref, a_out, b_out, c_out):
        a_out[...] = a_ref[...].astype(f32)
        b_out[...] = b_ref[...].astype(f32)
        c_out[...] = c_ref[...].astype(f32).T

    shape = jax.ShapeDtypeStruct
    return pl.pallas_call(
        kernel,
        out_shape=(shape(gate.shape, f32), shape(up.shape, f32), shape(down.shape[::-1], f32)),
        in_specs=[VMEM] * 3,
        out_specs=(VMEM,) * 3,
        compiler_params=params(),
        cost_estimate=cost(0, 0),
        name="widen",
    )(gate, up, down)


def finish_input(d_middle, near, far, x, gain):
    tok = x.shape[0]

    def kernel(dm_ref, near_ref, far_ref, x_ref, gain_ref, out_ref):
        v = x_ref[...].astype(f32)
        dh = near_ref[...] + far_ref[...].astype(f32)
        r = lax.rsqrt(jnp.mean(v * v, axis=-1, keepdims=True) + NORM_EPS)
        scaled = gain_ref[...] * dh
        inner = jnp.sum(scaled * v, axis=-1, keepdims=True)
        dv = r * scaled - v * (r * r * r) * (inner / MODEL_WIDTH)
        out_ref[...] = (dm_ref[...] + dv).astype(bf16)

    step = 64
    rows = pl.BlockSpec((step, MODEL_WIDTH), lambda i: (i, 0))
    return pl.pallas_call(
        kernel,
        out_shape=jax.ShapeDtypeStruct((tok, MODEL_WIDTH), bf16),
        grid=(tok // step,),
        in_specs=[rows] * 4 + [pl.BlockSpec((1, MODEL_WIDTH), lambda i: (0, 0))],
        out_specs=rows,
        compiler_params=params(),
        cost_estimate=cost(0, 0),
        name="finish_input",
    )(d_middle, near, far, x, gain)


def rms_back(dh, v, r, gain):
    inner = jnp.sum(gain * dh * v, axis=-1, keepdims=True)
    dv = r * gain * dh - v * (r * r * r) * (inner / MODEL_WIDTH)
    return dv, jnp.sum(dh * v * r, axis=0)


def body(
    hidden, cotangent, token_order, lengths, routes, attn_gain, w_query, key_weight,
    value_weight, w_out, ffn_gain, w_router, w_gate, w_up, w_down,
):
    tok, top = hidden.shape[1], routes.shape[2]
    n_exp, n_ctx, n_dp = (lax.axis_size(a) for a in ("expert", "context", "dp"))
    experts = n_exp * n_ctx
    cap = -(-(9 * tok * top // (8 * experts)) // 16) * 16
    qh, kvh = QUERY_HEADS // n_ctx, KEY_VALUE_HEADS // n_ctx
    qw, kw = qh * HEAD_SIZE, kvh * HEAD_SIZE
    rows = w_query.shape[0]
    ex, cx, dx = (lax.axis_index(a) for a in ("expert", "context", "dp"))
    my_expert = ex * n_ctx + cx
    total = n_ctx * tok

    def for_context(c):
        return jnp.concatenate(
            [
                lax.dynamic_slice_in_dim(w_query, c * qw, qw, 1),
                lax.dynamic_slice_in_dim(key_weight, c * kw, kw, 1),
                lax.dynamic_slice_in_dim(value_weight, c * kw, kw, 1),
            ],
            axis=1,
        )

    params_t = jnp.concatenate([attn_gain[None], ffn_gain[None], w_router.T], axis=0)
    p_rows = params_t.shape[0]
    params_t = jnp.pad(params_t, ((0, 0), (0, tok - rows)))
    routes_t = routes[0].T.astype(bf16)
    k_of = jnp.arange(n_dp, dtype=jnp.int32)
    d_of = lax.rem(dx - k_of + n_dp, n_dp)
    c_of = cx ^ jnp.arange(n_ctx, dtype=jnp.int32)
    places = (c_of[None, :] * n_dp + d_of[:, None]).reshape(-1).astype(jnp.int32)

    def own_params(stack):
        stack = stack.reshape(n_dp * n_ctx, p_rows, -1)[:, :, :rows]
        at = d_of[None, :] * n_ctx + (cx ^ jnp.arange(n_ctx, dtype=jnp.int32))[:, None]
        flat = stack[at.reshape(-1)].transpose(1, 0, 2).reshape(p_rows, MODEL_WIDTH)
        router = jnp.pad(flat[2:].T, ((0, 0), (0, LANES // 2 - experts)))
        return flat[0:1].astype(f32), flat[1:2].astype(f32), router

    def own_routes(stack):
        return stack.reshape(experts, top, tok).astype(jnp.int32)

    def positions(order_row, lengths_row):
        order_rel = order_row.reshape(n_ctx, tok)[c_of].reshape(-1)
        half = HEAD_SIZE // 2
        freq = ROPE_BASE ** (-(jnp.arange(half, dtype=f32) * 2.0 / HEAD_SIZE))
        row, col = order_rel[None, :], order_rel[:, None]
        return (row, col, *position_tables(lengths_row, row, freq[:, None]))

    order_row, ends_in = token_order[0], lengths[0]

    def gather_plane(v):
        return lax.all_gather(v, PLANE, axis=0, tiled=False)

    def gather_out(v):
        return lax.all_gather(v, "dp", axis=0, tiled=True)

    x_own, dy_own = hidden[0], cotangent[0]
    if small_plane():
        part = rows // 2

        def half_for(c):
            return lax.dynamic_slice_in_dim(for_context(c), ex * part, part, 0)

        got = [half_for(cx)] + [flip(half_for(cx ^ m), "context", m) for m in range(1, n_ctx)]
        shards = send_all(params_t, "dp")
        dy0 = plane_near(dy_own)
        w0, dy0, *shards = sync(jnp.stack(got), dy0, *shards)
        note = jnp.concatenate([routes_t] + shards, axis=0)
        mine, theirs = [w0], []
        for k in range(n_dp - 1):
            nxt, other = step_up(mine[-1], "dp"), flip(mine[-1], "expert", 1)
            if k == 0:
                note2 = jnp.stack([note, flip(note, "context", 2)])
                x2 = flip(after(x_own, note2), "context", 2)
                nxt, other, note2, order_row, ends_in = sync(nxt, other, note2, order_row, ends_in)
            elif k == 1:
                dy1 = hop_plane(after(dy0, mine[-1]), False)
                near = flip(note2, "context", 1)
                note4 = jnp.stack([note2[0], near[0], note2[1], near[1]])
                nxt, other, x2, note4 = sync(nxt, other, x2, note4)
                x1, x3 = flip(x_own, "context", 1), flip(x2, "context", 1)
                where = positions(order_row, ends_in)
                shards = note4[:, top:].reshape(n_ctx, n_dp, p_rows, tok).swapaxes(0, 1)
                gain_a, gain_b, router = own_params(shards)
            elif k == 2:
                routes_far = flip(note4[:, :top], "expert", 1)
                nxt, other, gain_a, dy1 = sync(nxt, other, gain_a, dy1)
                h1 = norm_rows([x_own, x1, x2, x3], gain_a)
            mine.append(nxt)
            theirs.append(other)
        theirs.append(flip(mine[-1], "expert", 1))
        c = lax.rem(cx, 2)
        routes_rel = jnp.stack([note4[:, :top], routes_far]).reshape(8, top, tok)
        even = jnp.array([0, 1, 2, 3, 4, 5, 6, 7], jnp.int32)
        odd = jnp.array([0, 1, 4, 5, 2, 3, 6, 7], jnp.int32)
        routes_all = own_routes(routes_rel[jnp.where(c == 0, even, odd)])
        theirs[-1], router, h1, routes_all, dy1 = sync(theirs[-1], router, h1, routes_all, dy1)
        wo = gather_out(after(w_out, mine[-1]))
        dy2, dy3 = plane_far(after(dy0, theirs[-1]), dy1)
        w_pieces = mine + theirs
        spots = jnp.concatenate(
            [places, places, jnp.broadcast_to(ex, (n_dp,)), jnp.broadcast_to(1 - ex, (n_dp,))]
        ).astype(jnp.int32)
    else:
        got = [for_context(cx)]
        for m in range(1, n_ctx):
            got.append(flip(for_context(cx ^ m), "context", m))
        w_pieces = ring(jnp.stack(got), "dp")
        shards = jnp.stack(send_all(jnp.stack(ctx_gather(params_t)), "dp"))
        gain_a, gain_b, router = own_params(shards)
        routes_all = own_routes(lax.all_gather(routes_t, PLANE, axis=0, tiled=False))
        h1 = norm_rows(ctx_gather(x_own), gain_a)
        dy_all, wo = gather_plane(cotangent[0]), gather_out(w_out)
        spots = jnp.concatenate([places, jnp.zeros((n_dp,), jnp.int32)])
        where = positions(order_row, ends_in)
    row, col, cos_d, sin_d, *placed, start_row = where
    near, far, q, k, v, lse, wqkv = attn_fwd(
        spots, w_pieces, n_dp, h1, row, col, start_row, cos_d, sin_d, qh, kvh
    )
    if small_plane():
        near, wo, dy2, dy3 = sync(near, wo, dy2, dy3)
        dy_list = plane_share((dy0, dy1, dy2, dy3))
    else:
        dy_list = [dy_all]
    partial_far = dot(far.reshape(-1, qw), wo).astype(bf16).reshape(-1, tok, MODEL_WIDTH)
    partial_near = dot(near.reshape(-1, qw), wo).astype(bf16).reshape(-1, tok, MODEL_WIDTH)
    late_gate = after(w_gate[0], partial_near)
    w_cat = jnp.concatenate([late_gate, w_up[0], router, router], axis=1)
    branch = ctx_sum([partial_near[0], partial_near[1], partial_far[0], partial_far[1]])
    branch, w_cat, *dy_list = sync(branch, w_cat, *dy_list)
    x_own = x_own.astype(f32)
    middle = x_own + branch
    r_b = lax.rsqrt(jnp.mean(middle * middle, axis=-1, keepdims=True) + NORM_EPS)
    h2 = (middle * r_b * gain_b).astype(bf16)
    h_list = plane_gather(h2)

    by_hand = small_plane()
    who = jnp.stack([my_expert, cx % 2]).astype(jnp.int32)
    out = run_experts(
        who, by_hand, h_list, dy_list, routes_all, w_cat, w_down[0], cap, tok
    )
    n_rows = 2 if by_hand else 1
    d_rows, y_rows, (xs, deout, act, dgate, dup, coef) = (
        out[:n_rows], out[n_rows : 2 * n_rows], out[2 * n_rows :],
    )
    small = small_plane()
    d_sum = PlaneSum(d_rows)
    if small:
        y_rows = (y_rows[0], after(y_rows[1], d_sum.far))
    y_sum = PlaneSum(y_rows)
    xs_late, deout_late = (after(xs, d_sum.far), after(deout, d_sum.far)) if small else (xs, deout)
    g_gate = dot(xs_late, dgate, TN).astype(bf16)
    g_up = dot(xs_late, dup, TN).astype(bf16)
    g_down = dot(deout_late, act, TN).astype(bf16)
    g_router = dot(xs_late, coef, TN)
    g_router = g_router[:, :experts] + g_router[:, LANES // 2 : LANES // 2 + experts]

    def over_dp(g, dim):
        return lax.psum_scatter(g, "dp", scatter_dimension=dim, tiled=True)

    if small:
        d_sum.first()
        sum_gate, sum_up, sum_down = over_dp(g_gate, 0), over_dp(g_up, 0), over_dp(g_down, 0)
        d_sum.got2, y_sum.far, g_gate, g_up, g_down, g_router = sync(
            d_sum.got2, y_sum.far, g_gate, g_up, g_down, g_router
        )
        d_sum.second()
    else:
        sum_gate, sum_up, sum_down = over_dp(g_gate, 0), over_dp(g_up, 0), over_dp(g_down, 0)
    dh2 = d_sum.finish()
    dy = dy_own.astype(f32)
    d_norm, g_gain_b = rms_back(dh2, middle, r_b, gain_b)
    d_middle = dy + d_norm
    if small:
        b0 = d_middle.astype(bf16)
        b2, b1 = flip(b0, "context", 2), flip(b0, "context", 1)
        b2, b1 = sync(b2, b1)
        db_pieces = [b0, b1, b2, flip(b2, "context", 1)]
        y_sum.far = after(y_sum.far, b2)
        y_sum.first()
    else:
        db_pieces = ctx_gather(d_middle.astype(bf16))
    db_last = after(db_pieces[-1], sum_gate)

    dqkv = attn_bwd(
        db_pieces[:-1] + [db_last], wo, near, far, q, k, v, lse, row, col, start_row, placed, qh, kvh
    )
    dqkv, sum_up = sync(dqkv, sum_up)
    attn = jnp.concatenate([near, after(far, dqkv)], axis=0).reshape(total, qw)
    g_out = dot(attn, jnp.concatenate(db_pieces, axis=0), TN).astype(bf16)
    dqkv_flat = dqkv.reshape(total, -1)
    h1_flat = h1.reshape(total, MODEL_WIDTH)
    g_qkv = dot(h1_flat, dqkv_flat, TN).astype(bf16)
    w_flat = wqkv.reshape(MODEL_WIDTH, -1)
    if small:
        part = rows // 2
        g5 = g_qkv.reshape(n_ctx * n_dp, 2, part, -1)
        theirs = lax.dynamic_index_in_dim(g5, 1 - ex, 1, keepdims=False)
        mine = lax.dynamic_index_in_dim(g5, ex, 1, keepdims=False)
        got = flip(theirs, "expert", 1)
        dh1_in = after(dqkv_flat, theirs, mine)
    else:
        dh1_in = dqkv_flat
    dh1_part = dot(dh1_in, w_flat, NT).astype(bf16)
    g_gain_a = jnp.sum(dh1_part.astype(f32) * h1_flat.astype(f32), axis=0) / gain_a[0]
    dh1_part = dh1_part.reshape(n_ctx, tok, MODEL_WIDTH)
    r_a = lax.rsqrt(jnp.mean(x_own * x_own, axis=-1, keepdims=True) + NORM_EPS)

    width = qw + 2 * kw
    s_out = lax.psum_scatter(g_out, "dp", scatter_dimension=0, tiled=True)

    def exchange(s):
        back = [lax.dynamic_index_in_dim(s, cx, 0, keepdims=False)]
        for m in range(1, n_ctx):
            one = lax.dynamic_index_in_dim(s, cx ^ m, 0, keepdims=False)
            back.append(flip(one, "context", m))
        return jnp.stack(back)

    tiny = jnp.concatenate([g_gain_a[None], g_gain_b[None], g_router.T], axis=0)

    def finish_rows(dh1):
        return (d_middle + rms_back(dh1, x_own, r_a, gain_a)[0]).astype(bf16)

    def spread(tiny):
        tiny = tiny.reshape(-1, n_ctx * n_dp, rows).transpose(1, 0, 2)
        tiny = lax.all_to_all(tiny, ("context", "dp"), split_axis=0, concat_axis=0, tiled=True)
        return jnp.sum(tiny, axis=0)

    if small:
        h3 = flip(dh1_part[3], "context", 1)
        hop = flip(add_low(dh1_part[2], h3), "context", 2)
        h1p = flip(dh1_part[1], "context", 1)
        dh1 = dh1_part[0].astype(f32) + h1p.astype(f32)
        y_sum.got2 = after(y_sum.got2, dqkv)
        both_g = add_low(after(mine, dh1_part), got).reshape(n_ctx, n_dp, part, width)
        sum_gate, sum_up, sum_down = widen(after(sum_gate, both_g), sum_up, sum_down)
        grad_input = finish_input(d_middle, after(dh1, both_g), hop, hidden[0], gain_a)
        y_sum.got2 = after(y_sum.got2, both_g)
        y_sum.second()
        s_qkv = ring_sum(
            lambda d: lax.dynamic_index_in_dim(both_g, d, 1, keepdims=False),
            "dp",
            [(), (hop,), (y_sum.got1,)],
        )
        tiny = after(tiny, both_g).reshape(-1, n_ctx * n_dp, rows).transpose(1, 0, 2)
        tiny = (tiny + flip(tiny, "expert", 1)).reshape(2, 2, n_dp, -1, rows)
        cy, cc = cx // 2, lax.rem(cx, 2)
        give = lax.dynamic_index_in_dim(tiny, 1 - cy, 0, keepdims=False)
        tiny = lax.dynamic_index_in_dim(tiny, cy, 0, keepdims=False) + flip(give, "context", 2)
        give = lax.dynamic_index_in_dim(tiny, 1 - cc, 0, keepdims=False)
        tiny = lax.dynamic_index_in_dim(tiny, cc, 0, keepdims=False) + flip(give, "context", 1)
        out_low = s_out.astype(bf16)
        out_far = flip(out_low, "expert", 1)
        s_qkv, out_far, y_sum.got1, tiny = sync(s_qkv, out_far, y_sum.got1, tiny)
        d_total = lax.dynamic_index_in_dim(tiny, dx, 0, keepdims=False)
        for k in range(1, n_dp):
            sent = lax.dynamic_index_in_dim(tiny, lax.rem(dx + k, n_dp), 0, keepdims=False)
            d_total = d_total + lax.ppermute(sent, "dp", [(i, (i + k) % n_dp) for i in range(n_dp)])
        tiny = d_total
        output = (middle + y_sum.finish()).astype(bf16)
        s_out = out_low.astype(f32) + out_far.astype(f32)
        near = exchange(s_qkv.astype(bf16))
        far = flip(near, "expert", 1)
        spots = jnp.concatenate([c_of, ex[None], 1 - ex[None]]).astype(jnp.int32)
        sum_q, sum_k, sum_v = columns_of(spots, near, far, qw, kw)
    else:
        dh1 = ctx_sum([dh1_part[m] for m in range(n_ctx)])
        sum_gate, sum_up, sum_down = widen(sum_gate, sum_up, sum_down)
        grad_input = finish_rows(dh1)
        tiny = spread(lax.psum(tiny, "expert"))
        g4 = g_qkv.reshape(n_ctx, n_dp, rows, width)
        s_qkv = direct_sum(lambda d: lax.dynamic_index_in_dim(g4, d, 1, keepdims=False), "dp")
        s_qkv = lax.psum(s_qkv.astype(bf16), "expert")
        s_out = lax.psum(s_out.astype(bf16), "expert").astype(f32)
        back = exchange(s_qkv)[c_of]

        def columns(lo, hi):
            return back[:, :, lo:hi].transpose(1, 0, 2).reshape(rows, -1).astype(f32)

        sum_q, sum_k, sum_v = columns(0, qw), columns(qw, qw + kw), columns(qw + kw, width)
        output = (middle + y_sum.finish()).astype(bf16)

    return (
        output[None], grad_input[None], tiny[0], sum_q, sum_k, sum_v, s_out,
        tiny[1], tiny[2:].T, sum_gate[None], sum_up[None], sum_down[None],
    )


def solution(mesh):
    tokens = P(("expert", "dp"), "context", None)
    group = P(("expert", "dp"), None)
    vec, mat = P(("context", "dp")), P(("context", "dp"), None)
    expert = P(("expert", "context"), None, None)
    by_rows = P(("expert", "context"), "dp", None)
    by_cols = P(("expert", "context"), None, "dp")
    return jax.shard_map(
        body,
        mesh=mesh,
        in_specs=(
            tokens, tokens, group, group, tokens, vec, mat, mat, mat, mat, vec, mat,
            expert, expert, expert,
        ),
        out_specs=(
            tokens, tokens, vec, mat, mat, mat, mat, vec, mat, by_rows, by_rows, by_cols,
        ),
        check_vma=False,
    )
```

```python
import functools

import jax
import jax.numpy as jnp
from jax import lax
from jax.experimental import pallas as pl
from jax.experimental.pallas import tpu as pltpu
from jax.sharding import PartitionSpec as P

MODEL_WIDTH = 1536
QUERY_HEADS = 24
KEY_VALUE_HEADS = 8
HEAD_SIZE = 64
MOST_LEN = 512
NORM_EPS = 1e-06
ROPE_BASE = 10000.0
MASKED = -1e30
QROWS = 128
LANES = 128
bf16 = jnp.bfloat16
f32 = jnp.float32
ANY = pl.BlockSpec(memory_space=pl.ANY)
VMEM = pl.BlockSpec(memory_space=pltpu.VMEM)
SMEM = pl.BlockSpec(memory_space=pltpu.SMEM)
NT = (((1,), (1,)), ((), ()))
TN = (((0,), (0,)), ((), ()))


def params(limit=56):
    return pltpu.CompilerParams(vmem_limit_bytes=limit * 1024 * 1024)


def cost(flops, nbytes):
    return pl.CostEstimate(flops=int(flops), bytes_accessed=int(nbytes), transcendentals=0)


def dot(a, b, dims=(((1,), (0,)), ((), ()))):
    return lax.dot_general(a, b, dims, preferred_element_type=f32)


def lane_iota(rows):
    return lax.broadcasted_iota(jnp.int32, (rows, LANES), 1)


def half_swap(v):
    lane = lane_iota(v.shape[0])
    low = lax.rem(lane, HEAD_SIZE) < HEAD_SIZE // 2
    up = pltpu.roll(v, LANES - HEAD_SIZE // 2, 1)
    down = pltpu.roll(v, HEAD_SIZE // 2, 1)
    return jnp.where(low, up, down)


def three_parts(v):
    hi = v.astype(bf16).astype(f32)
    mid = (v - hi).astype(bf16).astype(f32)
    return hi, mid, v - hi - mid


def norm_kernel(n_ctx, *refs):
    x_refs, (gain_ref, h1_ref, x_buf, sem) = refs[:n_ctx], refs[n_ctx:]
    tok = x_buf.shape[1]
    copies = [pltpu.make_async_copy(x_refs[m], x_buf.at[m], sem.at[m]) for m in range(n_ctx)]
    for c in copies:
        c.start()
    for c in copies:
        c.wait()
    step = 64

    def norm(i, carry):
        rows = pl.ds(pl.multiple_of(i % (tok // step) * step, step), step)
        x = x_buf[i // (tok // step), rows, :].astype(f32)
        r = lax.rsqrt(jnp.mean(x * x, axis=-1, keepdims=True) + NORM_EPS)
        h1_ref[i // (tok // step), rows, :] = (x * r * gain_ref[...]).astype(bf16)
        return carry

    lax.fori_loop(0, n_ctx * tok // step, norm, 0)


def norm_rows(x_pieces, gain):
    n_ctx, tok = len(x_pieces), x_pieces[0].shape[0]
    return pl.pallas_call(
        functools.partial(norm_kernel, n_ctx),
        out_shape=jax.ShapeDtypeStruct((n_ctx, tok, MODEL_WIDTH), bf16),
        in_specs=[ANY] * n_ctx + [VMEM],
        out_specs=VMEM,
        scratch_shapes=[
            pltpu.VMEM((n_ctx, tok, MODEL_WIDTH), bf16),
            pltpu.SemaphoreType.DMA((n_ctx,)),
        ],
        compiler_params=params(),
        cost_estimate=cost(7e9, 6e6),
        name="norm_rows",
    )(*x_pieces, gain)


def attn_fwd_kernel(n_ctx, n_w, qh, kvh, place_ref, *refs):
    w_refs, refs = refs[:n_w], refs[n_w:]
    (h1_ref, row_ref, col_ref, start_ref, cos_ref, sin_ref), refs = refs[:6], refs[6:]
    (near_ref, far_ref, q_ref, k_ref, v_ref, lse_ref, w_out), refs = refs[:7], refs[7:]
    w_ref, h1_buf, qkv_buf, sorted_buf, sem_w, sem_h, sem_out = refs
    tok = h1_buf.shape[1]
    total = n_ctx * tok
    group = qh // kvh
    part = w_refs[0].shape[1]
    w_copies = []
    for k in range(n_w):
        for m in range(n_ctx):
            i = k * n_ctx + m
            row0 = pl.multiple_of(place_ref[n_w * n_ctx + k] * part, 16)
            spot = w_ref.at[place_ref[i], pl.ds(row0, part), :]
            w_copies.append(pltpu.make_async_copy(w_refs[k].at[m], spot, sem_w.at[i]))
    h_copies = [pltpu.make_async_copy(h1_ref.at[m], h1_buf.at[m], sem_h.at[m]) for m in range(n_ctx)]
    for c in w_copies + h_copies:
        c.start()
    for c in w_copies + h_copies:
        c.wait()
    keep_w = pltpu.make_async_copy(w_ref, w_out, sem_out)
    keep_w.start()
    q_chunks = qh * HEAD_SIZE // LANES
    k_chunks = kvh * HEAD_SIZE // LANES

    def project(m, carry):
        w = w_ref[...].reshape(MODEL_WIDTH, w_ref.shape[2])
        qkv = dot(h1_buf[m], w)
        rows = pl.ds(m * tok, tok)
        cos, sin = cos_ref[rows, :], sin_ref[rows, :]
        out = []
        for j in range(q_chunks + 2 * k_chunks):
            piece = qkv[:, j * LANES : (j + 1) * LANES]
            if j < q_chunks + k_chunks:
                piece = piece * cos + half_swap(piece) * sin
                if j < q_chunks:
                    piece = piece * HEAD_SIZE**-0.5
            out.append(piece)
        qkv_buf[rows, :] = jnp.concatenate(out, axis=1).astype(bf16)
        return carry

    lax.fori_loop(0, n_ctx, project, 0)

    def arrange(b, carry):
        rows = pl.ds(b * tok, tok)
        place = lax.broadcasted_iota(jnp.int32, (tok, total), 0) + b * tok
        pick = (place == row_ref[...]).astype(f32).astype(bf16)
        s = dot(pick, qkv_buf[...])
        lane = lane_iota(tok)
        one = jnp.where(lane == HEAD_SIZE, 1.0, 0.0)
        for h in range(qh + 2 * kvh):
            piece = s[:, (h // 2) * LANES : (h // 2 + 1) * LANES]
            if h % 2:
                piece = pltpu.roll(piece, HEAD_SIZE, 1)
            fill = jnp.zeros_like(one) if h < qh + kvh else one
            piece = jnp.where(lane < HEAD_SIZE, piece, fill).astype(bf16)
            if h < qh:
                q_ref[h, rows, :] = piece
            elif h < qh + kvh:
                k_ref[h - qh, rows, :] = piece
            else:
                v_ref[h - qh - kvh, rows, :] = piece
        return carry

    lax.fori_loop(0, n_ctx, arrange, 0)
    window = min(MOST_LEN + QROWS, total)
    lse_ref[...] = jnp.zeros_like(lse_ref)

    def attend(b, carry):
        q0 = pl.multiple_of(b * QROWS, QROWS)
        k0 = pl.multiple_of(jnp.maximum(q0 + QROWS - window, 0), QROWS)
        rows, keys = pl.ds(q0, QROWS), pl.ds(k0, window)
        kidx = lax.broadcasted_iota(jnp.int32, (window, QROWS), 0) + k0
        qidx = lax.broadcasted_iota(jnp.int32, (window, QROWS), 1) + q0
        allowed = (kidx <= qidx) & (kidx >= start_ref[:, rows])
        for g in range(kvh):
            q = q_ref[g * group : (g + 1) * group, rows, :].reshape(group * QROWS, LANES)
            s = dot(k_ref[g, keys, :], q, NT)
            tops, exps = [], []
            for i in range(group):
                one = jnp.where(allowed, s[:, i * QROWS : (i + 1) * QROWS], MASKED)
                top = jnp.max(one, axis=0, keepdims=True)
                tops.append(top)
                exps.append(jnp.exp(one - top).astype(bf16))
            o = dot(v_ref[g, keys, :], jnp.concatenate(exps, axis=1), TN)
            total_e = o[HEAD_SIZE : HEAD_SIZE + 1, :]
            o = (o[:HEAD_SIZE, :] / total_e).astype(bf16)
            lse = jnp.log(total_e)
            for i in range(group):
                h = g * group + i
                cols = slice(i * QROWS, (i + 1) * QROWS)
                lse_ref[h : h + 1, rows] = tops[i] + lse[:, cols]
                sorted_buf[h * HEAD_SIZE : (h + 1) * HEAD_SIZE, rows] = o[:, cols]
        return carry

    lax.fori_loop(0, total // QROWS, attend, 0)

    def scatter(m, carry):
        place = lax.broadcasted_iota(jnp.int32, (tok, total), 1)
        pick = (place == col_ref[pl.ds(m * tok, tok), :]).astype(f32).astype(bf16)
        out = dot(pick, sorted_buf[...], NT).astype(bf16)

        @pl.when(m < n_ctx // 2)
        def _():
            near_ref[m] = out

        @pl.when(m >= n_ctx // 2)
        def _():
            far_ref[m - n_ctx // 2] = out

        return carry

    lax.fori_loop(0, n_ctx, scatter, 0)
    keep_w.wait()


def attn_fwd(places, w_pieces, n_dp, h1, row, col, start_row, cos, sin, qh, kvh):
    n_w = len(w_pieces)
    n_ctx, tok = h1.shape[:2]
    total = n_ctx * tok
    width = w_pieces[0].shape[2]
    rows = w_pieces[0].shape[1] * (n_w // n_dp)
    shape = jax.ShapeDtypeStruct
    return pl.pallas_call(
        functools.partial(attn_fwd_kernel, n_ctx, n_w, qh, kvh),
        out_shape=(
            shape((n_ctx // 2, tok, qh * HEAD_SIZE), bf16),
            shape((n_ctx // 2, tok, qh * HEAD_SIZE), bf16),
            shape((qh, total, LANES), bf16),
            shape((kvh, total, LANES), bf16),
            shape((kvh, total, LANES), bf16),
            shape((-(-qh // 8) * 8, total), f32),
            shape((n_ctx * n_dp, rows, width), bf16),
        ),
        in_specs=[SMEM] + [ANY] * (n_w + 1) + [VMEM] * 5,
        out_specs=(VMEM,) * 6 + (ANY,),
        scratch_shapes=[
            pltpu.VMEM((n_ctx * n_dp, rows, width), bf16),
            pltpu.VMEM((n_ctx, tok, MODEL_WIDTH), bf16),
            pltpu.VMEM((total, width), bf16),
            pltpu.VMEM((qh * HEAD_SIZE, total), bf16),
            pltpu.SemaphoreType.DMA((n_ctx * n_w,)),
            pltpu.SemaphoreType.DMA((n_ctx,)),
            pltpu.SemaphoreType.DMA,
        ],
        compiler_params=params(),
        cost_estimate=cost(20e9, 20e6),
        name="attn_fwd",
    )(places, *w_pieces, h1, row, col, start_row, cos, sin)


def attn_bwd_kernel(n_ctx, qh, kvh, *refs):
    db_refs, refs = refs[:n_ctx], refs[n_ctx:]
    (wo_ref, near_ref, far_ref, q_ref, k_ref, v_ref, lse_ref), refs = refs[:7], refs[7:]
    (row_ref, col_ref, start_ref, cos_ref, sin_ref, cos_t, sin_t), refs = refs[:7], refs[7:]
    out_ref, db_buf, dat_buf, del_buf, do_buf, dq_buf, dk_buf, dv_buf, kv_buf, sem = refs
    tok = db_buf.shape[1]
    total = n_ctx * tok
    group = qh // kvh
    k_chunks = kvh * HEAD_SIZE // LANES
    n_rows = lse_ref.shape[0]
    copies = [pltpu.make_async_copy(db_refs[m], db_buf.at[m], sem.at[m]) for m in range(n_ctx)]
    for c in copies:
        c.start()
    dk_buf[...] = jnp.zeros_like(dk_buf)
    dv_buf[...] = jnp.zeros_like(dv_buf)
    for c in copies:
        c.wait()
    q_width = qh * HEAD_SIZE
    head_of = lax.broadcasted_iota(jnp.int32, (n_rows, q_width), 1) // HEAD_SIZE
    ones = (head_of == lax.broadcasted_iota(jnp.int32, (n_rows, q_width), 0)).astype(f32).astype(bf16)

    def lift(m, carry):
        rows = pl.ds(pl.multiple_of(m * tok, tok), tok)
        low = dot(db_buf[m], wo_ref[...], NT).astype(bf16)
        dat_buf[rows, :] = low
        attn = jnp.where(m < n_ctx // 2, near_ref[m % (n_ctx // 2)], far_ref[m % (n_ctx // 2)])
        prod = low.astype(f32) * attn.astype(f32)
        hi = prod.astype(bf16)
        rest = (prod - hi.astype(f32)).astype(bf16)
        delta = dot(ones, hi, NT) + dot(ones, rest, NT)
        for i, v in enumerate(three_parts(delta)):
            del_buf[i * n_rows : (i + 1) * n_rows, rows] = v
        return carry

    lax.fori_loop(0, n_ctx, lift, 0)
    delta_parts = del_buf[...].astype(bf16)

    def arrange(b, carry):
        rows = pl.ds(pl.multiple_of(b * tok, tok), tok)
        place = lax.broadcasted_iota(jnp.int32, (tok, total), 0) + b * tok
        pick = (place == row_ref[...]).astype(f32).astype(bf16)
        s = dot(pick, dat_buf[...])
        lane = lane_iota(tok)
        for h in range(qh):
            piece = s[:, (h // 2) * LANES : (h // 2 + 1) * LANES]
            if h % 2:
                piece = pltpu.roll(piece, HEAD_SIZE, 1)
            do_buf[h, rows, :] = jnp.where(lane < HEAD_SIZE, piece, 0.0).astype(bf16)
        d = dot(delta_parts, pick, NT)
        del_buf[:n_rows, rows] = d[:n_rows] + d[n_rows : 2 * n_rows] + d[2 * n_rows :]
        return carry

    lax.fori_loop(0, n_ctx, arrange, 0)
    window = min(MOST_LEN + QROWS, total)

    def attend(b, carry):
        q0 = pl.multiple_of(b * QROWS, QROWS)
        k0 = pl.multiple_of(jnp.maximum(q0 + QROWS - window, 0), QROWS)
        rows, keys = pl.ds(q0, QROWS), pl.ds(k0, window)
        kidx = lax.broadcasted_iota(jnp.int32, (window, QROWS), 0) + k0
        qidx = lax.broadcasted_iota(jnp.int32, (window, QROWS), 1) + q0
        allowed = (kidx <= qidx) & (kidx >= start_ref[:, rows])
        for g in range(kvh):
            heads = slice(g * group, (g + 1) * group)
            q = q_ref[heads, rows, :].reshape(group * QROWS, LANES)
            do = do_buf[heads, rows, :].reshape(group * QROWS, LANES)
            k, v = k_ref[g, keys, :], v_ref[g, keys, :]
            s, dp = dot(k, q, NT), dot(v, do, NT)
            probs, grads = [], []
            for i in range(group):
                h = g * group + i
                cols = slice(i * QROWS, (i + 1) * QROWS)
                p = jnp.where(allowed, jnp.exp(s[:, cols] - lse_ref[h : h + 1, rows]), 0.0)
                probs.append(p.astype(bf16))
                grads.append((p * (dp[:, cols] - del_buf[h : h + 1, rows])).astype(bf16))
            p, ds = jnp.concatenate(probs, axis=1), jnp.concatenate(grads, axis=1)
            dv_buf[g, keys, :] += dot(p, do)
            dk_buf[g, keys, :] += dot(ds, q)
            dq = dot(k, ds, TN)
            for i in range(group):
                h = g * group + i
                turned = dq[:HEAD_SIZE, i * QROWS : (i + 1) * QROWS] * HEAD_SIZE**-0.5
                half = HEAD_SIZE // 2
                low, high = turned[:half], turned[half:]
                cos, sin = cos_t[:, rows], sin_t[:, rows]
                turned = jnp.concatenate([low * cos + high * sin, high * cos - low * sin], axis=0)
                dq_buf[h * HEAD_SIZE : (h + 1) * HEAD_SIZE, rows] = turned.astype(bf16)
        return carry

    lax.fori_loop(0, total // QROWS, attend, 0)

    def turn_back(b, carry):
        rows = pl.ds(b * tok, tok)
        cos, sin = cos_ref[rows, :], sin_ref[rows, :]
        lane = lane_iota(tok)
        heads = [dk_buf[h, rows, :] for h in range(kvh)] + [dv_buf[h, rows, :] for h in range(kvh)]
        for j in range(2 * k_chunks):
            pair = jnp.where(lane < HEAD_SIZE, heads[2 * j], pltpu.roll(heads[2 * j + 1], HEAD_SIZE, 1))
            if j < k_chunks:
                pair = pair * cos - half_swap(pair) * sin
            kv_buf[rows, j * LANES : (j + 1) * LANES] = pair.astype(bf16)
        return carry

    lax.fori_loop(0, n_ctx, turn_back, 0)

    def scatter(m, carry):
        place = lax.broadcasted_iota(jnp.int32, (tok, total), 1)
        pick = (place == col_ref[pl.ds(m * tok, tok), :]).astype(f32).astype(bf16)
        out_ref[m, :, :q_width] = dot(pick, dq_buf[...], NT).astype(bf16)
        out_ref[m, :, q_width:] = dot(pick, kv_buf[...]).astype(bf16)
        return carry

    lax.fori_loop(0, n_ctx, scatter, 0)


def attn_bwd(db_pieces, wo, near, far, q, k, v, lse, row, col, start_row, tables, qh, kvh):
    n_ctx = len(db_pieces)
    tok = db_pieces[0].shape[0]
    total = n_ctx * tok
    width = (qh + 2 * kvh) * HEAD_SIZE
    return pl.pallas_call(
        functools.partial(attn_bwd_kernel, n_ctx, qh, kvh),
        out_shape=jax.ShapeDtypeStruct((n_ctx, tok, width), bf16),
        in_specs=[ANY] * n_ctx + [VMEM] * 14,
        out_specs=VMEM,
        scratch_shapes=[
            pltpu.VMEM((n_ctx, tok, MODEL_WIDTH), bf16),
            pltpu.VMEM((total, qh * HEAD_SIZE), bf16),
            pltpu.VMEM((3 * lse.shape[0], total), f32),
            pltpu.VMEM((qh, total, LANES), bf16),
            pltpu.VMEM((qh * HEAD_SIZE, total), bf16),
            pltpu.VMEM((kvh, total, LANES), f32),
            pltpu.VMEM((kvh, total, LANES), f32),
            pltpu.VMEM((total, 2 * kvh * HEAD_SIZE), bf16),
            pltpu.SemaphoreType.DMA((n_ctx,)),
        ],
        compiler_params=params(),
        cost_estimate=cost(10e9, 20e6),
        name="attn_bwd",
    )(*db_pieces, wo, near, far, q, k, v, lse, row, col, start_row, *tables)


def pick_rows(e, cap, routes):
    tok = routes.shape[1]
    before = lax.broadcasted_iota(jnp.int32, (tok, tok), 0) < lax.broadcasted_iota(
        jnp.int32, (tok, tok), 1
    )
    names = lax.broadcasted_iota(jnp.int32, (LANES, tok), 0)
    slots = lax.broadcasted_iota(jnp.int32, (cap, tok), 0).astype(f32)
    hit = jnp.zeros((1, tok), f32)
    named = jnp.zeros((LANES, tok), f32)
    for j in range(routes.shape[0]):
        hit = hit + jnp.where(routes[j : j + 1] == e, 1.0, 0.0)
        named = named + jnp.where(names == routes[j : j + 1], 1.0, 0.0)
    hits = jnp.broadcast_to(hit, (8, tok)).astype(bf16)
    slot = dot(hits, before.astype(f32).astype(bf16))[0:1]
    pick = jnp.where((slots == slot) & (hit > 0.5), 1.0, 0.0).astype(bf16)
    return pick, dot(pick, named.astype(bf16), NT)


TILE = 512


def expert_kernel(by_hand, cap, who_ref, *refs):
    n_in = len(PIECES) if by_hand else 1
    h_refs, dy_refs, refs = refs[:n_in], refs[n_in : 2 * n_in], refs[2 * n_in :]
    (routes_ref, wc_ref, wd_ref), refs = refs[:3], refs[3:]
    n_rows = 4 if by_hand else 2
    row_refs, refs = refs[:n_rows], refs[n_rows:]
    (xs_ref, deout_ref, act_ref, dgu_ref, coef_ref), refs = refs[:5], refs[5:]
    dcat, drow, yrow, refs = *refs[:3], refs[3:]
    step = pl.program_id(0)
    core = who_ref[1]
    e = who_ref[0]
    ff = wd_ref.shape[0]
    if by_hand:
        h_buf, dy_buf, sem = refs

        def copies(chip):
            got = []
            for n, (j, sib) in enumerate(PIECES):
                if j != chip:
                    continue
                col = pl.multiple_of((core + sib) % 2 * HALF, HALF)
                for i in range(2):
                    spot = (2 * j + (i ^ sib), slice(None), pl.ds(col, HALF))
                    for k, (src, buf) in enumerate(((h_refs, h_buf), (dy_refs, dy_buf))):
                        got.append(
                            pltpu.make_async_copy(src[n].at[i], buf.at[spot], sem.at[k, n, i])
                        )
            return got

        @pl.when(step == 0)
        def _():
            for j in range(4):
                for c in copies(j):
                    c.start()

        for j in range(4):

            @pl.when(step == j)
            def _():
                for c in copies(j):
                    c.wait()

        def load(buf, i, cols):
            return buf[2 * step + i, :, cols]

    else:
        h_buf, dy_buf = h_refs[0], dy_refs[0]

        def load(buf, i, cols):
            return buf[i, :, cols]

    picks, masks = [], []
    for i in range(2):
        pick, mask = pick_rows(e, cap, routes_ref[2 * step + i])
        picks.append(pick)
        masks.append(mask)
    mask = jnp.concatenate(masks, axis=0) > 0.5
    tiles = [slice(t, t + TILE) for t in range(0, MODEL_WIDTH, TILE)]
    for cols in tiles:
        for i in range(2):
            rows = slice(i * cap, (i + 1) * cap)
            xs_ref[rows, cols] = dot(picks[i], load(h_buf, i, cols)).astype(bf16)
            deout_ref[rows, cols] = dot(picks[i], load(dy_buf, i, cols)).astype(bf16)
    xs = xs_ref[...]
    logits = jnp.where(mask, dot(xs, wc_ref[:, 2 * ff :]), MASKED)
    ex = jnp.where(mask, jnp.exp(logits - jnp.max(logits, axis=1, keepdims=True)), 0.0)
    lane = lax.broadcasted_iota(jnp.int32, ex.shape, 1)
    own = lane == e
    denom = jnp.sum(ex, axis=1, keepdims=True)
    probs = ex / jnp.where(denom > 0.0, denom, 1.0)
    gp = jnp.sum(jnp.where(own, probs, 0.0), axis=1, keepdims=True)
    gate = dot(xs, wc_ref[:, :ff])
    up = dot(xs, wc_ref[:, ff : 2 * ff])
    sig = jax.nn.sigmoid(gate)
    silu = gate * sig
    act = (silu * up).astype(bf16)
    act_ref[...] = act
    dgp = jnp.zeros((2 * cap, LANES), f32)
    for cols in tiles:
        eout = dot(act, wd_ref[:, cols]).astype(bf16).astype(f32)
        dys = deout_ref[:, cols].astype(f32)
        both = dys * eout
        for c in range(0, TILE, LANES):
            dgp = dgp + both[:, c : c + LANES]
        deout_ref[:, cols] = (gp * dys).astype(bf16)
        yrow[:, cols] = (gp * eout).astype(bf16)
    dgp = jnp.sum(dgp, axis=1, keepdims=True)
    coef = gp * dgp * (jnp.where(own, 1.0, 0.0) - probs)
    hi = coef.astype(bf16).astype(f32)
    low = pltpu.roll(coef - hi, LANES // 2, 1)
    coef = jnp.where(lane < LANES // 2, hi, low).astype(bf16)
    coef_ref[...] = coef
    dact = dot(deout_ref[...], wd_ref[...], NT)
    dgate = (dact * up * sig * (1.0 + gate * (1.0 - sig))).astype(bf16)
    dup = (dact * silu).astype(bf16)
    dgu_ref[:, :ff] = dgate
    dgu_ref[:, ff:] = dup
    dcat[:, :ff] = dgate
    dcat[:, ff : 2 * ff] = dup
    dcat[:, 2 * ff :] = coef
    for cols in tiles:
        drow[:, cols] = dot(dcat[...], wc_ref[cols, :], NT).astype(bf16)
    for k, buf in enumerate((drow, yrow)):
        for i in range(2):
            rows = slice(i * cap, (i + 1) * cap)
            if by_hand:
                mine = pl.multiple_of(core * HALF, HALF)
                other = pl.multiple_of((1 - core) * HALF, HALF)
                for ref, at, col in ((row_refs[2 * k], i, mine), (row_refs[2 * k + 1], 1 - i, other)):
                    ref[0, at] = dot(picks[i], buf[rows, pl.ds(col, HALF)], TN).astype(bf16)
            else:
                row_refs[k][0, i] = dot(picks[i], buf[rows, :], TN).astype(bf16)


def run_experts(who, by_hand, h_list, dy_list, routes_t, wc, wd, cap, tok):
    n_blocks = routes_t.shape[0]
    steps = n_blocks // 2
    ff = wd.shape[0]
    rows = 2 * cap
    shape = jax.ShapeDtypeStruct
    out_w = HALF if by_hand else MODEL_WIDTH
    block = pl.BlockSpec((1, 2, tok, out_w), lambda i, *_: (i, 0, 0, 0))
    other = pl.BlockSpec((1, 2, tok, out_w), lambda i, *_: (i // 2 + i % 2 * 2, 0, 0, 0))
    wide = pl.BlockSpec((rows, MODEL_WIDTH), lambda i, *_: (i, 0))
    thin = pl.BlockSpec((rows, ff), lambda i, *_: (i, 0))
    twin = pl.BlockSpec((rows, 2 * ff), lambda i, *_: (i, 0))
    edge = pl.BlockSpec((rows, LANES), lambda i, *_: (i, 0))
    whole = pl.BlockSpec((2, tok, MODEL_WIDTH), lambda i, *_: (i, 0, 0))
    n_in = len(h_list)
    scratch = [
        pltpu.VMEM((rows, wc.shape[1]), bf16),
        pltpu.VMEM((rows, MODEL_WIDTH), bf16),
        pltpu.VMEM((rows, MODEL_WIDTH), bf16),
    ]
    if by_hand:
        scratch += [
            pltpu.VMEM((n_blocks, tok, MODEL_WIDTH), bf16),
            pltpu.VMEM((n_blocks, tok, MODEL_WIDTH), bf16),
            pltpu.SemaphoreType.DMA((2, n_in, 2)),
        ]
    row_specs = [block, other] * 2 if by_hand else [block] * 2
    grid_spec = pltpu.PrefetchScalarGridSpec(
        num_scalar_prefetch=1,
        grid=(steps,),
        in_specs=[ANY if by_hand else whole] * (2 * n_in) + [VMEM] * 3,
        out_specs=row_specs + [wide] * 2 + [thin, twin, edge],
        scratch_shapes=scratch,
    )
    return pl.pallas_call(
        functools.partial(expert_kernel, by_hand, cap),
        out_shape=[shape((steps, 2, tok, out_w), bf16)] * len(row_specs)
        + [shape((steps * rows, MODEL_WIDTH), bf16)] * 2
        + [shape((steps * rows, w), bf16) for w in (ff, 2 * ff, LANES)],
        grid_spec=grid_spec,
        compiler_params=params(60),
        cost_estimate=cost(30e9, 30e6),
        name="experts",
    )(who, *h_list, *dy_list, routes_t, wc, wd)


def flip(v, axis, bit):
    n = lax.axis_size(axis)
    return lax.ppermute(v, axis, [(i, i ^ bit) for i in range(n)])


def step_up(v, axis):
    n = lax.axis_size(axis)
    return lax.ppermute(v, axis, [(i, (i + 1) % n) for i in range(n)])


def ctx_gather(v):
    n = lax.axis_size("context")
    pieces = {0: v}
    bit = n // 2
    while bit:
        for m in list(pieces):
            pieces[m | bit] = flip(pieces[m], "context", bit)
        bit //= 2
    return [pieces[m] for m in range(n)]


def add_low(a, b):
    return (a.astype(f32) + b.astype(f32)).astype(bf16)


def ring(v, axis, deps=()):
    pieces = [v]
    for i in range(lax.axis_size(axis) - 1):
        sent = after(pieces[-1], *deps[i]) if i < len(deps) else pieces[-1]
        pieces.append(step_up(sent, axis))
    return pieces


def send_all(v, axis):
    n = lax.axis_size(axis)
    return [v] + [
        lax.ppermute(v, axis, [(i, (i + k) % n) for i in range(n)]) for k in range(1, n)
    ]


def ring_sum(chunk, axis, deps=()):
    n, d = lax.axis_size(axis), lax.axis_index(axis)
    part = chunk(lax.rem(d + n - 1, n)).astype(bf16)
    for hop in range(n - 1):
        got = step_up(part, axis)
        own = chunk(lax.rem(d + 2 * n - 2 - hop, n))
        if hop < len(deps):
            own = after(own, *deps[hop])
        part = (got.astype(f32) + own.astype(f32)).astype(bf16)
    return part


def direct_sum(chunk, axis, *deps):
    n, d = lax.axis_size(axis), lax.axis_index(axis)
    total = chunk(d).astype(f32)
    if deps:
        total = after(total, *deps)
    for k in range(1, n):
        sent = chunk(lax.rem(d + k, n)).astype(bf16)
        got = lax.ppermute(sent, axis, [(i, (i + k) % n) for i in range(n)])
        total = total + got.astype(f32)
    return total


def after(v, *deps):
    return lax.optimization_barrier((v, *deps))[0]


HALF = MODEL_WIDTH // 2
PLANE = ("expert", "context")
PIECES = ((0, 0), (1, 0), (2, 0), (3, 0), (0, 1), (2, 1), (1, 1), (3, 1))


def small_plane():
    return lax.axis_size("expert") == 2 and lax.axis_size("context") == 4


def hop_plane(v, second):
    pairs = []
    for i in range(8):
        along_context = (i % 2 == 0) != second
        pairs.append((i, i ^ 2 if along_context else i ^ 4))
    return lax.ppermute(v, PLANE, pairs)


def halves(v, core):
    left, right = v[..., :HALF], v[..., HALF:]
    return jnp.where(core == 0, left, right), jnp.where(core == 0, right, left)


def sync(*values):
    return lax.optimization_barrier(values)


def plane_near(v):
    core = lax.axis_index("context") % 2
    mine, given = halves(v, core)
    return jnp.stack([mine, flip(given, "context", 1)])


def plane_far(u0, u1):
    return hop_plane(u0, True), hop_plane(u1, True)


def plane_share(own):
    return list(own) + [flip(u, "context", 1) for u in own]


def plane_gather(v):
    if not small_plane():
        return [lax.all_gather(v, PLANE, axis=0, tiled=False)]
    u0 = plane_near(v)
    u1 = hop_plane(u0, False)
    return plane_share((u0, u1) + plane_far(u0, u1))


class PlaneSum:
    def __init__(self, rows):
        self.small = small_plane()
        self.rows = rows
        if self.small:
            self.keep, give = rows
            self.got = flip(give, "context", 1)
            self.far = add_low(self.keep[2:], self.got[2:])

    def first(self):
        if self.small:
            self.got2 = hop_plane(self.far, True)

    def second(self):
        if self.small:
            near = self.keep[:2].astype(f32) + self.got[:2].astype(f32) + self.got2.astype(f32)
            self.near = near[0]
            self.got1 = hop_plane(near[1].astype(bf16), False)

    def finish(self):
        if not self.small:
            (both,) = self.rows
            flat = both.reshape(-1, both.shape[-1])
            return lax.psum_scatter(flat, PLANE, scatter_dimension=0, tiled=True).astype(f32)
        core = lax.axis_index("context") % 2
        whole = self.near + self.got1.astype(f32)
        other = flip(whole[1].astype(bf16), "context", 1).astype(f32)
        left = jnp.where(core == 0, whole[0], other)
        right = jnp.where(core == 0, other, whole[0])
        return jnp.concatenate([left, right], axis=1)


def ctx_sum(p):
    far = add_low(p[2], flip(p[3], "context", 1))
    own = p[0].astype(f32) + flip(p[1], "context", 1).astype(f32)
    return own + flip(far, "context", 2).astype(f32)


def put_in_order(places, pieces, name):
    n = len(pieces)
    rows, width = pieces[0].shape

    def kernel(place_ref, *refs):
        out_ref, sem = refs[n:]
        copies = [
            pltpu.make_async_copy(refs[k], out_ref.at[place_ref[k]], sem.at[k]) for k in range(n)
        ]
        for c in copies:
            c.start()
        for c in copies:
            c.wait()

    return pl.pallas_call(
        kernel,
        out_shape=jax.ShapeDtypeStruct((n, rows, width), pieces[0].dtype),
        in_specs=[SMEM] + [ANY] * n,
        out_specs=VMEM,
        scratch_shapes=[pltpu.SemaphoreType.DMA((n,))],
        cost_estimate=cost(0, 2 * n * rows * width * 2),
        name=name,
    )(places, *pieces)


def columns_of(spots, near, far, weights, qw, kw):
    n_ctx, part, width = near.shape

    def kernel(spot_ref, near_ref, far_ref, *refs):
        w_refs, outs, gain_ref = refs[:3], refs[3:6], refs[6]
        for k, ref in enumerate((near_ref, far_ref)):
            row = pl.multiple_of(spot_ref[n_ctx + k] * part, 16)
            for m in range(n_ctx):
                v = ref[m].astype(f32)
                lo = 0
                for out, w in zip(outs, (qw, kw, kw)):
                    col = pl.multiple_of(spot_ref[m] * w, LANES)
                    out[pl.ds(row, part), pl.ds(col, w)] = v[:, lo : lo + w]
                    lo += w
        total = jnp.zeros((2 * part, LANES), f32)
        for out, w_ref in zip(outs, w_refs):
            both = out[...] * w_ref[...].astype(f32)
            for c in range(0, both.shape[1], LANES):
                total = total + both[:, c : c + LANES]
        gain_ref[...] = jnp.sum(total, axis=1, keepdims=True)

    shape = jax.ShapeDtypeStruct
    return pl.pallas_call(
        kernel,
        out_shape=tuple(shape((2 * part, n_ctx * w), f32) for w in (qw, kw, kw))
        + (shape((2 * part, 1), f32),),
        in_specs=[SMEM] + [VMEM] * 5,
        out_specs=(VMEM,) * 4,
        cost_estimate=cost(0, 2e6),
        name="columns_of",
    )(spots, near, far, *weights)


def position_tables(lengths_row, row, freq):
    total = row.shape[1]
    half = HEAD_SIZE // 2

    def kernel(len_ref, row_ref, freq_ref, *outs):
        cos_d, sin_d, cos_s, sin_s, cos_t, sin_t, start_ref = outs

        def start_of(place):
            end, start = 0, jnp.zeros_like(place)
            for j in range(lengths_row.shape[0]):
                end = end + len_ref[j]
                start = start + jnp.where(place >= end, len_ref[j], 0)
            return start

        dealt = row_ref[...]
        placed = lax.broadcasted_iota(jnp.int32, (1, total), 1)
        start_ref[...] = start_of(placed)
        for place, cos_ref, sin_ref in ((dealt, cos_d, sin_d), (placed, cos_s, sin_s)):
            angle = freq_ref[...] * (place - start_of(place)).astype(f32)
            cos, sin = jnp.cos(angle), jnp.sin(angle)
            cos_ref[...] = jnp.concatenate([cos] * 4, axis=0).T
            sin_ref[...] = jnp.concatenate([-sin, sin] * 2, axis=0).T
        cos_t[...] = cos
        sin_t[...] = sin

    shape = jax.ShapeDtypeStruct
    wide, thin = shape((total, LANES), f32), shape((half, total), f32)
    return pl.pallas_call(
        kernel,
        out_shape=(wide, wide, wide, wide, thin, thin, shape((1, total), jnp.int32)),
        in_specs=[SMEM, VMEM, VMEM],
        out_specs=(VMEM,) * 7,
        compiler_params=params(),
        cost_estimate=cost(0, 0),
        name="position_tables",
    )(lengths_row, row, freq)


def widen(twin, down):
    rows, ff = down.shape

    def kernel(twin_ref, down_ref, gate_out, up_out, down_out):
        gate_out[...] = twin_ref[:, :ff].astype(f32)
        up_out[...] = twin_ref[:, ff:].astype(f32)
        down_out[...] = down_ref[...].astype(f32).T

    shape = jax.ShapeDtypeStruct
    return pl.pallas_call(
        kernel,
        out_shape=(shape((rows, ff), f32), shape((rows, ff), f32), shape((ff, rows), f32)),
        in_specs=[VMEM] * 2,
        out_specs=(VMEM,) * 3,
        compiler_params=params(),
        cost_estimate=cost(0, 0),
        name="widen",
    )(twin, down)


def finish_input(d_middle, near, far, x, gain):
    tok = x.shape[0]

    def kernel(dm_ref, near_ref, far_ref, x_ref, gain_ref, out_ref):
        v = x_ref[...].astype(f32)
        dh = near_ref[...] + far_ref[...].astype(f32)
        r = lax.rsqrt(jnp.mean(v * v, axis=-1, keepdims=True) + NORM_EPS)
        scaled = gain_ref[...] * dh
        inner = jnp.sum(scaled * v, axis=-1, keepdims=True)
        dv = r * scaled - v * (r * r * r) * (inner / MODEL_WIDTH)
        out_ref[...] = (dm_ref[...] + dv).astype(bf16)

    step = 64
    rows = pl.BlockSpec((step, MODEL_WIDTH), lambda i: (i, 0))
    return pl.pallas_call(
        kernel,
        out_shape=jax.ShapeDtypeStruct((tok, MODEL_WIDTH), bf16),
        grid=(tok // step,),
        in_specs=[rows] * 4 + [pl.BlockSpec((1, MODEL_WIDTH), lambda i: (0, 0))],
        out_specs=rows,
        compiler_params=params(),
        cost_estimate=cost(0, 0),
        name="finish_input",
    )(d_middle, near, far, x, gain)


def rms_back(dh, v, r, gain):
    inner = jnp.sum(gain * dh * v, axis=-1, keepdims=True)
    dv = r * gain * dh - v * (r * r * r) * (inner / MODEL_WIDTH)
    return dv, jnp.sum(dh * v * r, axis=0)


def body(
    hidden, cotangent, token_order, lengths, routes, attn_gain, w_query, key_weight,
    value_weight, w_out, ffn_gain, w_router, w_gate, w_up, w_down,
):
    tok, top = hidden.shape[1], routes.shape[2]
    n_exp, n_ctx, n_dp = (lax.axis_size(a) for a in ("expert", "context", "dp"))
    experts = n_exp * n_ctx
    cap = -(-(9 * tok * top // (8 * experts)) // 16) * 16
    qh, kvh = QUERY_HEADS // n_ctx, KEY_VALUE_HEADS // n_ctx
    qw, kw = qh * HEAD_SIZE, kvh * HEAD_SIZE
    rows = w_query.shape[0]
    ex, cx, dx = (lax.axis_index(a) for a in ("expert", "context", "dp"))
    my_expert = ex * n_ctx + cx
    total = n_ctx * tok

    def for_context(c):
        return jnp.concatenate(
            [
                lax.dynamic_slice_in_dim(w_query, c * qw, qw, 1),
                lax.dynamic_slice_in_dim(key_weight, c * kw, kw, 1),
                lax.dynamic_slice_in_dim(value_weight, c * kw, kw, 1),
            ],
            axis=1,
        )

    params_t = jnp.concatenate([attn_gain[None], ffn_gain[None], w_router.T], axis=0)
    p_rows = params_t.shape[0]
    params_t = jnp.pad(params_t, ((0, 0), (0, tok - rows)))
    routes_t = routes[0].T.astype(bf16)
    k_of = jnp.arange(n_dp, dtype=jnp.int32)
    d_of = lax.rem(dx - k_of + n_dp, n_dp)
    c_of = cx ^ jnp.arange(n_ctx, dtype=jnp.int32)
    places = (c_of[None, :] * n_dp + d_of[:, None]).reshape(-1).astype(jnp.int32)

    def own_params(stack):
        stack = stack.reshape(n_dp * n_ctx, p_rows, -1)[:, :, :rows]
        at = d_of[None, :] * n_ctx + (cx ^ jnp.arange(n_ctx, dtype=jnp.int32))[:, None]
        flat = stack[at.reshape(-1)].transpose(1, 0, 2).reshape(p_rows, MODEL_WIDTH)
        router = jnp.pad(flat[2:].T, ((0, 0), (0, LANES // 2 - experts)))
        return flat[0:1].astype(f32), flat[1:2].astype(f32), router

    def own_routes(stack):
        return stack.reshape(experts, top, tok).astype(jnp.int32)

    def positions(order_row, lengths_row):
        order_rel = order_row.reshape(n_ctx, tok)[c_of].reshape(-1)
        half = HEAD_SIZE // 2
        freq = ROPE_BASE ** (-(jnp.arange(half, dtype=f32) * 2.0 / HEAD_SIZE))
        row, col = order_rel[None, :], order_rel[:, None]
        return (row, col, *position_tables(lengths_row, row, freq[:, None]))

    order_row, ends_in = token_order[0], lengths[0]

    def gather_plane(v):
        return lax.all_gather(v, PLANE, axis=0, tiled=False)

    def gather_out(v):
        return lax.all_gather(v, "dp", axis=0, tiled=True)

    x_own, dy_own = hidden[0], cotangent[0]
    if small_plane():
        part = rows // 2

        def half_for(c):
            return lax.dynamic_slice_in_dim(for_context(c), ex * part, part, 0)

        got = [half_for(cx)] + [flip(half_for(cx ^ m), "context", m) for m in range(1, n_ctx)]
        shards = send_all(params_t, "dp")
        dy0 = plane_near(dy_own)
        w0, dy0, *shards = sync(jnp.stack(got), dy0, *shards)
        note = jnp.concatenate([routes_t] + shards, axis=0)
        mine, theirs = [w0], []
        for k in range(n_dp - 1):
            nxt, other = step_up(mine[-1], "dp"), flip(mine[-1], "expert", 1)
            if k == 0:
                note2 = jnp.stack([note, flip(note, "context", 2)])
                x2 = flip(after(x_own, note2), "context", 2)
                nxt, other, note2, order_row, ends_in = sync(nxt, other, note2, order_row, ends_in)
            elif k == 1:
                dy1 = hop_plane(after(dy0, mine[-1]), False)
                near = flip(note2, "context", 1)
                note4 = jnp.stack([note2[0], near[0], note2[1], near[1]])
                nxt, other, x2, note4 = sync(nxt, other, x2, note4)
                x1, x3 = flip(x_own, "context", 1), flip(x2, "context", 1)
                where = positions(order_row, ends_in)
                shards = note4[:, top:].reshape(n_ctx, n_dp, p_rows, tok).swapaxes(0, 1)
                gain_a, gain_b, router = own_params(shards)
            elif k == 2:
                routes_far = flip(note4[:, :top], "expert", 1)
                nxt, other, gain_a, dy1 = sync(nxt, other, gain_a, dy1)
                h1 = norm_rows([x_own, x1, x2, x3], gain_a)
            mine.append(nxt)
            theirs.append(other)
        theirs.append(flip(mine[-1], "expert", 1))
        c = lax.rem(cx, 2)
        routes_rel = jnp.stack([note4[:, :top], routes_far]).reshape(8, top, tok)
        even = jnp.array([0, 1, 2, 3, 4, 5, 6, 7], jnp.int32)
        odd = jnp.array([0, 1, 4, 5, 2, 3, 6, 7], jnp.int32)
        routes_all = own_routes(routes_rel[jnp.where(c == 0, even, odd)])
        theirs[-1], router, h1, routes_all, dy1 = sync(theirs[-1], router, h1, routes_all, dy1)
        wo = gather_out(after(w_out, mine[-1]))
        dy2, dy3 = plane_far(after(dy0, theirs[-1]), dy1)
        w_pieces = mine + theirs
        spots = jnp.concatenate(
            [places, places, jnp.broadcast_to(ex, (n_dp,)), jnp.broadcast_to(1 - ex, (n_dp,))]
        ).astype(jnp.int32)
    else:
        got = [for_context(cx)]
        for m in range(1, n_ctx):
            got.append(flip(for_context(cx ^ m), "context", m))
        w_pieces = ring(jnp.stack(got), "dp")
        shards = jnp.stack(send_all(jnp.stack(ctx_gather(params_t)), "dp"))
        gain_a, gain_b, router = own_params(shards)
        routes_all = own_routes(lax.all_gather(routes_t, PLANE, axis=0, tiled=False))
        h1 = norm_rows(ctx_gather(x_own), gain_a)
        dy_all, wo = gather_plane(cotangent[0]), gather_out(w_out)
        spots = jnp.concatenate([places, jnp.zeros((n_dp,), jnp.int32)])
        where = positions(order_row, ends_in)
    row, col, cos_d, sin_d, *placed, start_row = where
    near, far, q, k, v, lse, wqkv = attn_fwd(
        spots, w_pieces, n_dp, h1, row, col, start_row, cos_d, sin_d, qh, kvh
    )
    if small_plane():
        near, wo, dy2, dy3 = sync(near, wo, dy2, dy3)
        dy_list = plane_share((dy0, dy1, dy2, dy3))
    else:
        dy_list = [dy_all]
    partial_far = dot(far.reshape(-1, qw), wo).astype(bf16).reshape(-1, tok, MODEL_WIDTH)
    partial_near = dot(near.reshape(-1, qw), wo).astype(bf16).reshape(-1, tok, MODEL_WIDTH)
    late_gate = after(w_gate[0], partial_near)
    w_cat = jnp.concatenate([late_gate, w_up[0], router, router], axis=1)
    branch = ctx_sum([partial_near[0], partial_near[1], partial_far[0], partial_far[1]])
    branch, w_cat, *dy_list = sync(branch, w_cat, *dy_list)
    x_own = x_own.astype(f32)
    middle = x_own + branch
    r_b = lax.rsqrt(jnp.mean(middle * middle, axis=-1, keepdims=True) + NORM_EPS)
    h2 = (middle * r_b * gain_b).astype(bf16)
    h_list = plane_gather(h2)

    by_hand = small_plane()
    who = jnp.stack([my_expert, cx % 2]).astype(jnp.int32)
    out = run_experts(
        who, by_hand, h_list, dy_list, routes_all, w_cat, w_down[0], cap, tok
    )
    n_rows = 2 if by_hand else 1
    d_rows, y_rows, (xs, deout, act, dgu, coef) = (
        out[:n_rows], out[n_rows : 2 * n_rows], out[2 * n_rows :],
    )
    small = small_plane()
    d_sum = PlaneSum(d_rows)
    if small:
        y_rows = (y_rows[0], after(y_rows[1], d_sum.far))
    y_sum = PlaneSum(y_rows)
    xs_late, deout_late = (after(xs, d_sum.far), after(deout, d_sum.far)) if small else (xs, deout)
    g_twin = dot(xs_late, dgu, TN).astype(bf16)
    g_down = dot(deout_late, act, TN).astype(bf16)
    g_router = dot(xs_late, coef, TN)
    g_router = g_router[:, :experts] + g_router[:, LANES // 2 : LANES // 2 + experts]

    def over_dp(g, dim):
        return lax.psum_scatter(g, "dp", scatter_dimension=dim, tiled=True)

    if small:
        d_sum.first()
        sum_twin, sum_down = over_dp(g_twin, 0), over_dp(g_down, 0)
        d_sum.got2, y_sum.far, g_twin, g_down, g_router = sync(
            d_sum.got2, y_sum.far, g_twin, g_down, g_router
        )
        d_sum.second()
    else:
        sum_twin, sum_down = over_dp(g_twin, 0), over_dp(g_down, 0)
    dh2 = d_sum.finish()
    dy = dy_own.astype(f32)
    d_norm, g_gain_b = rms_back(dh2, middle, r_b, gain_b)
    d_middle = dy + d_norm
    tiny = jnp.concatenate([g_gain_b[None], g_router.T], axis=0)
    tiny = tiny.reshape(-1, n_ctx * n_dp, rows).transpose(1, 0, 2)
    if small:
        cy, cc = cx // 2, lax.rem(cx, 2)
        tiny = tiny.reshape(2, 2, n_dp, -1, rows)
        whole = lax.dynamic_index_in_dim(tiny, dx, 2, keepdims=False)
        for up in range(1, n_dp):
            sent = lax.dynamic_index_in_dim(tiny, lax.rem(dx + up, n_dp), 2, keepdims=False)
            pairs = [(i, (i + up) % n_dp) for i in range(n_dp)]
            whole = whole + lax.ppermute(sent, "dp", pairs)
        tiny = whole
        b0 = d_middle.astype(bf16)
        b2, b1 = flip(b0, "context", 2), flip(b0, "context", 1)
        b2, b1, tiny = sync(b2, b1, tiny)
        db_pieces = [b0, b1, b2, flip(b2, "context", 1)]
        y_sum.far = after(y_sum.far, b2)
        y_sum.first()
    else:
        db_pieces = ctx_gather(d_middle.astype(bf16))
    db_last = db_pieces[-1]
    if small:
        tiny_far = flip(tiny, "expert", 1)
    dqkv = attn_bwd(
        db_pieces[:-1] + [db_last], wo, near, far, q, k, v, lse, row, col, start_row, placed, qh, kvh
    )
    if small:
        dqkv, sum_twin, tiny_far = sync(dqkv, sum_twin, tiny_far)
        tiny = tiny + tiny_far
        give = lax.dynamic_index_in_dim(tiny, 1 - cc, 1, keepdims=False)
        tiny_far = flip(give, "context", 1)
    dqkv_flat = dqkv.reshape(total, -1)
    h1_flat = h1.reshape(total, MODEL_WIDTH)
    g_qkv = dot(h1_flat, dqkv_flat, TN).astype(bf16)
    w_flat = wqkv.reshape(MODEL_WIDTH, -1)
    if small:
        part = rows // 2
        g5 = g_qkv.reshape(n_ctx * n_dp, 2, part, -1)
        theirs = lax.dynamic_index_in_dim(g5, 1 - ex, 1, keepdims=False)
        mine = lax.dynamic_index_in_dim(g5, ex, 1, keepdims=False)
        got = flip(theirs, "expert", 1)
        dh1_in = after(dqkv_flat, theirs, mine)
    else:
        dh1_in = dqkv_flat
    dh1_part = dot(dh1_in, w_flat, NT).astype(bf16)
    attn = jnp.concatenate([near, after(far, dh1_part)], axis=0).reshape(total, qw)
    g_out = dot(attn, jnp.concatenate(db_pieces, axis=0), TN).astype(bf16)
    g_out = after(g_out, sum_down)
    dh1_part = dh1_part.reshape(n_ctx, tok, MODEL_WIDTH)
    r_a = lax.rsqrt(jnp.mean(x_own * x_own, axis=-1, keepdims=True) + NORM_EPS)

    width = qw + 2 * kw
    s_out = lax.psum_scatter(g_out, "dp", scatter_dimension=0, tiled=True)

    def exchange(s):
        back = [lax.dynamic_index_in_dim(s, cx, 0, keepdims=False)]
        for m in range(1, n_ctx):
            one = lax.dynamic_index_in_dim(s, cx ^ m, 0, keepdims=False)
            back.append(flip(one, "context", m))
        return jnp.stack(back)


    def finish_rows(dh1):
        return (d_middle + rms_back(dh1, x_own, r_a, gain_a)[0]).astype(bf16)

    if small:
        h3 = flip(dh1_part[3], "context", 1)
        hop = flip(add_low(dh1_part[2], h3), "context", 2)
        h1p = flip(dh1_part[1], "context", 1)
        dh1 = dh1_part[0].astype(f32) + h1p.astype(f32)
        y_sum.got2 = after(y_sum.got2, dqkv)
        both_g = add_low(after(mine, dh1_part), got).reshape(n_ctx, n_dp, part, width)
        tiny = lax.dynamic_index_in_dim(tiny, cc, 1, keepdims=False) + after(tiny_far, both_g)
        give = lax.dynamic_index_in_dim(tiny, 1 - cy, 0, keepdims=False)
        tiny_far = flip(give, "context", 2)
        sum_gate, sum_up, sum_down = widen(after(sum_twin, both_g), sum_down)
        grad_input = finish_input(d_middle, after(dh1, both_g), hop, hidden[0], gain_a)
        y_sum.got2 = after(y_sum.got2, both_g)
        y_sum.second()
        s_qkv = direct_sum(
            lambda d: lax.dynamic_index_in_dim(both_g, d, 1, keepdims=False),
            "dp",
        )
        out_low = s_out.astype(bf16)
        out_far = flip(out_low, "expert", 1)
        s_qkv, out_far, tiny_far = sync(s_qkv, out_far, tiny_far)
        tiny = lax.dynamic_index_in_dim(tiny, cy, 0, keepdims=False) + tiny_far
        s_out = out_low.astype(f32) + out_far.astype(f32)
        near = exchange(s_qkv.astype(bf16))
        near, y_sum.got1 = sync(near, y_sum.got1, hop)[:2]
        output = (middle + y_sum.finish()).astype(bf16)
        far = flip(near, "expert", 1)
        spots = jnp.concatenate([c_of, ex[None], 1 - ex[None]]).astype(jnp.int32)
        weights = (w_query, key_weight, value_weight)
        sum_q, sum_k, sum_v, g_gain_a = columns_of(spots, near, far, weights, qw, kw)
        g_gain_a = g_gain_a[:, 0] / attn_gain.astype(f32)
    else:
        dh1 = ctx_sum([dh1_part[m] for m in range(n_ctx)])
        sum_gate, sum_up, sum_down = widen(sum_twin, sum_down)
        grad_input = finish_rows(dh1)
        tiny = lax.all_to_all(
            lax.psum(tiny, "expert"), ("context", "dp"), split_axis=0, concat_axis=0, tiled=True
        )
        tiny = jnp.sum(tiny, axis=0)
        g4 = g_qkv.reshape(n_ctx, n_dp, rows, width)
        s_qkv = direct_sum(lambda d: lax.dynamic_index_in_dim(g4, d, 1, keepdims=False), "dp")
        s_qkv = lax.psum(s_qkv.astype(bf16), "expert")
        s_out = lax.psum(s_out.astype(bf16), "expert").astype(f32)
        back = exchange(s_qkv)[c_of]

        def columns(lo, hi):
            return back[:, :, lo:hi].transpose(1, 0, 2).reshape(rows, -1).astype(f32)

        sum_q, sum_k, sum_v = columns(0, qw), columns(qw, qw + kw), columns(qw + kw, width)
        g_gain_a = sum(
            jnp.sum(w.astype(f32) * g, axis=1)
            for w, g in ((w_query, sum_q), (key_weight, sum_k), (value_weight, sum_v))
        ) / attn_gain.astype(f32)
        output = (middle + y_sum.finish()).astype(bf16)

    return (
        output[None], grad_input[None], g_gain_a, sum_q, sum_k, sum_v, s_out,
        tiny[0], tiny[1:].T, sum_gate[None], sum_up[None], sum_down[None],
    )


def solution(mesh):
    tokens = P(("expert", "dp"), "context", None)
    group = P(("expert", "dp"), None)
    vec, mat = P(("context", "dp")), P(("context", "dp"), None)
    expert = P(("expert", "context"), None, None)
    by_rows = P(("expert", "context"), "dp", None)
    by_cols = P(("expert", "context"), None, "dp")
    return jax.shard_map(
        body,
        mesh=mesh,
        in_specs=(
            tokens, tokens, group, group, tokens, vec, mat, mat, mat, mat, vec, mat,
            expert, expert, expert,
        ),
        out_specs=(
            tokens, tokens, vec, mat, mat, mat, mat, vec, mat, by_rows, by_rows, by_cols,
        ),
        check_vma=False,
    )
```
